32 devices in a mesh: gx: 4 (over y, x), gy: 4 (over z), gz: 2 (over core).
Axes of the slice: x: 2, y: 2, z: 4, core: 2. Of those that a mesh axis runs over, the one named last changes fastest.
Arguments:
- velocity: float32 [3, 16, 16, 512], P(None, 'gx', 'gz', 'gy'), may hold values from -6 to 6
- stress: float32 [6, 16, 16, 512], P(None, 'gx', 'gz', 'gy'), may hold values from -6 to 6
- region_map: int32 [16, 16, 512], P('gx', 'gz', 'gy'), may hold values from 0 to 7
- lame_table: float32 [8], replicated, may hold values from 0.5 to 2
- shear_table: float32 [8], replicated, may hold values from 0.3 to 1.2
- buoy_table: float32 [8], replicated, may hold values from 0.5 to 2
- block_pattern: float32 [512, 3, 128], P(('gx', 'gy')), may hold values from -8 to 8
- block_wave: float32 [512, 4], P(('gx', 'gy')), may hold values from -1 to 1
- block_x: int32 [512], P(('gx', 'gy')), may hold values from 0 to 3
- block_dest: int32 [512, 1], P(('gx', 'gy')), may hold values from 0 to 3; in each aligned block of 32 rows (0 to 31, 32 to 63, ...) at most 16 rows name the same one
Outputs:
- velocity_out: float32 [3, 16, 16, 512], P(None, 'gx', 'gz', 'gy')
- stress_out: float32 [6, 16, 16, 512], P(None, 'gx', 'gz', 'gy')
The draws below stay inside these ranges and needn't reach their ends.
Inputs may be any that keep to these rules, and one draw needn't show every extreme that they name: `block_dest`: among one device's 32 blocks at most 16 name one y index.
All inputs are finite; a program needn't handle non-finite values.
Results may differ from the reference program's by a relative error of at most 0.0001.
Values sent between devices are 32-bit elements; how exact they have to be, the bound alone decides.
A program may use at most 64 MiB of HBM per device.

```python
import math
import jax
import jax.numpy as jnp
import numpy as np
from jax import lax

CX = 4
CY = 128
STEPS = 4
REGIONS = 8
BLK_DEV = 32
CAP = 16
NX = 16
NY = 512
NZ = 16
NBLK = 512
N_GY = 4


def set_ends(entries, rng, smallest, top_value):
    shape = entries.shape
    spot = [jax.random.randint(jax.random.fold_in(rng, axis), (), 0, shape[axis]) for axis in range(len(shape))]
    entries = entries.at[tuple(spot)].set(smallest)
    longest = shape.index(max(shape))
    spot[longest] = (spot[longest] + 1) % shape[longest]
    return entries.at[tuple(spot)].set(top_value)


def shard_levels(own_key, dims, shards, low, largest):
    def one(position, shards_of):
        heights = jax.random.uniform(jax.random.fold_in(jax.random.fold_in(own_key, 6), position), (shards_of,), jnp.float32, low / len(shards), largest / len(shards))
        return jnp.repeat(jnp.exp(heights), dims[position] // shards_of).reshape((-1,) + (1,) * (len(dims) - position - 1))

    factor_of = one(*shards[0])
    for cut in shards[1:]:
        factor_of = factor_of * one(*cut)
    return factor_of


def shared_out(rng, own, number, rows, number_of, top, bound, lean):
    order = jax.random.permutation(rng, number_of)
    crowded, usual = portions_of(number_of, rows * top, bound, lean, True), portions_of(number_of, rows * top, bound, lean, False)
    places = jnp.arange(number_of)

    def named(sizes, rotation):
        used = int((sizes > 0).sum())
        fixed = max(1, used // 4)
        moved = fixed + (places - fixed + rotation * (used - fixed)) % max(1, number_of - fixed)
        return jnp.zeros((number_of,), jnp.int32).at[order[jnp.where(places < fixed, places, moved)]].set(jnp.asarray(sizes, jnp.int32))

    sizes = jnp.where(number % 4 == 0, named(crowded, number // 4), named(usual, number - number // 4 - 1))
    mixed = jax.random.permutation(jax.random.fold_in(own, 3), number_of)
    giver, taker = mixed[0:number_of // 2 * 2:2], mixed[1:number_of // 2 * 2:2]
    margin = jnp.minimum(sizes[giver] - 1, bound - sizes[taker]) // 2
    margin = jnp.where((giver == order[0]) | (taker == order[0]) | (sizes[taker] == 0), 0, jnp.maximum(margin, 0))
    moved = jax.random.randint(jax.random.fold_in(own, 4), (number_of // 2,), 0, 1 << 20) % (margin + 1)
    sizes = sizes.at[giver].add(-moved).at[taker].add(moved)
    items = jnp.searchsorted(jnp.cumsum(sizes), jnp.arange(rows * top), side="right").astype(jnp.int32)
    listing = items.reshape(top, rows).T
    listing = listing[jax.random.permutation(jax.random.fold_in(own, 1), rows)]
    rotation = jax.random.randint(jax.random.fold_in(own, 2), (rows, 1), 0, top)
    return jnp.take_along_axis(listing, (jnp.arange(top)[None, :] + rotation) % top, axis=1)


def portions_of(amount, total, limit, skew, full):
    weights = [(1 << 20) // math.isqrt(grade ** skew) + 1 for grade in range(1, amount + 1)]
    largest = limit if full else min(limit, max(-(-total // amount), total * weights[0] // sum(weights)))
    least = 1 if total - largest >= amount - 1 else 0
    given, rest = [largest] + [least] * (amount - 1), total - largest - least * (amount - 1)
    while rest > 0:
        candidates = [i for i in range(1, amount) if given[i] < largest] or [i for i in range(1, amount) if given[i] < limit]
        mass, budget = sum([weights[i] for i in candidates]), rest
        for i in candidates:
            addition = min(limit - given[i], max(1, budget * weights[i] // mass), rest)
            given[i] = given[i] + addition
            rest = rest - addition
    return np.array(given)


def centred(stream_key, dims, scale, reach, cuts=(), kind=jnp.bfloat16):
    values = jax.random.normal(stream_key, dims, jnp.float32) * scale
    if len(cuts) > 0:
        values = shard_levels(stream_key, dims, cuts, -0.22, 0.18) * values
    return jnp.clip(values, min=-reach, max=reach).astype(kind)


def setup_inputs(seed: int = 0) -> dict:
    key_list = jax.random.split(jax.random.key(seed), 11)
    velocity = centred(key_list[0], (3, NX, NZ, NY), 1.0, 6.0, ((1, 4), (2, 2), (3, 4)), jnp.float32)
    stress = centred(key_list[1], (6, NX, NZ, NY), 1.0, 6.0, ((1, 4), (2, 2), (3, 4)), jnp.float32)
    region_map = set_ends(jax.random.randint(key_list[2], (NX, NZ, NY), 0, REGIONS), jax.random.fold_in(key_list[2], 1), 0, REGIONS - 1).astype(jnp.int32)
    lame_table = jnp.clip(jnp.exp(jax.random.uniform(key_list[3], (REGIONS,), jnp.float32, math.log(0.5), math.log(2.0))), 0.5, 2.0)
    shear_table = jnp.clip(jnp.exp(jax.random.uniform(key_list[4], (REGIONS,), jnp.float32, math.log(0.3), math.log(1.2))), 0.3, 1.2)
    buoy_table = jnp.clip(jnp.exp(jax.random.uniform(key_list[5], (REGIONS,), jnp.float32, math.log(0.5), math.log(2.0))), 0.5, 2.0)
    block_pattern = centred(key_list[6], (NBLK, 3, CY), 2.0, 8.0, ((0, 16),), jnp.float32)
    block_wave = jnp.clip(jax.random.uniform(key_list[7], (NBLK, STEPS), jnp.float32, -1.0, 1.0) * shard_levels(key_list[7], (NBLK, STEPS), ((0, 16),), -0.4, 0.0), -1.0, 1.0)
    block_x = set_ends(jax.random.randint(key_list[8], (NBLK,), 0, CX), jax.random.fold_in(key_list[8], 1), 0, CX - 1).astype(jnp.int32)
    block_dest_keys = jax.random.split(jax.random.fold_in(key_list[9], 1), NBLK // BLK_DEV)
    block_dest_turns = jax.random.permutation(jax.random.fold_in(key_list[9], 3), NBLK // BLK_DEV)
    block_dest = jax.vmap(lambda own, number: shared_out(jax.random.fold_in(key_list[9], 2), own, number, BLK_DEV, N_GY, 1, CAP, 2))(block_dest_keys, block_dest_turns).reshape((NBLK, 1))
    return {"velocity": velocity, "stress": stress, "region_map": region_map, "lame_table": lame_table, "shear_table": shear_table, "buoy_table": buoy_table, "block_pattern": block_pattern, "block_wave": block_wave, "block_x": block_x, "block_dest": block_dest}


coef_near = 9.0 / 8.0
coef_far = 1.0 / 24.0
time_step = 0.13


def shifted(padded, offset, along):
    length = padded.shape[along] - 4
    return lax.slice_in_dim(padded, offset, offset + length, axis=along)


def forward(padded, along):
    return coef_near * (shifted(padded, 3, along) - shifted(padded, 2, along)) - coef_far * (shifted(padded, 4, along) - shifted(padded, 1, along))


def backward(padded, along):
    return coef_near * (shifted(padded, 2, along) - shifted(padded, 1, along)) - coef_far * (shifted(padded, 3, along) - shifted(padded, 0, along))


def velocity_update(velocity, sides_x, sides_y, sides_z, buoyancy, forcing):
    rate_x = forward(sides_x[0], 0) + backward(sides_y[0], 2) + backward(sides_z[0], 1)
    rate_y = backward(sides_x[1], 0) + forward(sides_y[1], 2) + backward(sides_z[1], 1)
    rate_z = backward(sides_x[2], 0) + backward(sides_y[2], 2) + forward(sides_z[2], 1)
    rates = jnp.stack([rate_x, rate_y, rate_z])
    return velocity + time_step * buoyancy * (rates + forcing)


def stress_update(stress, vel_x, vel_y, vel_z, lame_first, shear):
    strain_xx = backward(vel_x[0], 0)
    strain_yy = backward(vel_y[1], 2)
    strain_zz = backward(vel_z[2], 1)
    trace = strain_xx + strain_yy + strain_zz
    normal_xx = stress[0] + time_step * (lame_first * trace + 2.0 * shear * strain_xx)
    normal_yy = stress[1] + time_step * (lame_first * trace + 2.0 * shear * strain_yy)
    normal_zz = stress[2] + time_step * (lame_first * trace + 2.0 * shear * strain_zz)
    shear_xy = stress[3] + time_step * shear * (forward(vel_y[0], 2) + forward(vel_x[1], 0))
    shear_xz = stress[4] + time_step * shear * (forward(vel_z[0], 1) + forward(vel_x[2], 0))
    shear_yz = stress[5] + time_step * shear * (forward(vel_z[1], 1) + forward(vel_y[2], 2))
    return jnp.stack([normal_xx, normal_yy, normal_zz, shear_xy, shear_xz, shear_yz])


def pad_along(field, along):
    widths = [(0, 0), (0, 0), (0, 0), (0, 0)]
    widths[along] = (2, 2)
    return jnp.pad(field, widths)


def reference(velocity, stress, region_map, lame_table, shear_table, buoy_table, block_pattern, block_wave, block_x, block_dest):
    lame_first = jnp.take(lame_table, region_map)
    shear = jnp.take(shear_table, region_map)
    buoyancy = jnp.take(buoy_table, region_map)
    block_count = block_pattern.shape[0]
    index = jnp.arange(block_count, dtype=jnp.int32)
    column = index // (BLK_DEV * N_GY)
    target = (column * CX + block_x) * N_GY + block_dest[:, 0]
    for moment in range(STEPS):
        weighted = block_pattern * block_wave[:, moment][:, None, None]
        summed = jax.ops.segment_sum(weighted, target, num_segments=NX * N_GY)
        surface = summed.reshape(NX, N_GY, 3, CY).transpose(2, 0, 1, 3).reshape(3, NX, NY)
        forcing = jnp.zeros_like(velocity).at[:, :, 0, :].set(surface)
        sides_x = pad_along(jnp.stack([stress[0], stress[3], stress[4]]), 1)
        sides_y = pad_along(jnp.stack([stress[3], stress[1], stress[5]]), 3)
        sides_z = pad_along(jnp.stack([stress[4], stress[5], stress[2]]), 2)
        velocity = velocity_update(velocity, sides_x, sides_y, sides_z, buoyancy, forcing)
        vel_x = pad_along(velocity, 1)
        vel_y = pad_along(velocity, 3)
        vel_z = pad_along(velocity, 2)
        stress = stress_update(stress, vel_x, vel_y, vel_z, lame_first, shear)
    return velocity, stress
```

```python
import functools
import jax
import jax.numpy as jnp
from jax import lax
from jax.experimental import pallas as pl
from jax.experimental.pallas import tpu as pltpu
from jax.sharding import PartitionSpec as P

STEPS = 4
ROUNDS = 2 * STEPS

NEAR = 9.0 / 8.0
FAR = 1.0 / 24.0
DT = 0.13
MESH = pl.DeviceIdType.MESH


def masks(shape, axis):
    n = shape[axis]
    at = lax.broadcasted_iota(jnp.int32, shape, axis)

    def split(test, value):
        inside = jnp.where(test, 0.0, value).astype(jnp.float32)
        across = jnp.where(test, value, 0.0).astype(jnp.float32)
        return inside, across

    fwd = (
        (n - 1, split(at == n - 1, NEAR)),
        (n - 2, split(at >= n - 2, -FAR)),
        (1, split(at == 0, FAR)),
    )
    bwd = (
        (1, split(at == 0, -NEAR)),
        (2, split(at < 2, FAR)),
        (n - 1, split(at == n - 1, -FAR)),
    )
    return {"f": (fwd, -NEAR), "b": (bwd, NEAR)}


def in_tile(f, way, coefs, axis):
    terms, own = coefs[way]
    inside = own * f
    across = None
    for turn, (here, there) in terms:
        rolled = pltpu.roll(f, turn, axis)
        inside = inside + here[None] * rolled
        add = there[None] * rolled
        across = add if across is None else across + add
    return inside, across


def kernel(
    sizes,
    vel_ref,
    str_ref,
    reg_ref,
    lame_ref,
    shear_ref,
    buoy_ref,
    pat_ref,
    wave_ref,
    bx_ref,
    dest_ref,
    vout_ref,
    sout_ref,
    part,
    got,
    sxr,
    sxl,
    hxl,
    hxr,
    sy,
    hy,
    vin,
    sin,
    rin,
    vo,
    so,
    ssem,
    rsem,
    fs,
    fr,
    ls,
    lr,
    ld,
):
    nx, ny, nz = sizes
    ix, iy, iz = lax.axis_index("gx"), lax.axis_index("gy"), lax.axis_index("gz")
    cx, half = vel_ref.shape[1:3]
    tile = (2 * half, vel_ref.shape[3])
    lead = iz == nz - 1
    low, high = pl.ds(0, half), pl.ds(half, half)
    has_l, has_r = lead & (ix > 0), lead & (ix < nx - 1)
    has_d, has_u = lead & (iy > 0), lead & (iy < ny - 1)

    barrier = pltpu.get_barrier_semaphore()

    def greet(cond, where):
        @pl.when(cond)
        def _():
            pl.semaphore_signal(barrier, inc=1, device_id=where, device_id_type=MESH)

        return cond.astype(jnp.int32)

    count = greet(has_l, {"gx": ix - 1}) + greet(has_r, {"gx": ix + 1}) + 1
    pl.semaphore_signal(barrier, inc=1, device_id={"gz": 1 - iz}, device_id_type=MESH)
    for d in range(ny):
        count = count + greet(lead & (iy != d), {"gy": d})

    def hand(src, dst, k):
        return pltpu.make_async_remote_copy(
            src_ref=src,
            dst_ref=dst,
            send_sem=ls.at[k],
            recv_sem=lr.at[k],
            device_id={"gz": 1 - iz},
            device_id_type=MESH,
        )

    given = (
        hand(str_ref, sin.at[:, :, low], 0),
        hand(vel_ref, vin.at[:, :, low], 1),
        hand(reg_ref, rin.at[:, low], 2),
    )
    back = (hand(vo, vout_ref, 3), hand(so, sout_ref, 4))

    @pl.when(jnp.logical_not(lead))
    def _():
        pl.semaphore_wait(barrier, count)
        for copy in given:
            copy.start()
        for copy in given:
            copy.wait_send()
        for copy in back:
            copy.wait_recv()

    @pl.when(lead)
    def _():
        own = (
            pltpu.make_async_copy(str_ref, sin.at[:, :, high], ld.at[0]),
            pltpu.make_async_copy(vel_ref, vin.at[:, :, high], ld.at[1]),
            pltpu.make_async_copy(reg_ref, rin.at[:, high], ld.at[2]),
        )
        for copy in own:
            copy.start()
        @pl.when(jnp.logical_not(has_l))
        def _():
            hxl[...] = jnp.zeros_like(hxl)

        @pl.when(jnp.logical_not(has_r))
        def _():
            hxr[...] = jnp.zeros_like(hxr)

        @pl.when(jnp.logical_not(has_d))
        def _():
            hy[:, 0] = jnp.zeros_like(hy[:, 0])

        @pl.when(jnp.logical_not(has_u))
        def _():
            hy[:, 1] = jnp.zeros_like(hy[:, 1])

        rows = STEPS * cx

        if True:
            blocks = pat_ref.shape[1]
            row = lax.broadcasted_iota(jnp.int32, (ny * rows, blocks), 0)
            moment = (row // cx) % STEPS
            spot = (row // rows) * cx + row % cx
            key = dest_ref[...] * cx + bx_ref[...]
            amount = jnp.zeros((ny * rows, blocks), jnp.float32)
            for t in range(STEPS):
                amount = jnp.where(moment == t, wave_ref[t : t + 1, :], amount)
            weights = jnp.where(spot == key, amount, 0.0)
            for c in range(3):
                sums = jnp.dot(
                    weights,
                    pat_ref[c],
                    precision=lax.Precision.HIGHEST,
                    preferred_element_type=jnp.float32,
                )
                for d in range(ny):
                    part[d, c] = sums[d * rows : (d + 1) * rows]
            got[iy] = part[iy]

        lane = masks(tile, 1)
        sub = masks(tile, 0)
        at_lane = lax.broadcasted_iota(jnp.int32, tile, 1)
        at_sub = lax.broadcasted_iota(jnp.int32, tile, 0)
        n_lane = tile[1]
        edge_lane = (at_lane < 2) | (at_lane >= n_lane - 2)
        from_low = at_lane % 4 < 2

        def rdma(src, dst, r, k, where):
            return pltpu.make_async_remote_copy(
                src_ref=src,
                dst_ref=dst,
                send_sem=ssem.at[r, k],
                recv_sem=rsem.at[r, k],
                device_id=where,
                device_id_type=MESH,
            )

        def copies(r):
            to_r, to_l = (5, 4) if r % 2 == 0 else (4, 5)
            return (
                (has_r, has_l, rdma(sxr.at[r, pl.ds(0, to_r)], hxl.at[r, pl.ds(0, to_r)], r, 0, {"gx": ix + 1})),
                (has_l, has_r, rdma(sxl.at[r, pl.ds(0, to_l)], hxr.at[r, pl.ds(0, to_l)], r, 1, {"gx": ix - 1})),
                (has_u, has_d, rdma(sy.at[r], hy.at[r, 0], r, 2, {"gy": iy + 1})),
                (has_d, has_u, rdma(sy.at[r], hy.at[r, 1], r, 3, {"gy": iy - 1})),
            )

        def when(cond, act):
            if cond is None:
                act()
            else:
                pl.when(cond)(act)

        def derivatives(r, fx, fy, fz, first=None):
            to_r = [(f, w) for f, w in fx]
            moves = copies(r)
            k = 0
            for f, way in fx:
                for p in (cx - 1,) if way == "f" else (cx - 2, cx - 1):
                    sxr[r, k] = f[p]
                    k += 1
            k = 0
            for f, way in fx:
                for p in (0, 1) if way == "f" else (0,):
                    sxl[r, k] = f[p]
                    k += 1
            if first is not None:
                first()
            odd = ix % 2 == 1
            when(has_r & odd, moves[0][2].start)
            when(has_l, moves[1][2].start)
            when(has_r & jnp.logical_not(odd), moves[0][2].start)
            dy, packed, slot = [], None, 0
            for f, way in fy:
                inside, across = in_tile(f, way, lane, 2)
                dy.append(inside)
                for p in range(cx):
                    turned = across[p] if slot == 0 else pltpu.roll(across[p], 4 * slot, 1)
                    packed = turned if packed is None else packed + turned
                    slot += 1
            sy[r] = packed
            for m in moves[2:4]:
                when(m[0], m[2].start)
            dz = []
            for f, way in fz:
                dz.append(in_tile(f, way, sub, 1)[0])

            def finish():
                out_z = dz
                for m in moves[2:4]:
                    when(m[1], m[2].wait_recv)
                both = jnp.where(from_low, hy[r, 0], hy[r, 1])
                out_y = []
                for c in range(3):
                    planes = []
                    for p in range(cx):
                        slot = c * cx + p
                        turned = both if slot == 0 else pltpu.roll(both, n_lane - 4 * slot, 1)
                        planes.append(jnp.where(edge_lane, turned, 0.0))
                    out_y.append(dy[c] + jnp.stack(planes))
                for m in moves[:2]:
                    when(m[1], m[2].wait_recv)
                out_x, kl, kr = [], 0, 0
                for f, way in fx:
                    left = 1 if way == "f" else 2
                    right = 3 - left
                    pad = jnp.concatenate([hxl[r, kl : kl + left], f, hxr[r, kr : kr + right]], axis=0)
                    kl, kr = kl + left, kr + right
                    s = [pad[i : i + cx] for i in range(4)]
                    out_x.append(NEAR * (s[2] - s[1]) - FAR * (s[3] - s[0]))
                return out_x, out_y, out_z

            return finish

        def forces(act):
            for d in range(ny):
                @pl.when(iy != d)
                def _():
                    copy = pltpu.make_async_remote_copy(
                        src_ref=part.at[d],
                        dst_ref=got.at[iy if act == "start" else d],
                        send_sem=fs.at[d],
                        recv_sem=fr.at[iy if act == "start" else d],
                        device_id={"gy": d},
                        device_id_type=MESH,
                    )
                    getattr(copy, act)()

        def enter():
            pl.semaphore_wait(barrier, count)
            forces("start")

        own[0].wait()
        given[0].wait_recv()
        vel = None
        txx, tyy, tzz, txy, txz, tyz = [sin[c] for c in range(6)]
        surface = None
        for t in range(STEPS):
            finish = derivatives(
                2 * t,
                ((txx, "f"), (txy, "b"), (txz, "b")),
                ((txy, "b"), (tyy, "f"), (tyz, "b")),
                ((txz, "b"), (tyz, "b"), (tzz, "f")),
                enter if t == 0 else None,
            )
            if t == 0:
                for k in (1, 2):
                    own[k].wait()
                    given[k].wait_recv()
                vel = [vin[c] for c in range(3)]
                region = rin[...]
                lame = jnp.zeros(region.shape, jnp.float32)
                shear, buoy = lame, lame
                for k in range(lame_ref.shape[0]):
                    hit = region == k
                    lame = jnp.where(hit, lame_ref[k], lame)
                    shear = jnp.where(hit, shear_ref[k], shear)
                    buoy = jnp.where(hit, buoy_ref[k], buoy)
                lame, shear, buoy = DT * lame, DT * shear, DT * buoy
                forces("wait_recv")
                for c in range(3):
                    total = got[0, c]
                    for s in range(1, ny):
                        total = total + got[s, c]
                    got[0, c] = total
            dx, dy, dz = finish()
            for c in range(3):
                push = jnp.stack(
                    [
                        jnp.where(at_sub == 0, got[0, c, t * cx + p : t * cx + p + 1, :], 0.0)
                        for p in range(cx)
                    ]
                )
                vel[c] = vel[c] + buoy * (dx[c] + dy[c] + dz[c] + push)
            vx, vy, vz = vel
            if t == STEPS - 1:
                for c in range(3):
                    vo[c] = vel[c][:, :half]
            finish = derivatives(
                2 * t + 1,
                ((vx, "b"), (vy, "f"), (vz, "f")),
                ((vx, "f"), (vy, "b"), (vz, "f")),
                ((vx, "f"), (vy, "f"), (vz, "b")),
            )
            if t == STEPS - 1:
                back[0].start()
                for c in range(3):
                    vout_ref[c] = vel[c][:, half:]
            dx, dy, dz = finish()
            trace = lame * (dx[0] + dy[1] + dz[2])
            twice = 2.0 * shear
            txx = txx + (trace + twice * dx[0])
            tyy = tyy + (trace + twice * dy[1])
            tzz = tzz + (trace + twice * dz[2])
            txy = txy + shear * (dy[0] + dx[1])
            txz = txz + shear * (dz[0] + dx[2])
            tyz = tyz + shear * (dz[1] + dy[2])
        for c, f in enumerate((txx, tyy, tzz, txy, txz, tyz)):
            so[c] = f[:, :half]
            sout_ref[c] = f[:, half:]
        back[1].start()
        forces("wait_send")
        for r in range(ROUNDS):
            for m in copies(r):
                when(m[0], m[2].wait_send)
        for copy in back:
            copy.wait_send()


def shards(sizes, velocity, stress, region_map, lame_table, shear_table, buoy_table,
           block_pattern, block_wave, block_x, block_dest):
    cx = velocity.shape[1]
    tile = (2 * velocity.shape[2], velocity.shape[3])
    blocks = block_pattern.shape[0]
    ny = sizes[1]
    vmem = pl.BlockSpec(memory_space=pltpu.VMEM)
    smem = pl.BlockSpec(memory_space=pltpu.SMEM)
    hbm = pl.BlockSpec(memory_space=pl.ANY)
    f32 = jnp.float32
    held = pl.pallas_call(
        functools.partial(kernel, sizes),
        out_shape=(pltpu.VMEM(velocity.shape, f32), pltpu.VMEM(stress.shape, f32)),
        in_specs=[hbm, hbm, hbm, smem, smem, smem, vmem, vmem, vmem, vmem],
        out_specs=(vmem, vmem),
        scratch_shapes=[
            pltpu.VMEM((ny, 3, STEPS * cx, tile[1]), f32),
            pltpu.VMEM((ny, 3, STEPS * cx, tile[1]), f32),
            pltpu.VMEM((ROUNDS, 5) + tile, f32),
            pltpu.VMEM((ROUNDS, 5) + tile, f32),
            pltpu.VMEM((ROUNDS, 5) + tile, f32),
            pltpu.VMEM((ROUNDS, 5) + tile, f32),
            pltpu.VMEM((ROUNDS,) + tile, f32),
            pltpu.VMEM((ROUNDS, 2) + tile, f32),
            pltpu.VMEM((3, cx) + tile, f32),
            pltpu.VMEM((6, cx) + tile, f32),
            pltpu.VMEM((cx,) + tile, jnp.int32),
            pltpu.VMEM(velocity.shape, f32),
            pltpu.VMEM(stress.shape, f32),
            pltpu.SemaphoreType.DMA((ROUNDS, 4)),
            pltpu.SemaphoreType.DMA((ROUNDS, 4)),
            pltpu.SemaphoreType.DMA((ny,)),
            pltpu.SemaphoreType.DMA((ny,)),
            pltpu.SemaphoreType.DMA((5,)),
            pltpu.SemaphoreType.DMA((5,)),
            pltpu.SemaphoreType.DMA((3,)),
        ],
        compiler_params=pltpu.CompilerParams(collective_id=0, has_side_effects=True),
        name="waves",
    )(
        velocity,
        stress,
        region_map,
        lame_table,
        shear_table,
        buoy_table,
        block_pattern.transpose(1, 0, 2),
        block_wave.T,
        block_x.reshape(1, blocks),
        block_dest.reshape(1, blocks),
    )
    return held


HALO = 16
WIDE = 64
FIELDS = 10


def slab_kernel(
    sizes,
    vel_ref,
    str_ref,
    reg_ref,
    lame_ref,
    shear_ref,
    buoy_ref,
    pat_ref,
    wave_ref,
    bx_ref,
    dest_ref,
    vout_ref,
    sout_ref,
    raw_v,
    raw_s,
    raw_r,
    pat,
    wave,
    bx,
    dest,
    lame_t,
    shear_t,
    buoy_t,
    packed,
    strip,
    got_strip,
    grid,
    coef,
    push_out,
    push_in,
    push,
    done,
    back,
    isem,
    bulk_s,
    bulk_r,
    own_sem,
    strip_s,
    strip_r,
    push_s,
    push_r,
    back_s,
    back_r,
    go,
):
    nx, ny, nz = sizes
    ix, iy, iz = lax.axis_index("gx"), lax.axis_index("gy"), lax.axis_index("gz")
    cx, half, lanes = vel_ref.shape[1:]
    pairs = cx // 2
    total = nx * pairs
    last = nx - 1
    top = nz - 1
    lead = iz == top
    slab = lanes // nx
    has_d, has_u = iy > 0, iy < ny - 1
    tall = pl.ds(half, 2 * half)

    barrier = pltpu.get_barrier_semaphore()

    def signal(where):
        pl.semaphore_signal(barrier, inc=1, device_id=where, device_id_type=MESH)

    at = lax.broadcasted_iota(jnp.int32, (half, lanes), 1)
    low = at < WIDE
    at = at % WIDE
    spin = [(HALO - slab * j) % lanes for j in range(nx)]

    def remote(src, dst, ssem, rsem, where):
        return pltpu.make_async_remote_copy(
            src_ref=src, dst_ref=dst, send_sem=ssem, recv_sem=rsem, device_id=where, device_id_type=MESH
        )

    loads = (
        pltpu.make_async_copy(str_ref, raw_s, isem.at[0]),
        pltpu.make_async_copy(vel_ref, raw_v, isem.at[1]),
        pltpu.make_async_copy(reg_ref, raw_r, isem.at[2]),
    )
    tables = (
        pltpu.make_async_copy(lame_ref, lame_t, isem.at[3]),
        pltpu.make_async_copy(shear_ref, shear_t, isem.at[4]),
        pltpu.make_async_copy(buoy_ref, buoy_t, isem.at[5]),
    )
    blocks_in = (
        pltpu.make_async_copy(pat_ref, pat, isem.at[6]),
        pltpu.make_async_copy(wave_ref, wave, isem.at[7]),
        pltpu.make_async_copy(bx_ref, bx, isem.at[8]),
        pltpu.make_async_copy(dest_ref, dest, isem.at[9]),
    )

    def pack():
        for copy in loads:
            copy.wait()

        def field(f, x):
            if f < 6:
                return raw_s[f, x]
            if f < 9:
                return raw_v[f - 6, x]
            return raw_r[x].astype(jnp.float32)

        edges = [None, None]
        for f in range(FIELDS):
            for p in range(pairs):
                even, odd = field(f, 2 * p), field(f, 2 * p + 1)
                turned = [pltpu.roll(even, r, 1) for r in spin], {r: pltpu.roll(odd, r, 1) for r in spin}
                g = (f % 2) * pairs + p
                mine = (at >= HALO * g) & (at < HALO * (g + 1))
                for j in range(nx):
                    both = jnp.where(low, turned[0][j], turned[1][(spin[j] + WIDE) % lanes])
                    if j == 0:
                        moved = pltpu.roll(both, HALO * g, 1) if g else both
                        edges[0] = moved if g == 0 else jnp.where(mine, moved, edges[0])
                        both = jnp.where(at < HALO, 0.0, both)
                    if j == last:
                        shift = (HALO * g - (WIDE - HALO)) % lanes
                        moved = pltpu.roll(both, shift, 1) if shift else both
                        edges[1] = moved if g == 0 else jnp.where(mine, moved, edges[1])
                        both = jnp.where(at >= WIDE - HALO, 0.0, both)
                    packed[j, f, p] = both
            if f % 2 == 1:
                for way in range(2):
                    strip[way, f // 2] = edges[way]

    def bulk(j, zt, to):
        return remote(
            packed.at[j],
            grid.at[:, pl.ds(pairs * ix, pairs), pl.ds(half * (zt + 1), half)],
            bulk_s.at[j],
            bulk_r.at[ix, zt],
            {"gx": j, "gz": to},
        )

    def arrived(j, zt):
        return remote(
            packed.at[j],
            grid.at[:, pl.ds(pairs * j, pairs), pl.ds(half * (zt + 1), half)],
            bulk_s.at[j],
            bulk_r.at[j, zt],
            {"gx": j, "gz": top},
        )

    def edge(way, zt):
        where = {"gx": 0, "gy": iy + 1, "gz": top} if way == 0 else {"gx": last, "gy": iy - 1, "gz": top}
        return remote(strip.at[way], got_strip.at[ix, zt], strip_s.at[way], strip_r.at[ix, zt], where)

    def edge_arrived(j, zt):
        return remote(strip.at[0], got_strip.at[j, zt], strip_s.at[0], strip_r.at[j, zt], {"gx": j, "gz": top})

    def edges_do(zt, act):
        @pl.when(has_u)
        def _():
            getattr(edge(0, zt), act)()

        @pl.when(has_d)
        def _():
            getattr(edge(1, zt), act)()

    def result(j, zt):
        return remote(
            done.at[j, zt], back.at[ix], back_s.at[j, zt], back_r.at[ix], {"gx": j, "gz": zt}
        )

    def results_wait():
        for j in range(nx):
            remote(done.at[j, 0], back.at[j], back_s.at[j, 0], back_r.at[j], {"gx": j, "gz": top}).wait_recv()

    def unpack():
        offset = (0, WIDE, slab, WIDE + slab)
        lane = lax.broadcasted_iota(jnp.int32, (half, lanes), 1)
        for f in range(9):
            came = [back[j, f] for j in range(nx)]
            for x in range(cx):
                out = None
                for j in range(nx):
                    shift = (slab * j - HALO - offset[x]) % lanes
                    moved = pltpu.roll(came[j], shift, 1) if shift else came[j]
                    out = moved if out is None else jnp.where(lane >= slab * j, moved, out)
                if f < 6:
                    sout_ref[f, x] = out
                else:
                    vout_ref[f - 6, x] = out

    keep = pltpu.make_async_copy(
        packed.at[ix], grid.at[:, pl.ds(pairs * ix, pairs), pl.ds(2 * half, half)], own_sem.at[0]
    )

    @pl.when(lead)
    def _():
        for o in range(1, nx):
            signal({"gx": lax.rem(ix + o, nx)})

        @pl.when((ix == 0) & has_d)
        def _():
            for j in range(nx):
                signal({"gx": j, "gy": iy - 1})

        @pl.when((ix == last) & has_u)
        def _():
            for j in range(nx):
                signal({"gx": j, "gy": iy + 1})

        for copy in loads + tables:
            copy.start()
        for d in range(ny):
            for j in range(nx):
                signal({"gx": j, "gy": d, "gz": 0})
        blank = jnp.zeros((FIELDS, total, half, lanes), jnp.float32)
        grid[:, :, pl.ds(0, half)] = blank
        grid[:, :, pl.ds(3 * half, half)] = blank
        pack()
        count = nx + has_d.astype(jnp.int32) + has_u.astype(jnp.int32)
        pl.semaphore_wait(barrier, count)
        pl.semaphore_signal(go, inc=1, device_id={"gz": 0}, device_id_type=MESH)
        for o in range(nx - 1, 0, -1):
            to = lax.rem(ix + o, nx)
            remote(
                packed.at[to],
                grid.at[:, pl.ds(pairs * ix, pairs), pl.ds(2 * half, half)],
                bulk_s.at[to],
                bulk_r.at[ix, top],
                {"gx": to},
            ).start()
        edges_do(1, "start")
        keep.start()

    @pl.when(jnp.logical_not(lead))
    def _():
        signal({"gz": top})
        for copy in loads + blocks_in:
            copy.start()
        pack()
        pl.semaphore_wait(go, 1)
        for o in range(nx - 1, -1, -1):
            bulk_to = lax.rem(ix + o, nx)
            remote(
                packed.at[bulk_to],
                grid.at[:, pl.ds(pairs * ix, pairs), pl.ds(half, half)],
                bulk_s.at[bulk_to],
                bulk_r.at[ix, 0],
                {"gx": bulk_to, "gz": top},
            ).start()
        edges_do(0, "start")

        for copy in blocks_in:
            copy.wait()
        blocks = pat.shape[1]
        rows = STEPS * cx
        row = lax.broadcasted_iota(jnp.int32, (ny * rows, blocks), 0)
        moment = (row // pairs) % STEPS
        spot = (row // rows) * cx + (row % pairs) * 2 + (row // (pairs * STEPS)) % 2
        key = dest[...] * cx + bx[...]
        amount = jnp.zeros((ny * rows, blocks), jnp.float32)
        for t in range(STEPS):
            amount = jnp.where(moment == t, wave[t : t + 1, :], amount)
        weights = jnp.where(spot == key, amount, 0.0)
        size = rows // 2
        for c in range(3):
            sums = jnp.dot(
                weights, pat[c], precision=lax.Precision.HIGHEST, preferred_element_type=jnp.float32
            )
            windows = []
            for d in range(ny):
                even = sums[d * rows : d * rows + size]
                odd = sums[d * rows + size : (d + 1) * rows]
                turned = [pltpu.roll(even, r, 1) for r in spin], {r: pltpu.roll(odd, r, 1) for r in spin}
                windows.append(
                    [jnp.where(low, turned[0][j], turned[1][(spin[j] + WIDE) % lanes]) for j in range(nx)]
                )
            for d in range(ny):
                for j in range(nx):
                    both = windows[d][j]
                    if j == 0:
                        both = jnp.where(at < HALO, windows[d - 1][j] if d > 0 else 0.0, both)
                    if j == last:
                        both = jnp.where(at >= WIDE - HALO, windows[d + 1][j] if d < ny - 1 else 0.0, both)
                    push_out[d, j, c] = both

        def forces(d, j):
            return remote(
                push_out.at[d, j],
                push_in.at[ix, iy],
                push_s.at[d, j],
                push_r.at[ix, iy],
                {"gx": j, "gy": d, "gz": top},
            )

        pl.semaphore_wait(barrier, nx * ny)
        for d in range(ny):
            for j in range(nx):
                forces(d, j).start()
        for d in range(ny):
            for j in range(nx):
                forces(d, j).wait_send()
        for j in range(nx):
            arrived(j, 0).wait_send()
        edges_do(0, "wait_send")
        results_wait()

    @pl.when(lead)
    def _():
        for copy in tables:
            copy.wait()
        keep.wait()
        for j in range(nx):
            arrived(j, 0).wait_recv()

            @pl.when(ix != j)
            def _():
                arrived(j, 1).wait_recv()

        def merge(way):
            for j in range(nx):
                for zt in range(2):
                    edge_arrived(j, zt).wait_recv()

            def body(j, carry):
                for zt in range(2):
                    for f in range(FIELDS):
                        came = got_strip[j, zt, f // 2]
                        for p in range(pairs):
                            g = (f % 2) * pairs + p
                            shift = (-HALO * g if way == 0 else WIDE - HALO - HALO * g) % lanes
                            moved = pltpu.roll(came, shift, 1) if shift else came
                            here = (f, pairs * j + p, pl.ds(half * (zt + 1), half))
                            inside = at >= HALO if way == 0 else at < WIDE - HALO
                            grid[here] = jnp.where(inside, grid[here], moved)
                return carry

            lax.fori_loop(0, nx, body, 0)

        @pl.when((ix == 0) & has_d)
        def _():
            merge(0)

        @pl.when((ix == last) & has_u)
        def _():
            merge(1)

        shape = (2 * half, lanes)
        lane = lax.broadcasted_iota(jnp.int32, shape, 1)
        left = lane < WIDE
        lane = lane % WIDE
        first = lax.broadcasted_iota(jnp.int32, shape, 0) == 0
        beyond = ((lane < HALO) & (ix == 0) & (iy == 0)) | (
            (lane >= WIDE - HALO) & (ix == last) & (iy == ny - 1)
        )
        within = jnp.where(beyond, 0.0, DT * NEAR).astype(jnp.float32)
        for k in range(total):
            region = grid[9, k, tall]
            picks = [jnp.zeros(shape, jnp.float32) for _ in range(3)]
            for r in range(lame_t.shape[0]):
                hit = region == float(r)
                for q, table in enumerate((lame_t, shear_t, buoy_t)):
                    picks[q] = jnp.where(hit, table[r], picks[q])
            for q in range(3):
                coef[q, k] = within * picks[q]

        for j in range(nx):
            for i in range(ny):
                remote(
                    push_out.at[0, 0], push_in.at[j, i], push_s.at[0, 0], push_r.at[j, i], {"gz": 0}
                ).wait_recv()
            for c in range(3):
                amount = push_in[j, 0, c]
                for i in range(1, ny):
                    amount = amount + push_in[j, i, c]
                push[j, c] = (1.0 / NEAR) * amount

        ratio = FAR / NEAR
        zero = jnp.zeros(shape, jnp.float32)

        def rows(f, k, s):
            return grid[f, k, pl.ds(half + s, 2 * half)]

        def along_x(f, way):
            v = [grid[f, k, tall] for k in range(total)]
            turned = [zero] + [pltpu.roll(a, WIDE, 1) for a in v] + [zero]
            step = [jnp.where(left, turned[k], turned[k + 1]) for k in range(total + 1)]
            out = []
            for k in range(total):
                if way == "f":
                    after = v[k + 1] if k + 1 < total else zero
                    out.append((step[k + 1] - v[k]) - ratio * (after - step[k]))
                else:
                    before = v[k - 1] if k > 0 else zero
                    out.append((v[k] - step[k]) - ratio * (step[k + 1] - before))
            return out

        def along_y(f, way, k):
            v = grid[f, k, tall]
            if way == "f":
                a, b, c, d = pltpu.roll(v, lanes - 1, 1), v, pltpu.roll(v, lanes - 2, 1), pltpu.roll(v, 1, 1)
            else:
                a, b, c, d = v, pltpu.roll(v, 1, 1), pltpu.roll(v, lanes - 1, 1), pltpu.roll(v, 2, 1)
            return (a - b) - ratio * (c - d)

        def along_z(f, way, k):
            o = 0 if way == "b" else 1
            return (rows(f, k, o) - rows(f, k, o - 1)) - ratio * (rows(f, k, o + 1) - rows(f, k, o - 2))

        txx, tyy, tzz, txy, txz, tyz, vx, vy, vz = range(9)

        def advance(t):
            for c, fx, wx, fy, wy, fz, wz in (
                (0, txx, "f", txy, "b", txz, "b"),
                (1, txy, "b", tyy, "f", tyz, "b"),
                (2, txz, "b", tyz, "b", tzz, "f"),
            ):
                dx = along_x(fx, wx)
                for k in range(total):
                    now = push[k // pairs, c, pl.ds(t * pairs + k % pairs, 1), :]
                    rate = dx[k] + along_y(fy, wy, k) + along_z(fz, wz, k) + jnp.where(first, now, 0.0)
                    grid[vx + c, k, tall] = grid[vx + c, k, tall] + coef[2, k] * rate

            exx = along_x(vx, "b")
            for k in range(total):
                eyy, ezz = along_y(vy, "b", k), along_z(vz, "b", k)
                twice = 2.0 * coef[1, k]
                trace = coef[0, k] * (exx[k] + eyy + ezz)
                grid[txx, k, tall] = grid[txx, k, tall] + (trace + twice * exx[k])
                grid[tyy, k, tall] = grid[tyy, k, tall] + (trace + twice * eyy)
                grid[tzz, k, tall] = grid[tzz, k, tall] + (trace + twice * ezz)
            dx = along_x(vy, "f")
            for k in range(total):
                grid[txy, k, tall] = grid[txy, k, tall] + coef[1, k] * (along_y(vx, "f", k) + dx[k])
            dx = along_x(vz, "f")
            for k in range(total):
                grid[txz, k, tall] = grid[txz, k, tall] + coef[1, k] * (along_z(vx, "f", k) + dx[k])
                grid[tyz, k, tall] = grid[tyz, k, tall] + coef[1, k] * (
                    along_z(vy, "f", k) + along_y(vz, "f", k)
                )

        lax.fori_loop(0, STEPS, lambda t, carry: (advance(t), carry)[1], 0)

        own_lanes = (at >= HALO) & (at < HALO + slab)
        for j in range(nx):
            for zt in range(2):
                for f in range(9):
                    here = pl.ds(half * (zt + 1), half)
                    a, b = grid[f, pairs * j, here], grid[f, pairs * j + 1, here]
                    done[j, zt, f] = jnp.where(own_lanes, a, pltpu.roll(b, slab, 1))
        for o in range(nx - 1, -1, -1):
            to = lax.rem(ix + o, nx)
            for zt in range(2):
                if o == 0 and zt == top:
                    mine = pltpu.make_async_copy(done.at[ix, top], back.at[ix], own_sem.at[1])
                    mine.start()
                    mine.wait()
                else:
                    result(to, zt).start()
        for j in range(nx):
            @pl.when(ix != j)
            def _():
                remote(done.at[j, 0], back.at[j], back_s.at[j, 0], back_r.at[j], {"gx": j}).wait_recv()
        unpack()
        for o in range(1, nx):
            bulk(lax.rem(ix + o, nx), 1, top).wait_send()
        edges_do(1, "wait_send")
        for o in range(nx):
            for zt in range(2):
                if o > 0 or zt != top:
                    result(lax.rem(ix + o, nx), zt).wait_send()

    @pl.when(jnp.logical_not(lead))
    def _():
        unpack()


def slabs(sizes, velocity, stress, region_map, lame_table, shear_table, buoy_table,
          block_pattern, block_wave, block_x, block_dest):
    nx, ny, nz = sizes
    cx, half, lanes = velocity.shape[1:]
    blocks = block_pattern.shape[0]
    pairs = cx // 2
    total = nx * pairs
    tile = (half, lanes)
    vmem = pl.BlockSpec(memory_space=pltpu.VMEM)
    hbm = pl.BlockSpec(memory_space=pl.ANY)
    f32, i32 = jnp.float32, jnp.int32
    dma = pltpu.SemaphoreType.DMA
    return pl.pallas_call(
        functools.partial(slab_kernel, sizes),
        out_shape=(pltpu.VMEM(velocity.shape, f32), pltpu.VMEM(stress.shape, f32)),
        in_specs=[hbm] * 10,
        out_specs=(vmem, vmem),
        scratch_shapes=[
            pltpu.VMEM(velocity.shape, f32),
            pltpu.VMEM(stress.shape, f32),
            pltpu.VMEM(region_map.shape, i32),
            pltpu.VMEM((3, blocks, lanes), f32),
            pltpu.VMEM((STEPS, blocks), f32),
            pltpu.VMEM((1, blocks), i32),
            pltpu.VMEM((1, blocks), i32),
            pltpu.SMEM(lame_table.shape, f32),
            pltpu.SMEM(lame_table.shape, f32),
            pltpu.SMEM(lame_table.shape, f32),
            pltpu.VMEM((nx, FIELDS, pairs) + tile, f32),
            pltpu.VMEM((2, FIELDS // 2) + tile, f32),
            pltpu.VMEM((nx, 2, FIELDS // 2) + tile, f32),
            pltpu.VMEM((FIELDS, total, 4 * half, lanes), f32),
            pltpu.VMEM((3, total, 2 * half, lanes), f32),
            pltpu.VMEM((ny, nx, 3) + tile, f32),
            pltpu.VMEM((nx, ny, 3) + tile, f32),
            pltpu.VMEM((nx, 3) + tile, f32),
            pltpu.VMEM((nx, 2, 9) + tile, f32),
            pltpu.VMEM((nx, 9) + tile, f32),
            dma((10,)),
            dma((nx,)),
            dma((nx, 2)),
            dma((2,)),
            dma((2,)),
            dma((nx, 2)),
            dma((ny, nx)),
            dma((nx, ny)),
            dma((nx, 2)),
            dma((nx,)),
            pltpu.SemaphoreType.REGULAR,
        ],
        compiler_params=pltpu.CompilerParams(collective_id=0, has_side_effects=True),
        name="slabs",
    )(
        velocity,
        stress,
        region_map,
        lame_table,
        shear_table,
        buoy_table,
        block_pattern.transpose(1, 0, 2),
        block_wave.T,
        block_x.reshape(1, blocks),
        block_dest.reshape(1, blocks),
    )


def local(sizes, velocity, *rest):
    nx, ny, nz = sizes
    cx, half, lanes = velocity.shape[1:]
    fits = nz == 2 and cx == 4 and half == 8 and lanes == 128 and lanes // nx + 2 * HALO == WIDE
    return (slabs if fits else shards)(sizes, velocity, *rest)


def solution(mesh):
    sizes = tuple(mesh.shape[a] for a in ("gx", "gy", "gz"))
    field = P(None, "gx", "gz", "gy")
    both = ("gx", "gy")
    placed = (
        field,
        field,
        P("gx", "gz", "gy"),
        P(),
        P(),
        P(),
        P(both, None, None),
        P(both, None),
        P(both),
        P(both, None),
    )
    return jax.shard_map(
        functools.partial(local, sizes),
        mesh=mesh,
        in_specs=placed,
        out_specs=(field, field),
        check_vma=False,
    )
```

```python
import functools
import jax
import jax.numpy as jnp
from jax import lax
from jax.experimental import pallas as pl
from jax.experimental.pallas import tpu as pltpu
from jax.sharding import PartitionSpec as P

STEPS = 4
ROUNDS = 2 * STEPS

NEAR = 9.0 / 8.0
FAR = 1.0 / 24.0
DT = 0.13
MESH = pl.DeviceIdType.MESH


def masks(shape, axis):
    n = shape[axis]
    at = lax.broadcasted_iota(jnp.int32, shape, axis)

    def split(test, value):
        inside = jnp.where(test, 0.0, value).astype(jnp.float32)
        across = jnp.where(test, value, 0.0).astype(jnp.float32)
        return inside, across

    fwd = (
        (n - 1, split(at == n - 1, NEAR)),
        (n - 2, split(at >= n - 2, -FAR)),
        (1, split(at == 0, FAR)),
    )
    bwd = (
        (1, split(at == 0, -NEAR)),
        (2, split(at < 2, FAR)),
        (n - 1, split(at == n - 1, -FAR)),
    )
    return {"f": (fwd, -NEAR), "b": (bwd, NEAR)}


def in_tile(f, way, coefs, axis):
    terms, own = coefs[way]
    inside = own * f
    across = None
    for turn, (here, there) in terms:
        rolled = pltpu.roll(f, turn, axis)
        inside = inside + here[None] * rolled
        add = there[None] * rolled
        across = add if across is None else across + add
    return inside, across


def kernel(
    sizes,
    vel_ref,
    str_ref,
    reg_ref,
    lame_ref,
    shear_ref,
    buoy_ref,
    pat_ref,
    wave_ref,
    bx_ref,
    dest_ref,
    vout_ref,
    sout_ref,
    part,
    got,
    sxr,
    sxl,
    hxl,
    hxr,
    sy,
    hy,
    vin,
    sin,
    rin,
    vo,
    so,
    ssem,
    rsem,
    fs,
    fr,
    ls,
    lr,
    ld,
):
    nx, ny, nz = sizes
    ix, iy, iz = lax.axis_index("gx"), lax.axis_index("gy"), lax.axis_index("gz")
    cx, half = vel_ref.shape[1:3]
    tile = (2 * half, vel_ref.shape[3])
    lead = iz == nz - 1
    low, high = pl.ds(0, half), pl.ds(half, half)
    has_l, has_r = lead & (ix > 0), lead & (ix < nx - 1)
    has_d, has_u = lead & (iy > 0), lead & (iy < ny - 1)

    barrier = pltpu.get_barrier_semaphore()

    def greet(cond, where):
        @pl.when(cond)
        def _():
            pl.semaphore_signal(barrier, inc=1, device_id=where, device_id_type=MESH)

        return cond.astype(jnp.int32)

    count = greet(has_l, {"gx": ix - 1}) + greet(has_r, {"gx": ix + 1}) + 1
    pl.semaphore_signal(barrier, inc=1, device_id={"gz": 1 - iz}, device_id_type=MESH)
    for d in range(ny):
        count = count + greet(lead & (iy != d), {"gy": d})

    def hand(src, dst, k):
        return pltpu.make_async_remote_copy(
            src_ref=src,
            dst_ref=dst,
            send_sem=ls.at[k],
            recv_sem=lr.at[k],
            device_id={"gz": 1 - iz},
            device_id_type=MESH,
        )

    given = (
        hand(str_ref, sin.at[:, :, low], 0),
        hand(vel_ref, vin.at[:, :, low], 1),
        hand(reg_ref, rin.at[:, low], 2),
    )
    back = (hand(vo, vout_ref, 3), hand(so, sout_ref, 4))

    @pl.when(jnp.logical_not(lead))
    def _():
        pl.semaphore_wait(barrier, count)
        for copy in given:
            copy.start()
        for copy in given:
            copy.wait_send()
        for copy in back:
            copy.wait_recv()

    @pl.when(lead)
    def _():
        own = (
            pltpu.make_async_copy(str_ref, sin.at[:, :, high], ld.at[0]),
            pltpu.make_async_copy(vel_ref, vin.at[:, :, high], ld.at[1]),
            pltpu.make_async_copy(reg_ref, rin.at[:, high], ld.at[2]),
        )
        for copy in own:
            copy.start()
        @pl.when(jnp.logical_not(has_l))
        def _():
            hxl[...] = jnp.zeros_like(hxl)

        @pl.when(jnp.logical_not(has_r))
        def _():
            hxr[...] = jnp.zeros_like(hxr)

        @pl.when(jnp.logical_not(has_d))
        def _():
            hy[:, 0] = jnp.zeros_like(hy[:, 0])

        @pl.when(jnp.logical_not(has_u))
        def _():
            hy[:, 1] = jnp.zeros_like(hy[:, 1])

        rows = STEPS * cx

        if True:
            blocks = pat_ref.shape[1]
            row = lax.broadcasted_iota(jnp.int32, (ny * rows, blocks), 0)
            moment = (row // cx) % STEPS
            spot = (row // rows) * cx + row % cx
            key = dest_ref[...] * cx + bx_ref[...]
            amount = jnp.zeros((ny * rows, blocks), jnp.float32)
            for t in range(STEPS):
                amount = jnp.where(moment == t, wave_ref[t : t + 1, :], amount)
            weights = jnp.where(spot == key, amount, 0.0)
            for c in range(3):
                sums = jnp.dot(
                    weights,
                    pat_ref[c],
                    precision=lax.Precision.HIGHEST,
                    preferred_element_type=jnp.float32,
                )
                for d in range(ny):
                    part[d, c] = sums[d * rows : (d + 1) * rows]
            got[iy] = part[iy]

        lane = masks(tile, 1)
        sub = masks(tile, 0)
        at_lane = lax.broadcasted_iota(jnp.int32, tile, 1)
        at_sub = lax.broadcasted_iota(jnp.int32, tile, 0)
        n_lane = tile[1]
        edge_lane = (at_lane < 2) | (at_lane >= n_lane - 2)
        from_low = at_lane % 4 < 2

        def rdma(src, dst, r, k, where):
            return pltpu.make_async_remote_copy(
                src_ref=src,
                dst_ref=dst,
                send_sem=ssem.at[r, k],
                recv_sem=rsem.at[r, k],
                device_id=where,
                device_id_type=MESH,
            )

        def copies(r):
            to_r, to_l = (5, 4) if r % 2 == 0 else (4, 5)
            return (
                (has_r, has_l, rdma(sxr.at[r, pl.ds(0, to_r)], hxl.at[r, pl.ds(0, to_r)], r, 0, {"gx": ix + 1})),
                (has_l, has_r, rdma(sxl.at[r, pl.ds(0, to_l)], hxr.at[r, pl.ds(0, to_l)], r, 1, {"gx": ix - 1})),
                (has_u, has_d, rdma(sy.at[r], hy.at[r, 0], r, 2, {"gy": iy + 1})),
                (has_d, has_u, rdma(sy.at[r], hy.at[r, 1], r, 3, {"gy": iy - 1})),
            )

        def when(cond, act):
            if cond is None:
                act()
            else:
                pl.when(cond)(act)

        def derivatives(r, fx, fy, fz, first=None):
            to_r = [(f, w) for f, w in fx]
            moves = copies(r)
            k = 0
            for f, way in fx:
                for p in (cx - 1,) if way == "f" else (cx - 2, cx - 1):
                    sxr[r, k] = f[p]
                    k += 1
            k = 0
            for f, way in fx:
                for p in (0, 1) if way == "f" else (0,):
                    sxl[r, k] = f[p]
                    k += 1
            if first is not None:
                first()
            odd = ix % 2 == 1
            when(has_r & odd, moves[0][2].start)
            when(has_l, moves[1][2].start)
            when(has_r & jnp.logical_not(odd), moves[0][2].start)
            dy, packed, slot = [], None, 0
            for f, way in fy:
                inside, across = in_tile(f, way, lane, 2)
                dy.append(inside)
                for p in range(cx):
                    turned = across[p] if slot == 0 else pltpu.roll(across[p], 4 * slot, 1)
                    packed = turned if packed is None else packed + turned
                    slot += 1
            sy[r] = packed
            for m in moves[2:4]:
                when(m[0], m[2].start)
            dz = []
            for f, way in fz:
                dz.append(in_tile(f, way, sub, 1)[0])

            def finish():
                out_z = dz
                for m in moves[2:4]:
                    when(m[1], m[2].wait_recv)
                both = jnp.where(from_low, hy[r, 0], hy[r, 1])
                out_y = []
                for c in range(3):
                    planes = []
                    for p in range(cx):
                        slot = c * cx + p
                        turned = both if slot == 0 else pltpu.roll(both, n_lane - 4 * slot, 1)
                        planes.append(jnp.where(edge_lane, turned, 0.0))
                    out_y.append(dy[c] + jnp.stack(planes))
                for m in moves[:2]:
                    when(m[1], m[2].wait_recv)
                out_x, kl, kr = [], 0, 0
                for f, way in fx:
                    left = 1 if way == "f" else 2
                    right = 3 - left
                    pad = jnp.concatenate([hxl[r, kl : kl + left], f, hxr[r, kr : kr + right]], axis=0)
                    kl, kr = kl + left, kr + right
                    s = [pad[i : i + cx] for i in range(4)]
                    out_x.append(NEAR * (s[2] - s[1]) - FAR * (s[3] - s[0]))
                return out_x, out_y, out_z

            return finish

        def forces(act):
            for d in range(ny):
                @pl.when(iy != d)
                def _():
                    copy = pltpu.make_async_remote_copy(
                        src_ref=part.at[d],
                        dst_ref=got.at[iy if act == "start" else d],
                        send_sem=fs.at[d],
                        recv_sem=fr.at[iy if act == "start" else d],
                        device_id={"gy": d},
                        device_id_type=MESH,
                    )
                    getattr(copy, act)()

        def enter():
            pl.semaphore_wait(barrier, count)
            forces("start")

        own[0].wait()
        given[0].wait_recv()
        vel = None
        txx, tyy, tzz, txy, txz, tyz = [sin[c] for c in range(6)]
        surface = None
        for t in range(STEPS):
            finish = derivatives(
                2 * t,
                ((txx, "f"), (txy, "b"), (txz, "b")),
                ((txy, "b"), (tyy, "f"), (tyz, "b")),
                ((txz, "b"), (tyz, "b"), (tzz, "f")),
                enter if t == 0 else None,
            )
            if t == 0:
                for k in (1, 2):
                    own[k].wait()
                    given[k].wait_recv()
                vel = [vin[c] for c in range(3)]
                region = rin[...]
                lame = jnp.zeros(region.shape, jnp.float32)
                shear, buoy = lame, lame
                for k in range(lame_ref.shape[0]):
                    hit = region == k
                    lame = jnp.where(hit, lame_ref[k], lame)
                    shear = jnp.where(hit, shear_ref[k], shear)
                    buoy = jnp.where(hit, buoy_ref[k], buoy)
                lame, shear, buoy = DT * lame, DT * shear, DT * buoy
                forces("wait_recv")
                for c in range(3):
                    total = got[0, c]
                    for s in range(1, ny):
                        total = total + got[s, c]
                    got[0, c] = total
            dx, dy, dz = finish()
            for c in range(3):
                push = jnp.stack(
                    [
                        jnp.where(at_sub == 0, got[0, c, t * cx + p : t * cx + p + 1, :], 0.0)
                        for p in range(cx)
                    ]
                )
                vel[c] = vel[c] + buoy * (dx[c] + dy[c] + dz[c] + push)
            vx, vy, vz = vel
            if t == STEPS - 1:
                for c in range(3):
                    vo[c] = vel[c][:, :half]
            finish = derivatives(
                2 * t + 1,
                ((vx, "b"), (vy, "f"), (vz, "f")),
                ((vx, "f"), (vy, "b"), (vz, "f")),
                ((vx, "f"), (vy, "f"), (vz, "b")),
            )
            if t == STEPS - 1:
                back[0].start()
                for c in range(3):
                    vout_ref[c] = vel[c][:, half:]
            dx, dy, dz = finish()
            trace = lame * (dx[0] + dy[1] + dz[2])
            twice = 2.0 * shear
            txx = txx + (trace + twice * dx[0])
            tyy = tyy + (trace + twice * dy[1])
            tzz = tzz + (trace + twice * dz[2])
            txy = txy + shear * (dy[0] + dx[1])
            txz = txz + shear * (dz[0] + dx[2])
            tyz = tyz + shear * (dz[1] + dy[2])
        for c, f in enumerate((txx, tyy, tzz, txy, txz, tyz)):
            so[c] = f[:, :half]
            sout_ref[c] = f[:, half:]
        back[1].start()
        forces("wait_send")
        for r in range(ROUNDS):
            for m in copies(r):
                when(m[0], m[2].wait_send)
        for copy in back:
            copy.wait_send()


def shards(sizes, velocity, stress, region_map, lame_table, shear_table, buoy_table,
           block_pattern, block_wave, block_x, block_dest):
    cx = velocity.shape[1]
    tile = (2 * velocity.shape[2], velocity.shape[3])
    blocks = block_pattern.shape[0]
    ny = sizes[1]
    vmem = pl.BlockSpec(memory_space=pltpu.VMEM)
    smem = pl.BlockSpec(memory_space=pltpu.SMEM)
    hbm = pl.BlockSpec(memory_space=pl.ANY)
    f32 = jnp.float32
    held = pl.pallas_call(
        functools.partial(kernel, sizes),
        out_shape=(pltpu.VMEM(velocity.shape, f32), pltpu.VMEM(stress.shape, f32)),
        in_specs=[hbm, hbm, hbm, smem, smem, smem, vmem, vmem, vmem, vmem],
        out_specs=(vmem, vmem),
        scratch_shapes=[
            pltpu.VMEM((ny, 3, STEPS * cx, tile[1]), f32),
            pltpu.VMEM((ny, 3, STEPS * cx, tile[1]), f32),
            pltpu.VMEM((ROUNDS, 5) + tile, f32),
            pltpu.VMEM((ROUNDS, 5) + tile, f32),
            pltpu.VMEM((ROUNDS, 5) + tile, f32),
            pltpu.VMEM((ROUNDS, 5) + tile, f32),
            pltpu.VMEM((ROUNDS,) + tile, f32),
            pltpu.VMEM((ROUNDS, 2) + tile, f32),
            pltpu.VMEM((3, cx) + tile, f32),
            pltpu.VMEM((6, cx) + tile, f32),
            pltpu.VMEM((cx,) + tile, jnp.int32),
            pltpu.VMEM(velocity.shape, f32),
            pltpu.VMEM(stress.shape, f32),
            pltpu.SemaphoreType.DMA((ROUNDS, 4)),
            pltpu.SemaphoreType.DMA((ROUNDS, 4)),
            pltpu.SemaphoreType.DMA((ny,)),
            pltpu.SemaphoreType.DMA((ny,)),
            pltpu.SemaphoreType.DMA((5,)),
            pltpu.SemaphoreType.DMA((5,)),
            pltpu.SemaphoreType.DMA((3,)),
        ],
        compiler_params=pltpu.CompilerParams(collective_id=0, has_side_effects=True),
        name="waves",
    )(
        velocity,
        stress,
        region_map,
        lame_table,
        shear_table,
        buoy_table,
        block_pattern.transpose(1, 0, 2),
        block_wave.T,
        block_x.reshape(1, blocks),
        block_dest.reshape(1, blocks),
    )
    return held


HALO = 16
WIDE = 64
FIELDS = 10
FIRST = 7
BAND = 12
BANDS = WIDE // BAND


def slab_kernel(
    sizes,
    vel_ref,
    str_ref,
    reg_ref,
    lame_ref,
    shear_ref,
    buoy_ref,
    pat_ref,
    wave_ref,
    bx_ref,
    dest_ref,
    back_v,
    back_s,
    raw_v,
    raw_s,
    raw_r,
    pat,
    wave,
    bx,
    dest,
    lame_t,
    shear_t,
    buoy_t,
    packed,
    strip,
    got_strip,
    grid,
    coef,
    early,
    taps,
    push_out,
    push_in,
    push,
    done_v,
    done_s,
    isem,
    bulk_ss,
    bulk_rs,
    own_ss,
    strip_ss,
    strip_rs,
    push_ss,
    push_rs,
    back_ss,
    back_rs,
    go,
    far,
):
    nx, ny, nz = sizes
    ix, iy, iz = lax.axis_index("gx"), lax.axis_index("gy"), lax.axis_index("gz")
    cx, half, lanes = vel_ref.shape[1:]
    pairs = cx // 2
    total = nx * pairs
    last = nx - 1
    top = nz - 1
    lead = iz == top
    slab = lanes // nx
    has_d, has_u = iy > 0, iy < ny - 1
    tall = pl.ds(half, 2 * half)
    peers = (last - ix, lax.rem(ix + 2, nx), ix + 1 - 2 * lax.rem(ix, 2))
    groups = (pl.ds(0, FIRST), pl.ds(FIRST, FIELDS - FIRST))

    barrier = pltpu.get_barrier_semaphore()

    def signal(where):
        pl.semaphore_signal(barrier, inc=1, device_id=where, device_id_type=MESH)

    at = lax.broadcasted_iota(jnp.int32, (half, lanes), 1)
    low = at < WIDE
    at = at % WIDE
    spin = [(HALO - slab * j) % lanes for j in range(nx)]

    def remote(src, dst, ssem, rsem, where):
        return pltpu.make_async_remote_copy(
            src_ref=src, dst_ref=dst, send_sem=ssem, recv_sem=rsem, device_id=where, device_id_type=MESH
        )

    loads = (
        pltpu.make_async_copy(str_ref, raw_s, isem.at[0]),
        pltpu.make_async_copy(vel_ref, raw_v, isem.at[1]),
        pltpu.make_async_copy(reg_ref, raw_r, isem.at[2]),
    )
    tables = (
        pltpu.make_async_copy(lame_ref, lame_t, isem.at[3]),
        pltpu.make_async_copy(shear_ref, shear_t, isem.at[4]),
        pltpu.make_async_copy(buoy_ref, buoy_t, isem.at[5]),
    )
    blocks_in = (
        pltpu.make_async_copy(pat_ref, pat, isem.at[6]),
        pltpu.make_async_copy(wave_ref, wave, isem.at[7]),
        pltpu.make_async_copy(bx_ref, bx, isem.at[8]),
        pltpu.make_async_copy(dest_ref, dest, isem.at[9]),
    )

    def window(even, odd, j):
        r = spin[j]
        return jnp.where(low, pltpu.roll(even, r, 1), pltpu.roll(odd, (r + WIDE) % lanes, 1))

    def pack():
        for copy in loads:
            copy.wait()

        def field(f, x):
            if f < 6:
                return raw_s[f, x]
            if f < FIRST:
                return raw_r[x].astype(jnp.float32)
            return raw_v[f - FIRST, x]

        edges = [None, None]
        for f in range(FIELDS):
            for p in range(pairs):
                even, odd = field(f, 2 * p), field(f, 2 * p + 1)
                i = f * pairs + p
                g = i % BANDS
                mine = at >= BAND * g
                for j in range(nx):
                    both = window(even, odd, j)
                    if j in (0, last):
                        way = 0 if j == 0 else 1
                        origin = HALO - BAND if j == 0 else WIDE - HALO
                        moved = pltpu.roll(both, (BAND * g - origin) % lanes, 1)
                        edges[way] = moved if g == 0 else jnp.where(mine, moved, edges[way])
                        if g == BANDS - 1 or i == FIELDS * pairs - 1:
                            strip[way, i // BANDS] = edges[way]
                        both = jnp.where(at < HALO if j == 0 else at >= WIDE - HALO, 0.0, both)
                    packed[j, f, p] = both

    def place(j, zt, part):
        return grid.at[groups[part], pl.ds(pairs * j, pairs), pl.ds(half * (zt + 1), half)]

    def bulk(to, zt, part):
        return remote(
            packed.at[to, groups[part]],
            place(ix, zt, part),
            bulk_ss.at[to, part],
            bulk_rs.at[ix, zt, part],
            {"gx": to, "gz": top},
        )

    def arrived(j, zt, part):
        remote(
            packed.at[j, groups[part]],
            place(j, zt, part),
            bulk_ss.at[j, part],
            bulk_rs.at[j, zt, part],
            {"gx": j, "gz": top},
        ).wait_recv()

    def edge(way, zt):
        where = {"gx": 0, "gy": iy + 1, "gz": top} if way == 0 else {"gx": last, "gy": iy - 1, "gz": top}
        return remote(strip.at[way], got_strip.at[ix, zt], strip_ss.at[way], strip_rs.at[ix, zt], where)

    def edge_arrived(j, zt):
        remote(strip.at[0], got_strip.at[j, zt], strip_ss.at[0], strip_rs.at[j, zt], {"gx": j, "gz": top}).wait_recv()

    def edges_do(zt, act):
        @pl.when(has_u)
        def _():
            getattr(edge(0, zt), act)()

        @pl.when(has_d)
        def _():
            getattr(edge(1, zt), act)()

    def result(to, zt, part):
        done, back = ((done_v, back_v), (done_s, back_s))[part]
        return remote(
            done.at[to, zt], back.at[ix], back_ss.at[to, zt, part], back_rs.at[ix, part], {"gx": to, "gz": zt}
        )

    def result_wait(j):
        for part in range(2):
            done, back = ((done_v, back_v), (done_s, back_s))[part]
            remote(
                done.at[j, 0], back.at[j], back_ss.at[j, 0, part], back_rs.at[j, part], {"gx": j, "gz": top}
            ).wait_recv()

    def keep(part):
        return pltpu.make_async_copy(packed.at[ix, groups[part]], place(ix, top, part), own_ss.at[part])

    def send(d, j, part):
        src, dst = (
            (push_out.at[d, j, pl.ds(0, 1)], push_in.at[ix, iy, pl.ds(0, 1)]),
            (push_out.at[d, j, pl.ds(1, STEPS - 1)], push_in.at[ix, iy, pl.ds(1, STEPS - 1)]),
        )[part]
        return remote(
            src, dst, push_ss.at[d, j, part], push_rs.at[ix, iy, part], {"gx": j, "gy": d, "gz": top}
        )

    def force_maker():
        for copy in blocks_in:
            copy.wait()
        blocks = pat.shape[1]
        size = 2 * half
        row = lax.broadcasted_iota(jnp.int32, (ny * size, blocks), 0)
        kind = (row // pairs) % (half // pairs)
        spot = (row // size) * cx + (row % pairs) * 2 + (row // half) % 2
        hit = spot == dest[...] * cx + bx[...]
        hits = [hit & (kind == c) for c in range(3)]

        def forces(t):
            sums = None
            for c in range(3):
                term = jnp.dot(
                    jnp.where(hits[c], wave[t : t + 1, :], 0.0),
                    pat[c],
                    precision=lax.Precision.HIGHEST,
                    preferred_element_type=jnp.float32,
                )
                sums = term if sums is None else sums + term
            at_d = [(sums[d * size : d * size + half], sums[d * size + half : (d + 1) * size]) for d in range(ny)]
            views = [[window(*at_d[d], j) for j in range(nx)] for d in range(ny)]
            for d in range(ny):
                for j in range(nx):
                    both = views[d][j]
                    if j == 0:
                        both = jnp.where(at < HALO, views[d - 1][j] if d > 0 else 0.0, both)
                    if j == last:
                        both = jnp.where(at >= WIDE - HALO, views[d + 1][j] if d < ny - 1 else 0.0, both)
                    push_out[d, j, t] = both

        return forces

    late = pl.ds(1, STEPS - 1)
    rest = pltpu.make_async_copy(push_out.at[iy, ix, late], push_in.at[ix, iy, late], own_ss.at[4])

    @pl.when(lead)
    def _():
        for to in peers:
            signal({"gx": to})

        @pl.when((ix == 0) & has_d)
        def _():
            for j in range(nx):
                signal({"gx": j, "gy": iy - 1})

        @pl.when((ix == last) & has_u)
        def _():
            for j in range(nx):
                signal({"gx": j, "gy": iy + 1})

        for copy in loads + tables + blocks_in:
            copy.start()
        for d in range(ny):
            for j in range(nx):
                signal({"gx": j, "gy": d, "gz": 0})
        blank = jnp.zeros((FIELDS, total, half, lanes), jnp.float32)
        grid[:, :, pl.ds(0, half)] = blank
        grid[:, :, pl.ds(3 * half, half)] = blank
        pack()
        source = lax.broadcasted_iota(jnp.int32, (lanes, lanes), 0)
        target = lax.broadcasted_iota(jnp.int32, (lanes, lanes), 1)
        for way in range(2):
            off = source - target + way
            tap = jnp.where(off == 1, NEAR / FAR, 0.0) + jnp.where(off == 0, -NEAR / FAR, 0.0)
            tap = tap + jnp.where(off == -1, 1.0, 0.0) + jnp.where(off == 2, -1.0, 0.0)
            tap = jnp.where(source // WIDE == target // WIDE, tap, 0.0).astype(jnp.bfloat16)
            taps[way, pl.ds(0, lanes)] = tap
            taps[way, pl.ds(lanes, lanes)] = tap
        pl.semaphore_wait(barrier, nx + has_d.astype(jnp.int32) + has_u.astype(jnp.int32))
        pl.semaphore_signal(go, inc=1, device_id={"gz": 0}, device_id_type=MESH)
        edges_do(top, "start")
        for part in range(2):
            for to in peers:
                bulk(to, top, part).start()
            keep(part).start()
        forces = force_maker()
        for t in range(1, STEPS):
            forces(t)
        pl.semaphore_wait(far, 1)
        for d in range(ny):
            for j in range(nx):
                pl.when((ix != j) | (iy != d))(send(d, j, 1).start)
        rest.start()

    @pl.when(jnp.logical_not(lead))
    def _():
        signal({"gz": top})
        for copy in blocks_in + loads:
            copy.start()
        pack()
        pl.semaphore_wait(go, 1)
        edges_do(0, "start")
        for to in peers:
            bulk(to, 0, 0).start()
        bulk(ix, 0, 0).start()
        for to in peers:
            bulk(to, 0, 1).start()
        bulk(ix, 0, 1).start()
        forces = force_maker()
        forces(0)
        for j in range(nx):
            remote(
                push_out.at[iy, j, pl.ds(0, 1)],
                push_in.at[ix, iy, pl.ds(0, 1)],
                push_ss.at[iy, j, 0],
                push_rs.at[ix, iy, 0],
                {"gx": j, "gz": top},
            ).start()
        pl.semaphore_wait(barrier, nx * ny)
        pl.semaphore_signal(far, inc=1, device_id={"gz": top}, device_id_type=MESH)
        for d in range(ny):
            for j in range(nx):
                pl.when(iy != d)(send(d, j, 0).start)
        for d in range(ny):
            for j in range(nx):
                send(d, j, 0).wait_send()
        for part in range(2):
            for j in range(nx):
                bulk(j, 0, part).wait_send()
        edges_do(0, "wait_send")
        for j in range(nx):
            result_wait(j)

    @pl.when(lead)
    def _():
        shape = (2 * half, lanes)
        lane = lax.broadcasted_iota(jnp.int32, shape, 1)
        left = lane < WIDE
        lane = lane % WIDE
        first = lax.broadcasted_iota(jnp.int32, shape, 0) == 0
        beyond = ((lane < HALO) & (ix == 0) & (iy == 0)) | (
            (lane >= WIDE - HALO) & (ix == last) & (iy == ny - 1)
        )
        within = jnp.where(beyond, 0.0, DT * FAR).astype(jnp.float32)
        ratio = NEAR / FAR
        zero = jnp.zeros(shape, jnp.float32)

        def bulk_wait(part):
            keep(part).wait()
            for j in range(nx):
                arrived(j, 0, part)

                @pl.when(ix != j)
                def _():
                    arrived(j, top, part)

        def merge(way, part):
            def body(j, carry):
                for zt in range(2):
                    for f in range(*((0, FIRST), (FIRST, FIELDS))[part]):
                        for p in range(pairs):
                            i = f * pairs + p
                            came = got_strip[j, zt, i // BANDS]
                            origin = HALO - BAND if way == 0 else WIDE - HALO
                            moved = pltpu.roll(came, (origin - BAND * (i % BANDS)) % lanes, 1)
                            here = (f, pairs * j + p, pl.ds(half * (zt + 1), half))
                            inside = at >= HALO if way == 0 else at < WIDE - HALO
                            grid[here] = jnp.where(inside, grid[here], moved)
                return carry

            lax.fori_loop(0, nx, body, 0)

        def merges(part):
            for way, cond in enumerate(((ix == 0) & has_d, (ix == last) & has_u)):
                @pl.when(cond)
                def _():
                    if part == 0:
                        for j in range(nx):
                            for zt in range(2):
                                edge_arrived(j, zt)
                    merge(way, part)

        def push_wait(part):
            if part == 1:
                rest.wait()
            for j in range(nx):
                for i in range(ny):
                    span = pl.ds(0, 1) if part == 0 else late
                    came = remote(
                        push_out.at[0, 0, span],
                        push_in.at[j, i, span],
                        push_ss.at[0, 0, part],
                        push_rs.at[j, i, part],
                        {"gz": 0},
                    )
                    if part == 0:
                        came.wait_recv()
                    else:
                        pl.when((ix != j) | (iy != i))(came.wait_recv)
                for t in (0,) if part == 0 else range(1, STEPS):
                    amount = push_in[j, 0, t]
                    for i in range(1, ny):
                        amount = amount + push_in[j, i, t]
                    push[t, j] = (1.0 / FAR) * amount

        def rows(f, k, s):
            return grid[f, k, pl.ds(half + s, 2 * half)]

        def turned(memo, f, k):
            if k < 0 or k >= total:
                return zero
            if (f, k) not in memo:
                memo[f, k] = pltpu.roll(grid[f, k, tall], WIDE, 1)
            return memo[f, k]

        def step(memo, f, k):
            if (f, k, "s") not in memo:
                memo[f, k, "s"] = jnp.where(left, turned(memo, f, k - 1), turned(memo, f, k))
            return memo[f, k, "s"]

        def along_x(memo, f, way, k):
            v, near, far = grid[f, k, tall], step(memo, f, k), step(memo, f, k + 1)
            if way == "f":
                after = grid[f, k + 1, tall] if k + 1 < total else zero
                return ratio * (far - v) - (after - near)
            before = grid[f, k - 1, tall] if k > 0 else zero
            return ratio * (v - near) - (far - before)

        def along_y(f, way):
            v = grid[f, :, tall].reshape(total * 2 * half, lanes)
            coarse = v.astype(jnp.bfloat16)
            fine = (v - coarse.astype(jnp.float32)).astype(jnp.bfloat16)
            out = jnp.dot(
                jnp.concatenate([coarse, fine], axis=1),
                taps[0 if way == "f" else 1],
                preferred_element_type=jnp.float32,
            )
            return [out[2 * half * k : 2 * half * (k + 1)] for k in range(total)]

        def along_z(f, way, k):
            o = 0 if way == "b" else 1
            return ratio * (rows(f, k, o) - rows(f, k, o - 1)) - (rows(f, k, o + 1) - rows(f, k, o - 2))

        txx, tyy, tzz, txy, txz, tyz = range(6)
        vx, vy, vz = range(FIRST, FIRST + 3)

        def rates(use):
            memo = {}
            dy = along_y(txy, "b"), along_y(tyy, "f"), along_y(tyz, "b")
            for k in range(total):
                for c, (fx, wx, fz, wz) in enumerate(
                    ((txx, "f", txz, "b"), (txy, "b", tyz, "b"), (txz, "b", tzz, "f"))
                ):
                    use(c, k, along_x(memo, fx, wx, k) + along_z(fz, wz, k) + dy[c][k])

        def kick(t, c, k, rate):
            now = push[t, k // pairs, pl.ds(c * pairs + k % pairs, 1), :]
            grid[vx + c, k, tall] = grid[vx + c, k, tall] + coef[2, k] * (rate + jnp.where(first, now, 0.0))

        def strain():
            memo = {}
            dy = along_y(vx, "f"), along_y(vy, "b"), along_y(vz, "f")
            for k in range(total):
                exx, eyy, ezz = along_x(memo, vx, "b", k), dy[1][k], along_z(vz, "b", k)
                shear = coef[1, k]
                twice = 2.0 * shear
                trace = coef[0, k] * (exx + eyy + ezz)
                grid[txx, k, tall] = grid[txx, k, tall] + (trace + twice * exx)
                grid[tyy, k, tall] = grid[tyy, k, tall] + (trace + twice * eyy)
                grid[tzz, k, tall] = grid[tzz, k, tall] + (trace + twice * ezz)
                grid[txy, k, tall] = grid[txy, k, tall] + shear * (dy[0][k] + along_x(memo, vy, "f", k))
                grid[txz, k, tall] = grid[txz, k, tall] + shear * (along_z(vx, "f", k) + along_x(memo, vz, "f", k))
                grid[tyz, k, tall] = grid[tyz, k, tall] + shear * (along_z(vy, "f", k) + dy[2][k])

        own_lanes = (at >= HALO) & (at < HALO + slab)

        def finish(part):
            done, start, count = ((done_v, FIRST, 3), (done_s, 0, 6))[part]
            for j in range(nx):
                for zt in range(2):
                    for f in range(count):
                        here = pl.ds(half * (zt + 1), half)
                        a, b = grid[start + f, pairs * j, here], grid[start + f, pairs * j + 1, here]
                        done[j, zt, f] = jnp.where(own_lanes, a, pltpu.roll(b, slab, 1))
            for to in peers:
                for zt in range(2):
                    result(to, zt, part).start()
            result(ix, 0, part).start()

        def mine(part):
            done, back = ((done_v, back_v), (done_s, back_s))[part]
            return pltpu.make_async_copy(done.at[ix, top], back.at[ix], own_ss.at[2 + part])

        for copy in tables:
            copy.wait()
        bulk_wait(0)
        merges(0)
        for k in range(total):
            region = grid[6, k, tall]
            picks = [zero] * 3
            for r in range(lame_t.shape[0]):
                hit = region == float(r)
                for q, table in enumerate((lame_t, shear_t, buoy_t)):
                    picks[q] = jnp.where(hit, table[r], picks[q])
            for q in range(3):
                coef[q, k] = within * picks[q]

        def store(c, k, rate):
            early[c, k] = rate

        rates(store)
        bulk_wait(1)
        merges(1)
        push_wait(0)
        for c in range(3):
            for k in range(total):
                kick(0, c, k, early[c, k])
        strain()
        push_wait(1)

        def middle(t, carry):
            rates(functools.partial(kick, t))
            strain()
            return carry

        lax.fori_loop(1, STEPS - 1, middle, 0)
        rates(functools.partial(kick, STEPS - 1))
        finish(0)
        mine(0).start()
        strain()
        finish(1)
        mine(1).start()

        for part in range(2):
            mine(part).wait()
        for j in range(nx):
            @pl.when(ix != j)
            def _():
                result_wait(j)
        for part in range(2):
            for to in peers:
                bulk(to, top, part).wait_send()
                for zt in range(2):
                    result(to, zt, part).wait_send()
            result(ix, 0, part).wait_send()
        for d in range(ny):
            for j in range(nx):
                pl.when((ix != j) | (iy != d))(send(d, j, 1).wait_send)
        edges_do(top, "wait_send")


def weave(back_v, back_s, vout_ref, sout_ref, vbuf, sbuf, sems):
    nx, _, half, lanes = back_v.shape
    slab = lanes // nx
    cx = vbuf.shape[1]
    offset = (0, WIDE, slab, WIDE + slab)
    lane = lax.broadcasted_iota(jnp.int32, (half, lanes), 1)
    for k, (back, buf, out) in enumerate(((back_v, vbuf, vout_ref), (back_s, sbuf, sout_ref))):
        for f in range(back.shape[1]):
            came = [back[j, f] for j in range(nx)]
            for x in range(cx):
                whole = None
                for j in range(nx):
                    moved = pltpu.roll(came[j], (slab * j - HALO - offset[x]) % lanes, 1)
                    whole = moved if whole is None else jnp.where(lane >= slab * j, moved, whole)
                buf[f, x] = whole
        pltpu.make_async_copy(buf, out, sems.at[k]).start()
    for k, (buf, out) in enumerate(((vbuf, vout_ref), (sbuf, sout_ref))):
        pltpu.make_async_copy(buf, out, sems.at[k]).wait()


def slabs(sizes, velocity, stress, region_map, lame_table, shear_table, buoy_table,
          block_pattern, block_wave, block_x, block_dest):
    nx, ny, nz = sizes
    cx, half, lanes = velocity.shape[1:]
    blocks = block_pattern.shape[0]
    pairs = cx // 2
    total = nx * pairs
    tile = (half, lanes)
    vmem = pl.BlockSpec(memory_space=pltpu.VMEM)
    hbm = pl.BlockSpec(memory_space=pl.ANY)
    f32, i32 = jnp.float32, jnp.int32
    dma = pltpu.SemaphoreType.DMA
    came = pl.pallas_call(
        functools.partial(slab_kernel, sizes),
        out_shape=(pltpu.VMEM((nx, 3) + tile, f32), pltpu.VMEM((nx, 6) + tile, f32)),
        in_specs=[hbm] * 10,
        out_specs=(vmem, vmem),
        scratch_shapes=[
            pltpu.VMEM(velocity.shape, f32),
            pltpu.VMEM(stress.shape, f32),
            pltpu.VMEM(region_map.shape, i32),
            pltpu.VMEM((3, blocks, lanes), f32),
            pltpu.VMEM((STEPS, blocks), f32),
            pltpu.VMEM((1, blocks), i32),
            pltpu.VMEM((1, blocks), i32),
            pltpu.SMEM(lame_table.shape, f32),
            pltpu.SMEM(lame_table.shape, f32),
            pltpu.SMEM(lame_table.shape, f32),
            pltpu.VMEM((nx, FIELDS, pairs) + tile, f32),
            pltpu.VMEM((2, -(-FIELDS * pairs // BANDS)) + tile, f32),
            pltpu.VMEM((nx, 2, -(-FIELDS * pairs // BANDS)) + tile, f32),
            pltpu.VMEM((FIELDS, total, 4 * half, lanes), f32),
            pltpu.VMEM((3, total, 2 * half, lanes), f32),
            pltpu.VMEM((3, total, 2 * half, lanes), f32),
            pltpu.VMEM((2, 2 * lanes, lanes), jnp.bfloat16),
            pltpu.VMEM((ny, nx, STEPS) + tile, f32),
            pltpu.VMEM((nx, ny, STEPS) + tile, f32),
            pltpu.VMEM((STEPS, nx) + tile, f32),
            pltpu.VMEM((nx, 2, 3) + tile, f32),
            pltpu.VMEM((nx, 2, 6) + tile, f32),
            dma((10,)),
            dma((nx, 2)),
            dma((nx, 2, 2)),
            dma((5,)),
            dma((2,)),
            dma((nx, 2)),
            dma((ny, nx, 2)),
            dma((nx, ny, 2)),
            dma((nx, 2, 2)),
            dma((nx, 2)),
            pltpu.SemaphoreType.REGULAR,
            pltpu.SemaphoreType.REGULAR,
        ],
        compiler_params=pltpu.CompilerParams(collective_id=0, has_side_effects=True),
        name="slabs",
    )(
        velocity,
        stress,
        region_map,
        lame_table,
        shear_table,
        buoy_table,
        block_pattern.transpose(1, 0, 2),
        block_wave.T,
        block_x.reshape(1, blocks),
        block_dest.reshape(1, blocks),
    )
    return pl.pallas_call(
        weave,
        out_shape=(jax.ShapeDtypeStruct(velocity.shape, f32), jax.ShapeDtypeStruct(stress.shape, f32)),
        in_specs=[vmem, vmem],
        out_specs=(hbm, hbm),
        scratch_shapes=[pltpu.VMEM(velocity.shape, f32), pltpu.VMEM(stress.shape, f32), dma((2,))],
        name="weave",
    )(*(pltpu.with_memory_space_constraint(c, pltpu.VMEM) for c in came))


def local(sizes, velocity, *rest):
    nx, ny, nz = sizes
    cx, half, lanes = velocity.shape[1:]
    fits = nz == 2 and cx == 4 and half == 8 and lanes == 128 and lanes // nx + 2 * HALO == WIDE
    return (slabs if fits else shards)(sizes, velocity, *rest)


def solution(mesh):
    sizes = tuple(mesh.shape[a] for a in ("gx", "gy", "gz"))
    field = P(None, "gx", "gz", "gy")
    both = ("gx", "gy")
    placed = (
        field,
        field,
        P("gx", "gz", "gy"),
        P(),
        P(),
        P(),
        P(both, None, None),
        P(both, None),
        P(both),
        P(both, None),
    )
    return jax.shard_map(
        functools.partial(local, sizes),
        mesh=mesh,
        in_specs=placed,
        out_specs=(field, field),
        check_vma=False,
    )
```

```python
import functools
import jax
import jax.numpy as jnp
from jax import lax
from jax.experimental import pallas as pl
from jax.experimental.pallas import tpu as pltpu
from jax.sharding import PartitionSpec as P

STEPS = 4
ROUNDS = 2 * STEPS

NEAR = 9.0 / 8.0
FAR = 1.0 / 24.0
DT = 0.13
MESH = pl.DeviceIdType.MESH


def masks(shape, axis):
    n = shape[axis]
    at = lax.broadcasted_iota(jnp.int32, shape, axis)

    def split(test, value):
        inside = jnp.where(test, 0.0, value).astype(jnp.float32)
        across = jnp.where(test, value, 0.0).astype(jnp.float32)
        return inside, across

    fwd = (
        (n - 1, split(at == n - 1, NEAR)),
        (n - 2, split(at >= n - 2, -FAR)),
        (1, split(at == 0, FAR)),
    )
    bwd = (
        (1, split(at == 0, -NEAR)),
        (2, split(at < 2, FAR)),
        (n - 1, split(at == n - 1, -FAR)),
    )
    return {"f": (fwd, -NEAR), "b": (bwd, NEAR)}


def in_tile(f, way, coefs, axis):
    terms, own = coefs[way]
    inside = own * f
    across = None
    for turn, (here, there) in terms:
        rolled = pltpu.roll(f, turn, axis)
        inside = inside + here[None] * rolled
        add = there[None] * rolled
        across = add if across is None else across + add
    return inside, across


def kernel(
    sizes,
    vel_ref,
    str_ref,
    reg_ref,
    lame_ref,
    shear_ref,
    buoy_ref,
    pat_ref,
    wave_ref,
    bx_ref,
    dest_ref,
    vout_ref,
    sout_ref,
    part,
    got,
    sxr,
    sxl,
    hxl,
    hxr,
    sy,
    hy,
    vin,
    sin,
    rin,
    vo,
    so,
    ssem,
    rsem,
    fs,
    fr,
    ls,
    lr,
    ld,
):
    nx, ny, nz = sizes
    ix, iy, iz = lax.axis_index("gx"), lax.axis_index("gy"), lax.axis_index("gz")
    cx, half = vel_ref.shape[1:3]
    tile = (2 * half, vel_ref.shape[3])
    lead = iz == nz - 1
    low, high = pl.ds(0, half), pl.ds(half, half)
    has_l, has_r = lead & (ix > 0), lead & (ix < nx - 1)
    has_d, has_u = lead & (iy > 0), lead & (iy < ny - 1)

    barrier = pltpu.get_barrier_semaphore()

    def greet(cond, where):
        @pl.when(cond)
        def _():
            pl.semaphore_signal(barrier, inc=1, device_id=where, device_id_type=MESH)

        return cond.astype(jnp.int32)

    count = greet(has_l, {"gx": ix - 1}) + greet(has_r, {"gx": ix + 1}) + 1
    pl.semaphore_signal(barrier, inc=1, device_id={"gz": 1 - iz}, device_id_type=MESH)
    for d in range(ny):
        count = count + greet(lead & (iy != d), {"gy": d})

    def hand(src, dst, k):
        return pltpu.make_async_remote_copy(
            src_ref=src,
            dst_ref=dst,
            send_sem=ls.at[k],
            recv_sem=lr.at[k],
            device_id={"gz": 1 - iz},
            device_id_type=MESH,
        )

    given = (
        hand(str_ref, sin.at[:, :, low], 0),
        hand(vel_ref, vin.at[:, :, low], 1),
        hand(reg_ref, rin.at[:, low], 2),
    )
    back = (hand(vo, vout_ref, 3), hand(so, sout_ref, 4))

    @pl.when(jnp.logical_not(lead))
    def _():
        pl.semaphore_wait(barrier, count)
        for copy in given:
            copy.start()
        for copy in given:
            copy.wait_send()
        for copy in back:
            copy.wait_recv()

    @pl.when(lead)
    def _():
        own = (
            pltpu.make_async_copy(str_ref, sin.at[:, :, high], ld.at[0]),
            pltpu.make_async_copy(vel_ref, vin.at[:, :, high], ld.at[1]),
            pltpu.make_async_copy(reg_ref, rin.at[:, high], ld.at[2]),
        )
        for copy in own:
            copy.start()
        @pl.when(jnp.logical_not(has_l))
        def _():
            hxl[...] = jnp.zeros_like(hxl)

        @pl.when(jnp.logical_not(has_r))
        def _():
            hxr[...] = jnp.zeros_like(hxr)

        @pl.when(jnp.logical_not(has_d))
        def _():
            hy[:, 0] = jnp.zeros_like(hy[:, 0])

        @pl.when(jnp.logical_not(has_u))
        def _():
            hy[:, 1] = jnp.zeros_like(hy[:, 1])

        rows = STEPS * cx

        if True:
            blocks = pat_ref.shape[1]
            row = lax.broadcasted_iota(jnp.int32, (ny * rows, blocks), 0)
            moment = (row // cx) % STEPS
            spot = (row // rows) * cx + row % cx
            key = dest_ref[...] * cx + bx_ref[...]
            amount = jnp.zeros((ny * rows, blocks), jnp.float32)
            for t in range(STEPS):
                amount = jnp.where(moment == t, wave_ref[t : t + 1, :], amount)
            weights = jnp.where(spot == key, amount, 0.0)
            for c in range(3):
                sums = jnp.dot(
                    weights,
                    pat_ref[c],
                    precision=lax.Precision.HIGHEST,
                    preferred_element_type=jnp.float32,
                )
                for d in range(ny):
                    part[d, c] = sums[d * rows : (d + 1) * rows]
            got[iy] = part[iy]

        lane = masks(tile, 1)
        sub = masks(tile, 0)
        at_lane = lax.broadcasted_iota(jnp.int32, tile, 1)
        at_sub = lax.broadcasted_iota(jnp.int32, tile, 0)
        n_lane = tile[1]
        edge_lane = (at_lane < 2) | (at_lane >= n_lane - 2)
        from_low = at_lane % 4 < 2

        def rdma(src, dst, r, k, where):
            return pltpu.make_async_remote_copy(
                src_ref=src,
                dst_ref=dst,
                send_sem=ssem.at[r, k],
                recv_sem=rsem.at[r, k],
                device_id=where,
                device_id_type=MESH,
            )

        def copies(r):
            to_r, to_l = (5, 4) if r % 2 == 0 else (4, 5)
            return (
                (has_r, has_l, rdma(sxr.at[r, pl.ds(0, to_r)], hxl.at[r, pl.ds(0, to_r)], r, 0, {"gx": ix + 1})),
                (has_l, has_r, rdma(sxl.at[r, pl.ds(0, to_l)], hxr.at[r, pl.ds(0, to_l)], r, 1, {"gx": ix - 1})),
                (has_u, has_d, rdma(sy.at[r], hy.at[r, 0], r, 2, {"gy": iy + 1})),
                (has_d, has_u, rdma(sy.at[r], hy.at[r, 1], r, 3, {"gy": iy - 1})),
            )

        def when(cond, act):
            if cond is None:
                act()
            else:
                pl.when(cond)(act)

        def derivatives(r, fx, fy, fz, first=None):
            to_r = [(f, w) for f, w in fx]
            moves = copies(r)
            k = 0
            for f, way in fx:
                for p in (cx - 1,) if way == "f" else (cx - 2, cx - 1):
                    sxr[r, k] = f[p]
                    k += 1
            k = 0
            for f, way in fx:
                for p in (0, 1) if way == "f" else (0,):
                    sxl[r, k] = f[p]
                    k += 1
            if first is not None:
                first()
            odd = ix % 2 == 1
            when(has_r & odd, moves[0][2].start)
            when(has_l, moves[1][2].start)
            when(has_r & jnp.logical_not(odd), moves[0][2].start)
            dy, packed, slot = [], None, 0
            for f, way in fy:
                inside, across = in_tile(f, way, lane, 2)
                dy.append(inside)
                for p in range(cx):
                    turned = across[p] if slot == 0 else pltpu.roll(across[p], 4 * slot, 1)
                    packed = turned if packed is None else packed + turned
                    slot += 1
            sy[r] = packed
            for m in moves[2:4]:
                when(m[0], m[2].start)
            dz = []
            for f, way in fz:
                dz.append(in_tile(f, way, sub, 1)[0])

            def finish():
                out_z = dz
                for m in moves[2:4]:
                    when(m[1], m[2].wait_recv)
                both = jnp.where(from_low, hy[r, 0], hy[r, 1])
                out_y = []
                for c in range(3):
                    planes = []
                    for p in range(cx):
                        slot = c * cx + p
                        turned = both if slot == 0 else pltpu.roll(both, n_lane - 4 * slot, 1)
                        planes.append(jnp.where(edge_lane, turned, 0.0))
                    out_y.append(dy[c] + jnp.stack(planes))
                for m in moves[:2]:
                    when(m[1], m[2].wait_recv)
                out_x, kl, kr = [], 0, 0
                for f, way in fx:
                    left = 1 if way == "f" else 2
                    right = 3 - left
                    pad = jnp.concatenate([hxl[r, kl : kl + left], f, hxr[r, kr : kr + right]], axis=0)
                    kl, kr = kl + left, kr + right
                    s = [pad[i : i + cx] for i in range(4)]
                    out_x.append(NEAR * (s[2] - s[1]) - FAR * (s[3] - s[0]))
                return out_x, out_y, out_z

            return finish

        def forces(act):
            for d in range(ny):
                @pl.when(iy != d)
                def _():
                    copy = pltpu.make_async_remote_copy(
                        src_ref=part.at[d],
                        dst_ref=got.at[iy if act == "start" else d],
                        send_sem=fs.at[d],
                        recv_sem=fr.at[iy if act == "start" else d],
                        device_id={"gy": d},
                        device_id_type=MESH,
                    )
                    getattr(copy, act)()

        def enter():
            pl.semaphore_wait(barrier, count)
            forces("start")

        own[0].wait()
        given[0].wait_recv()
        vel = None
        txx, tyy, tzz, txy, txz, tyz = [sin[c] for c in range(6)]
        surface = None
        for t in range(STEPS):
            finish = derivatives(
                2 * t,
                ((txx, "f"), (txy, "b"), (txz, "b")),
                ((txy, "b"), (tyy, "f"), (tyz, "b")),
                ((txz, "b"), (tyz, "b"), (tzz, "f")),
                enter if t == 0 else None,
            )
            if t == 0:
                for k in (1, 2):
                    own[k].wait()
                    given[k].wait_recv()
                vel = [vin[c] for c in range(3)]
                region = rin[...]
                lame = jnp.zeros(region.shape, jnp.float32)
                shear, buoy = lame, lame
                for k in range(lame_ref.shape[0]):
                    hit = region == k
                    lame = jnp.where(hit, lame_ref[k], lame)
                    shear = jnp.where(hit, shear_ref[k], shear)
                    buoy = jnp.where(hit, buoy_ref[k], buoy)
                lame, shear, buoy = DT * lame, DT * shear, DT * buoy
                forces("wait_recv")
                for c in range(3):
                    total = got[0, c]
                    for s in range(1, ny):
                        total = total + got[s, c]
                    got[0, c] = total
            dx, dy, dz = finish()
            for c in range(3):
                push = jnp.stack(
                    [
                        jnp.where(at_sub == 0, got[0, c, t * cx + p : t * cx + p + 1, :], 0.0)
                        for p in range(cx)
                    ]
                )
                vel[c] = vel[c] + buoy * (dx[c] + dy[c] + dz[c] + push)
            vx, vy, vz = vel
            if t == STEPS - 1:
                for c in range(3):
                    vo[c] = vel[c][:, :half]
            finish = derivatives(
                2 * t + 1,
                ((vx, "b"), (vy, "f"), (vz, "f")),
                ((vx, "f"), (vy, "b"), (vz, "f")),
                ((vx, "f"), (vy, "f"), (vz, "b")),
            )
            if t == STEPS - 1:
                back[0].start()
                for c in range(3):
                    vout_ref[c] = vel[c][:, half:]
            dx, dy, dz = finish()
            trace = lame * (dx[0] + dy[1] + dz[2])
            twice = 2.0 * shear
            txx = txx + (trace + twice * dx[0])
            tyy = tyy + (trace + twice * dy[1])
            tzz = tzz + (trace + twice * dz[2])
            txy = txy + shear * (dy[0] + dx[1])
            txz = txz + shear * (dz[0] + dx[2])
            tyz = tyz + shear * (dz[1] + dy[2])
        for c, f in enumerate((txx, tyy, tzz, txy, txz, tyz)):
            so[c] = f[:, :half]
            sout_ref[c] = f[:, half:]
        back[1].start()
        forces("wait_send")
        for r in range(ROUNDS):
            for m in copies(r):
                when(m[0], m[2].wait_send)
        for copy in back:
            copy.wait_send()


def shards(sizes, velocity, stress, region_map, lame_table, shear_table, buoy_table,
           block_pattern, block_wave, block_x, block_dest):
    cx = velocity.shape[1]
    tile = (2 * velocity.shape[2], velocity.shape[3])
    blocks = block_pattern.shape[0]
    ny = sizes[1]
    vmem = pl.BlockSpec(memory_space=pltpu.VMEM)
    smem = pl.BlockSpec(memory_space=pltpu.SMEM)
    hbm = pl.BlockSpec(memory_space=pl.ANY)
    f32 = jnp.float32
    held = pl.pallas_call(
        functools.partial(kernel, sizes),
        out_shape=(pltpu.VMEM(velocity.shape, f32), pltpu.VMEM(stress.shape, f32)),
        in_specs=[hbm, hbm, hbm, smem, smem, smem, vmem, vmem, vmem, vmem],
        out_specs=(vmem, vmem),
        scratch_shapes=[
            pltpu.VMEM((ny, 3, STEPS * cx, tile[1]), f32),
            pltpu.VMEM((ny, 3, STEPS * cx, tile[1]), f32),
            pltpu.VMEM((ROUNDS, 5) + tile, f32),
            pltpu.VMEM((ROUNDS, 5) + tile, f32),
            pltpu.VMEM((ROUNDS, 5) + tile, f32),
            pltpu.VMEM((ROUNDS, 5) + tile, f32),
            pltpu.VMEM((ROUNDS,) + tile, f32),
            pltpu.VMEM((ROUNDS, 2) + tile, f32),
            pltpu.VMEM((3, cx) + tile, f32),
            pltpu.VMEM((6, cx) + tile, f32),
            pltpu.VMEM((cx,) + tile, jnp.int32),
            pltpu.VMEM(velocity.shape, f32),
            pltpu.VMEM(stress.shape, f32),
            pltpu.SemaphoreType.DMA((ROUNDS, 4)),
            pltpu.SemaphoreType.DMA((ROUNDS, 4)),
            pltpu.SemaphoreType.DMA((ny,)),
            pltpu.SemaphoreType.DMA((ny,)),
            pltpu.SemaphoreType.DMA((5,)),
            pltpu.SemaphoreType.DMA((5,)),
            pltpu.SemaphoreType.DMA((3,)),
        ],
        compiler_params=pltpu.CompilerParams(collective_id=0, has_side_effects=True),
        name="waves",
    )(
        velocity,
        stress,
        region_map,
        lame_table,
        shear_table,
        buoy_table,
        block_pattern.transpose(1, 0, 2),
        block_wave.T,
        block_x.reshape(1, blocks),
        block_dest.reshape(1, blocks),
    )
    return held


HALO = 16
WIDE = 64
FIELDS = 10
FIRST = 7
BAND = 12
BANDS = WIDE // BAND


def slab_kernel(
    sizes,
    vel_ref,
    str_ref,
    reg_ref,
    lame_ref,
    shear_ref,
    buoy_ref,
    pat_ref,
    wave_ref,
    bx_ref,
    dest_ref,
    back_v,
    back_s,
    raw,
    raw_r,
    pat,
    wave,
    bx,
    dest,
    lame_t,
    shear_t,
    buoy_t,
    packed,
    strip,
    got_strip,
    grid,
    coef,
    early,
    taps,
    push_out,
    push_in,
    push,
    done_v,
    done_s,
    isem,
    bulk_ss,
    bulk_rs,
    own_ss,
    strip_ss,
    strip_rs,
    push_ss,
    push_rs,
    back_ss,
    back_rs,
    go,
    far,
):
    nx, ny, nz = sizes
    ix, iy, iz = lax.axis_index("gx"), lax.axis_index("gy"), lax.axis_index("gz")
    cx, half, lanes = vel_ref.shape[1:]
    pairs = cx // 2
    total = nx * pairs
    last = nx - 1
    top = nz - 1
    lead = iz == top
    slab = lanes // nx
    has_d, has_u = iy > 0, iy < ny - 1
    tall = pl.ds(half, 2 * half)
    peers = (last - ix, lax.rem(ix + 2, nx), ix + 1 - 2 * lax.rem(ix, 2))
    groups = (pl.ds(0, FIRST), pl.ds(FIRST, FIELDS - FIRST))

    barrier = pltpu.get_barrier_semaphore()

    def signal(where):
        pl.semaphore_signal(barrier, inc=1, device_id=where, device_id_type=MESH)

    at = lax.broadcasted_iota(jnp.int32, (half, lanes), 1)
    at_lane = at
    at = at % WIDE
    spin = [(HALO - slab * j) % lanes for j in range(nx)]

    def remote(src, dst, ssem, rsem, where):
        return pltpu.make_async_remote_copy(
            src_ref=src, dst_ref=dst, send_sem=ssem, recv_sem=rsem, device_id=where, device_id_type=MESH
        )

    loads = (
        pltpu.make_async_copy(str_ref, raw.at[pl.ds(0, FIRST - 1)], isem.at[0]),
        pltpu.make_async_copy(vel_ref, raw.at[pl.ds(FIRST, 3)], isem.at[1]),
        pltpu.make_async_copy(reg_ref, raw_r, isem.at[2]),
    )
    tables = (
        pltpu.make_async_copy(lame_ref, lame_t, isem.at[3]),
        pltpu.make_async_copy(shear_ref, shear_t, isem.at[4]),
        pltpu.make_async_copy(buoy_ref, buoy_t, isem.at[5]),
    )
    blocks_in = (
        pltpu.make_async_copy(pat_ref, pat, isem.at[6]),
        pltpu.make_async_copy(wave_ref, wave, isem.at[7]),
        pltpu.make_async_copy(bx_ref, bx, isem.at[8]),
        pltpu.make_async_copy(dest_ref, dest, isem.at[9]),
    )

    def blends(even, odd):
        odd = pltpu.roll(odd, WIDE, 1)
        out = []
        for r in spin:
            begin = (lanes - r) % lanes
            inside = at_lane >= begin
            if begin + WIDE <= lanes:
                inside = inside & (at_lane < begin + WIDE)
            else:
                inside = inside | (at_lane < begin + WIDE - lanes)
            out.append(jnp.where(inside, even, odd))
        return out

    def windows(even, odd):
        return [pltpu.roll(both, r, 1) for both, r in zip(blends(even, odd), spin, strict=True)]

    def pack():
        for copy in loads:
            copy.wait()
        edges = [None, None]
        for f in range(FIELDS):
            for p in range(pairs):
                i = f * pairs + p
                g = i % BANDS
                pair = [raw_r[2 * p + q].astype(jnp.float32) if f == FIRST - 1 else raw[f, 2 * p + q] for q in range(2)]
                mixed = blends(*pair)
                for j in range(nx):
                    both = pltpu.roll(mixed[j], spin[j], 1)
                    if j in (0, last):
                        way = 0 if j == 0 else 1
                        origin = HALO - BAND if j == 0 else WIDE - HALO
                        moved = pltpu.roll(mixed[j], (spin[j] + BAND * g - origin) % lanes, 1)
                        edges[way] = moved if g == 0 else jnp.where(at >= BAND * g, moved, edges[way])
                        if g == BANDS - 1:
                            strip[way, i // BANDS] = edges[way]
                        both = jnp.where(at < HALO if j == 0 else at >= WIDE - HALO, 0.0, both)
                    packed[j, f, p] = both

    def place(j, zt, part):
        return grid.at[groups[part], pl.ds(pairs * j, pairs), pl.ds(half * (zt + 1), half)]

    def bulk(to, zt, part):
        return remote(
            packed.at[to, groups[part]],
            place(ix, zt, part),
            bulk_ss.at[to, part],
            bulk_rs.at[ix, zt, part],
            {"gx": to, "gz": top},
        )

    def arrived(j, zt, part):
        remote(
            packed.at[j, groups[part]],
            place(j, zt, part),
            bulk_ss.at[j, part],
            bulk_rs.at[j, zt, part],
            {"gx": j, "gz": top},
        ).wait_recv()

    def edge(way, zt):
        where = {"gx": 0, "gy": iy + 1, "gz": top} if way == 0 else {"gx": last, "gy": iy - 1, "gz": top}
        return remote(strip.at[way], got_strip.at[ix, zt], strip_ss.at[way], strip_rs.at[ix, zt], where)

    def edge_arrived(j, zt):
        remote(strip.at[0], got_strip.at[j, zt], strip_ss.at[0], strip_rs.at[j, zt], {"gx": j, "gz": top}).wait_recv()

    def edges_do(zt, act):
        @pl.when(has_u)
        def _():
            getattr(edge(0, zt), act)()

        @pl.when(has_d)
        def _():
            getattr(edge(1, zt), act)()

    def result(to, zt, part):
        done, back = ((done_v, back_v), (done_s, back_s))[part]
        return remote(
            done.at[to, zt], back.at[ix], back_ss.at[to, zt, part], back_rs.at[ix, part], {"gx": to, "gz": zt}
        )

    def result_wait(j):
        for part in range(2):
            done, back = ((done_v, back_v), (done_s, back_s))[part]
            remote(
                done.at[j, 0], back.at[j], back_ss.at[j, 0, part], back_rs.at[j, part], {"gx": j, "gz": top}
            ).wait_recv()

    def keep(part):
        return pltpu.make_async_copy(packed.at[ix, groups[part]], place(ix, top, part), own_ss.at[part])

    def send(d, j, part):
        src, dst = push_out.at[d, j, spans[part]], push_in.at[ix, iy, spans[part]]
        return remote(src, dst, push_ss.at[d, j, part], push_rs.at[ix, iy, part], {"gx": j, "gy": d, "gz": top})

    def force_maker():
        for copy in blocks_in:
            copy.wait()
        blocks = pat.shape[1]
        size = 2 * half
        row = lax.broadcasted_iota(jnp.int32, (ny * size, blocks), 0)
        spot = (row // size) * cx + (row % pairs) * 2 + (row // half) % 2
        hit = spot == dest[...] * cx + bx[...]

        def forces(m):
            entry = half * m + row % half
            moment, kind = entry // (3 * pairs), (entry // pairs) % 3
            amount = jnp.zeros(row.shape, jnp.float32)
            for t in range(STEPS):
                amount = jnp.where(hit & (moment == t), wave[t : t + 1, :], amount)
            sums = None
            for c in range(3):
                term = jnp.dot(
                    jnp.where(kind == c, amount, 0.0),
                    pat[c],
                    precision=lax.Precision.HIGHEST,
                    preferred_element_type=jnp.float32,
                )
                sums = term if sums is None else sums + term
            views = [
                windows(sums[d * size : d * size + half], sums[d * size + half : (d + 1) * size])
                for d in range(ny)
            ]
            for d in range(ny):
                for j in range(nx):
                    both = views[d][j]
                    if j == 0:
                        both = jnp.where(at < HALO, views[d - 1][j] if d > 0 else 0.0, both)
                    if j == last:
                        both = jnp.where(at >= WIDE - HALO, views[d + 1][j] if d < ny - 1 else 0.0, both)
                    push_out[d, j, m] = both

        return forces

    tiles = push_in.shape[2]
    spans = (pl.ds(0, 1), pl.ds(1, tiles - 1))
    rest = pltpu.make_async_copy(push_out.at[iy, ix, spans[1]], push_in.at[ix, iy, spans[1]], own_ss.at[4])

    @pl.when(lead)
    def _():
        for to in peers:
            signal({"gx": to})

        @pl.when((ix == 0) & has_d)
        def _():
            for j in range(nx):
                signal({"gx": j, "gy": iy - 1})

        @pl.when((ix == last) & has_u)
        def _():
            for j in range(nx):
                signal({"gx": j, "gy": iy + 1})

        for copy in loads + tables + blocks_in:
            copy.start()
        for d in range(ny):
            for j in range(nx):
                signal({"gx": j, "gy": d, "gz": 0})
        blank = jnp.zeros((FIELDS, total, half, lanes), jnp.float32)
        grid[:, :, pl.ds(0, half)] = blank
        grid[:, :, pl.ds(3 * half, half)] = blank
        pack()
        source = lax.broadcasted_iota(jnp.int32, (lanes, lanes), 0)
        target = lax.broadcasted_iota(jnp.int32, (lanes, lanes), 1)
        for way in range(2):
            off = source - target + way
            tap = jnp.where(off == 1, NEAR / FAR, 0.0) + jnp.where(off == 0, -NEAR / FAR, 0.0)
            tap = tap + jnp.where(off == -1, 1.0, 0.0) + jnp.where(off == 2, -1.0, 0.0)
            tap = jnp.where(source // WIDE == target // WIDE, tap, 0.0).astype(jnp.bfloat16)
            taps[way, pl.ds(0, lanes)] = tap
            taps[way, pl.ds(lanes, lanes)] = tap
        pl.semaphore_wait(barrier, nx + has_d.astype(jnp.int32) + has_u.astype(jnp.int32))
        pl.semaphore_signal(go, inc=1, device_id={"gz": 0}, device_id_type=MESH)
        edges_do(top, "start")
        for part in range(2):
            for to in peers:
                bulk(to, top, part).start()
            keep(part).start()
        forces = force_maker()
        lax.fori_loop(1, tiles, lambda m, carry: (forces(m), carry)[1], 0)
        pl.semaphore_wait(far, 1)
        for d in range(ny):
            for j in range(nx):
                pl.when((ix != j) | (iy != d))(send(d, j, 1).start)
        rest.start()

    @pl.when(jnp.logical_not(lead))
    def _():
        signal({"gz": top})
        for copy in loads + blocks_in:
            copy.start()
        pack()
        pl.semaphore_wait(go, 1)
        edges_do(0, "start")
        for to in peers:
            bulk(to, 0, 0).start()
        bulk(ix, 0, 0).start()
        for to in peers:
            bulk(to, 0, 1).start()
        bulk(ix, 0, 1).start()
        forces = force_maker()
        forces(0)
        for j in range(nx):
            remote(
                push_out.at[iy, j, pl.ds(0, 1)],
                push_in.at[ix, iy, pl.ds(0, 1)],
                push_ss.at[iy, j, 0],
                push_rs.at[ix, iy, 0],
                {"gx": j, "gz": top},
            ).start()
        pl.semaphore_wait(barrier, nx * ny)
        pl.semaphore_signal(far, inc=1, device_id={"gz": top}, device_id_type=MESH)
        for d in range(ny):
            for j in range(nx):
                pl.when(iy != d)(send(d, j, 0).start)
        for d in range(ny):
            for j in range(nx):
                send(d, j, 0).wait_send()
        for part in range(2):
            for j in range(nx):
                bulk(j, 0, part).wait_send()
        edges_do(0, "wait_send")
        for j in range(nx):
            result_wait(j)

    @pl.when(lead)
    def _():
        shape = (2 * half, lanes)
        lane = lax.broadcasted_iota(jnp.int32, shape, 1)
        left = lane < WIDE
        lane = lane % WIDE
        first = lax.broadcasted_iota(jnp.int32, shape, 0) == 0
        beyond = ((lane < HALO) & (ix == 0) & (iy == 0)) | (
            (lane >= WIDE - HALO) & (ix == last) & (iy == ny - 1)
        )
        within = jnp.where(beyond, 0.0, DT * FAR).astype(jnp.float32)
        ratio = NEAR / FAR
        zero = jnp.zeros(shape, jnp.float32)

        def bulk_wait(part):
            keep(part).wait()
            for j in range(nx):
                arrived(j, 0, part)

                @pl.when(ix != j)
                def _():
                    arrived(j, top, part)

        def merges(part):
            at_low = (ix == 0) & has_d
            at_high = (ix == last) & has_u

            @pl.when(at_low | at_high)
            def _():
                if part == 0:
                    for j in range(nx):
                        for zt in range(2):
                            edge_arrived(j, zt)
                origin = jnp.where(ix == 0, HALO - BAND, WIDE - HALO)
                bound = jnp.where(ix == 0, HALO, WIDE - HALO)
                inside = (at >= bound) == (ix == 0)

                def body(j, carry):
                    for zt in range(2):
                        for f in range(*((0, FIRST), (FIRST, FIELDS))[part]):
                            for p in range(pairs):
                                i = f * pairs + p
                                shift = lax.rem(origin + lanes - BAND * (i % BANDS), lanes)
                                moved = pltpu.roll(got_strip[j, zt, i // BANDS], shift, 1)
                                here = (f, pairs * j + p, pl.ds(half * (zt + 1), half))
                                grid[here] = jnp.where(inside, grid[here], moved)
                    return carry

                lax.fori_loop(0, nx, body, 0)

        def push_wait(part):
            if part == 1:
                rest.wait()
            for j in range(nx):
                for i in range(ny):
                    came = remote(
                        push_out.at[0, 0, spans[part]],
                        push_in.at[j, i, spans[part]],
                        push_ss.at[0, 0, part],
                        push_rs.at[j, i, part],
                        {"gz": 0},
                    )
                    if part == 0:
                        came.wait_recv()
                    else:
                        pl.when((ix != j) | (iy != i))(came.wait_recv)
            for m in (0,) if part == 0 else range(1, tiles):
                for j in range(nx):
                    amount = push_in[j, 0, m]
                    for i in range(1, ny):
                        amount = amount + push_in[j, i, m]
                    push[j, half * m : half * (m + 1)] = (1.0 / FAR) * amount

        def rows(f, k, s):
            return grid[f, k, pl.ds(half + s, 2 * half)]

        def turned(memo, f, k):
            if k < 0 or k >= total:
                return zero
            if (f, k) not in memo:
                memo[f, k] = pltpu.roll(grid[f, k, tall], WIDE, 1)
            return memo[f, k]

        def step(memo, f, k):
            if (f, k, "s") not in memo:
                memo[f, k, "s"] = jnp.where(left, turned(memo, f, k - 1), turned(memo, f, k))
            return memo[f, k, "s"]

        def along_x(memo, f, way, k):
            v, near, far = grid[f, k, tall], step(memo, f, k), step(memo, f, k + 1)
            if way == "f":
                after = grid[f, k + 1, tall] if k + 1 < total else zero
                return ratio * (far - v) - (after - near)
            before = grid[f, k - 1, tall] if k > 0 else zero
            return ratio * (v - near) - (far - before)

        def along_y(f, way):
            v = grid[f, :, tall].reshape(total * 2 * half, lanes)
            coarse = v.astype(jnp.bfloat16)
            fine = (v - coarse.astype(jnp.float32)).astype(jnp.bfloat16)
            out = jnp.dot(
                jnp.concatenate([coarse, fine], axis=1),
                taps[0 if way == "f" else 1],
                preferred_element_type=jnp.float32,
            )
            return [out[2 * half * k : 2 * half * (k + 1)] for k in range(total)]

        def along_z(f, way, k):
            o = 0 if way == "b" else 1
            return ratio * (rows(f, k, o) - rows(f, k, o - 1)) - (rows(f, k, o + 1) - rows(f, k, o - 2))

        txx, tyy, tzz, txy, txz, tyz = range(6)
        vx, vy, vz = range(FIRST, FIRST + 3)

        def rates(use):
            memo = {}
            dy = along_y(txy, "b"), along_y(tyy, "f"), along_y(tyz, "b")
            for k in range(total):
                for c, (fx, wx, fz, wz) in enumerate(
                    ((txx, "f", txz, "b"), (txy, "b", tyz, "b"), (txz, "b", tzz, "f"))
                ):
                    use(c, k, along_x(memo, fx, wx, k) + along_z(fz, wz, k) + dy[c][k])

        def kick(t, c, k, rate):
            now = push[k // pairs, pl.ds((t * 3 + c) * pairs + k % pairs, 1), :]
            grid[vx + c, k, tall] = grid[vx + c, k, tall] + coef[2, k] * (rate + jnp.where(first, now, 0.0))

        def strain():
            memo = {}
            dy = along_y(vx, "f"), along_y(vy, "b"), along_y(vz, "f")
            for k in range(total):
                exx, eyy, ezz = along_x(memo, vx, "b", k), dy[1][k], along_z(vz, "b", k)
                shear = coef[1, k]
                twice = 2.0 * shear
                trace = coef[0, k] * (exx + eyy + ezz)
                grid[txx, k, tall] = grid[txx, k, tall] + (trace + twice * exx)
                grid[tyy, k, tall] = grid[tyy, k, tall] + (trace + twice * eyy)
                grid[tzz, k, tall] = grid[tzz, k, tall] + (trace + twice * ezz)
                grid[txy, k, tall] = grid[txy, k, tall] + shear * (dy[0][k] + along_x(memo, vy, "f", k))
                grid[txz, k, tall] = grid[txz, k, tall] + shear * (along_z(vx, "f", k) + along_x(memo, vz, "f", k))
                grid[tyz, k, tall] = grid[tyz, k, tall] + shear * (along_z(vy, "f", k) + dy[2][k])

        own_lanes = (at >= HALO) & (at < HALO + slab)

        def finish(part):
            done, start, count = ((done_v, FIRST, 3), (done_s, 0, 6))[part]
            def body(j, carry):
                for zt in range(2):
                    for f in range(count):
                        here = pl.ds(half * (zt + 1), half)
                        a, b = grid[start + f, pairs * j, here], grid[start + f, pairs * j + 1, here]
                        done[j, zt, f] = jnp.where(own_lanes, a, pltpu.roll(b, slab, 1))
                return carry

            lax.fori_loop(0, nx, body, 0)
            for to in peers:
                for zt in range(2):
                    result(to, zt, part).start()
            result(ix, 0, part).start()

        def mine(part):
            done, back = ((done_v, back_v), (done_s, back_s))[part]
            return pltpu.make_async_copy(done.at[ix, top], back.at[ix], own_ss.at[2 + part])

        for copy in tables:
            copy.wait()
        bulk_wait(0)
        merges(0)

        def fill(k, carry):
            region = grid[FIRST - 1, k, tall]
            picks = [zero] * 3
            for r in range(lame_t.shape[0]):
                hit = region == float(r)
                for q, table in enumerate((lame_t, shear_t, buoy_t)):
                    picks[q] = jnp.where(hit, table[r], picks[q])
            for q in range(3):
                coef[q, k] = within * picks[q]
            return carry

        for k in range(total):
            fill(k, 0)

        def store(c, k, rate):
            early[c, k] = rate

        rates(store)
        bulk_wait(1)
        merges(1)
        push_wait(0)
        for c in range(3):
            for k in range(total):
                kick(0, c, k, early[c, k])
        strain()
        push_wait(1)

        def middle(t, carry):
            rates(functools.partial(kick, t))
            strain()
            return carry

        lax.fori_loop(1, STEPS - 1, middle, 0)
        rates(functools.partial(kick, STEPS - 1))
        finish(0)
        mine(0).start()
        strain()
        finish(1)
        mine(1).start()

        for part in range(2):
            for to in peers:
                bulk(to, top, part).wait_send()
        for d in range(ny):
            for j in range(nx):
                pl.when((ix != j) | (iy != d))(send(d, j, 1).wait_send)
        edges_do(top, "wait_send")
        for part in range(2):
            mine(part).wait()
            for to in peers:
                for zt in range(2):
                    result(to, zt, part).wait_send()
            result(ix, 0, part).wait_send()
        for j in range(nx):
            @pl.when(ix != j)
            def _():
                result_wait(j)


def weave(back_v, back_s, vout_ref, sout_ref, vbuf, sbuf, sems):
    nx, _, half, lanes = back_v.shape
    slab = lanes // nx
    cx = vbuf.shape[1]
    offset = (0, WIDE, slab, WIDE + slab)
    lane = lax.broadcasted_iota(jnp.int32, (half, lanes), 1)
    for k, (back, buf, out) in enumerate(((back_v, vbuf, vout_ref), (back_s, sbuf, sout_ref))):
        for f in range(back.shape[1]):
            came = [back[j, f] for j in range(nx)]
            for x in range(cx):
                whole = None
                for j in range(nx):
                    moved = pltpu.roll(came[j], (slab * j - HALO - offset[x]) % lanes, 1)
                    whole = moved if whole is None else jnp.where(lane >= slab * j, moved, whole)
                buf[f, x] = whole
        pltpu.make_async_copy(buf, out, sems.at[k]).start()
    for k, (buf, out) in enumerate(((vbuf, vout_ref), (sbuf, sout_ref))):
        pltpu.make_async_copy(buf, out, sems.at[k]).wait()


def slabs(sizes, velocity, stress, region_map, lame_table, shear_table, buoy_table,
          block_pattern, block_wave, block_x, block_dest):
    nx, ny, nz = sizes
    cx, half, lanes = velocity.shape[1:]
    blocks = block_pattern.shape[0]
    pairs = cx // 2
    total = nx * pairs
    tile = (half, lanes)
    vmem = pl.BlockSpec(memory_space=pltpu.VMEM)
    hbm = pl.BlockSpec(memory_space=pl.ANY)
    tiles = STEPS * 3 * pairs // half
    f32, i32 = jnp.float32, jnp.int32
    dma = pltpu.SemaphoreType.DMA
    came = pl.pallas_call(
        functools.partial(slab_kernel, sizes),
        out_shape=(pltpu.VMEM((nx, 3) + tile, f32), pltpu.VMEM((nx, 6) + tile, f32)),
        in_specs=[hbm] * 10,
        out_specs=(vmem, vmem),
        scratch_shapes=[
            pltpu.VMEM((FIELDS, cx) + tile, f32),
            pltpu.VMEM(region_map.shape, i32),
            pltpu.VMEM((3, blocks, lanes), f32),
            pltpu.VMEM((STEPS, blocks), f32),
            pltpu.VMEM((1, blocks), i32),
            pltpu.VMEM((1, blocks), i32),
            pltpu.SMEM(lame_table.shape, f32),
            pltpu.SMEM(lame_table.shape, f32),
            pltpu.SMEM(lame_table.shape, f32),
            pltpu.VMEM((nx, FIELDS, pairs) + tile, f32),
            pltpu.VMEM((2, -(-FIELDS * pairs // BANDS)) + tile, f32),
            pltpu.VMEM((nx, 2, -(-FIELDS * pairs // BANDS)) + tile, f32),
            pltpu.VMEM((FIELDS, total, 4 * half, lanes), f32),
            pltpu.VMEM((3, total, 2 * half, lanes), f32),
            pltpu.VMEM((3, total, 2 * half, lanes), f32),
            pltpu.VMEM((2, 2 * lanes, lanes), jnp.bfloat16),
            pltpu.VMEM((ny, nx, tiles) + tile, f32),
            pltpu.VMEM((nx, ny, tiles) + tile, f32),
            pltpu.VMEM((nx, tiles * half, lanes), f32),
            pltpu.VMEM((nx, 2, 3) + tile, f32),
            pltpu.VMEM((nx, 2, 6) + tile, f32),
            dma((10,)),
            dma((nx, 2)),
            dma((nx, 2, 2)),
            dma((5,)),
            dma((2,)),
            dma((nx, 2)),
            dma((ny, nx, 2)),
            dma((nx, ny, 2)),
            dma((nx, 2, 2)),
            dma((nx, 2)),
            pltpu.SemaphoreType.REGULAR,
            pltpu.SemaphoreType.REGULAR,
        ],
        compiler_params=pltpu.CompilerParams(collective_id=0, has_side_effects=True),
        name="slabs",
    )(
        velocity,
        stress,
        region_map,
        lame_table,
        shear_table,
        buoy_table,
        block_pattern.transpose(1, 0, 2),
        block_wave.T,
        block_x.reshape(1, blocks),
        block_dest.reshape(1, blocks),
    )
    return pl.pallas_call(
        weave,
        out_shape=(jax.ShapeDtypeStruct(velocity.shape, f32), jax.ShapeDtypeStruct(stress.shape, f32)),
        in_specs=[vmem, vmem],
        out_specs=(hbm, hbm),
        scratch_shapes=[pltpu.VMEM(velocity.shape, f32), pltpu.VMEM(stress.shape, f32), dma((2,))],
        name="weave",
    )(*(pltpu.with_memory_space_constraint(c, pltpu.VMEM) for c in came))


def local(sizes, velocity, *rest):
    nx, ny, nz = sizes
    cx, half, lanes = velocity.shape[1:]
    fits = nz == 2 and cx == 4 and half == 8 and lanes == 128 and lanes // nx + 2 * HALO == WIDE
    return (slabs if fits else shards)(sizes, velocity, *rest)


def solution(mesh):
    sizes = tuple(mesh.shape[a] for a in ("gx", "gy", "gz"))
    field = P(None, "gx", "gz", "gy")
    both = ("gx", "gy")
    placed = (
        field,
        field,
        P("gx", "gz", "gy"),
        P(),
        P(),
        P(),
        P(both, None, None),
        P(both, None),
        P(both),
        P(both, None),
    )
    return jax.shard_map(
        functools.partial(local, sizes),
        mesh=mesh,
        in_specs=placed,
        out_specs=(field, field),
        check_vma=False,
    )
```

```python
import functools
import jax
import jax.numpy as jnp
from jax import lax
from jax.experimental import pallas as pl
from jax.experimental.pallas import tpu as pltpu
from jax.sharding import PartitionSpec as P

STEPS = 4
ROUNDS = 2 * STEPS

NEAR = 9.0 / 8.0
FAR = 1.0 / 24.0
DT = 0.13
MESH = pl.DeviceIdType.MESH


def masks(shape, axis):
    n = shape[axis]
    at = lax.broadcasted_iota(jnp.int32, shape, axis)

    def split(test, value):
        inside = jnp.where(test, 0.0, value).astype(jnp.float32)
        across = jnp.where(test, value, 0.0).astype(jnp.float32)
        return inside, across

    fwd = (
        (n - 1, split(at == n - 1, NEAR)),
        (n - 2, split(at >= n - 2, -FAR)),
        (1, split(at == 0, FAR)),
    )
    bwd = (
        (1, split(at == 0, -NEAR)),
        (2, split(at < 2, FAR)),
        (n - 1, split(at == n - 1, -FAR)),
    )
    return {"f": (fwd, -NEAR), "b": (bwd, NEAR)}


def in_tile(f, way, coefs, axis):
    terms, own = coefs[way]
    inside = own * f
    across = None
    for turn, (here, there) in terms:
        rolled = pltpu.roll(f, turn, axis)
        inside = inside + here[None] * rolled
        add = there[None] * rolled
        across = add if across is None else across + add
    return inside, across


def kernel(
    sizes,
    vel_ref,
    str_ref,
    reg_ref,
    lame_ref,
    shear_ref,
    buoy_ref,
    pat_ref,
    wave_ref,
    bx_ref,
    dest_ref,
    vout_ref,
    sout_ref,
    part,
    got,
    sxr,
    sxl,
    hxl,
    hxr,
    sy,
    hy,
    vin,
    sin,
    rin,
    vo,
    so,
    ssem,
    rsem,
    fs,
    fr,
    ls,
    lr,
    ld,
):
    nx, ny, nz = sizes
    ix, iy, iz = lax.axis_index("gx"), lax.axis_index("gy"), lax.axis_index("gz")
    cx, half = vel_ref.shape[1:3]
    tile = (2 * half, vel_ref.shape[3])
    lead = iz == nz - 1
    low, high = pl.ds(0, half), pl.ds(half, half)
    has_l, has_r = lead & (ix > 0), lead & (ix < nx - 1)
    has_d, has_u = lead & (iy > 0), lead & (iy < ny - 1)

    barrier = pltpu.get_barrier_semaphore()

    def greet(cond, where):
        @pl.when(cond)
        def _():
            pl.semaphore_signal(barrier, inc=1, device_id=where, device_id_type=MESH)

        return cond.astype(jnp.int32)

    count = greet(has_l, {"gx": ix - 1}) + greet(has_r, {"gx": ix + 1}) + 1
    pl.semaphore_signal(barrier, inc=1, device_id={"gz": 1 - iz}, device_id_type=MESH)
    for d in range(ny):
        count = count + greet(lead & (iy != d), {"gy": d})

    def hand(src, dst, k):
        return pltpu.make_async_remote_copy(
            src_ref=src,
            dst_ref=dst,
            send_sem=ls.at[k],
            recv_sem=lr.at[k],
            device_id={"gz": 1 - iz},
            device_id_type=MESH,
        )

    given = (
        hand(str_ref, sin.at[:, :, low], 0),
        hand(vel_ref, vin.at[:, :, low], 1),
        hand(reg_ref, rin.at[:, low], 2),
    )
    back = (hand(vo, vout_ref, 3), hand(so, sout_ref, 4))

    @pl.when(jnp.logical_not(lead))
    def _():
        pl.semaphore_wait(barrier, count)
        for copy in given:
            copy.start()
        for copy in given:
            copy.wait_send()
        for copy in back:
            copy.wait_recv()

    @pl.when(lead)
    def _():
        own = (
            pltpu.make_async_copy(str_ref, sin.at[:, :, high], ld.at[0]),
            pltpu.make_async_copy(vel_ref, vin.at[:, :, high], ld.at[1]),
            pltpu.make_async_copy(reg_ref, rin.at[:, high], ld.at[2]),
        )
        for copy in own:
            copy.start()
        @pl.when(jnp.logical_not(has_l))
        def _():
            hxl[...] = jnp.zeros_like(hxl)

        @pl.when(jnp.logical_not(has_r))
        def _():
            hxr[...] = jnp.zeros_like(hxr)

        @pl.when(jnp.logical_not(has_d))
        def _():
            hy[:, 0] = jnp.zeros_like(hy[:, 0])

        @pl.when(jnp.logical_not(has_u))
        def _():
            hy[:, 1] = jnp.zeros_like(hy[:, 1])

        rows = STEPS * cx

        if True:
            blocks = pat_ref.shape[1]
            row = lax.broadcasted_iota(jnp.int32, (ny * rows, blocks), 0)
            moment = (row // cx) % STEPS
            spot = (row // rows) * cx + row % cx
            key = dest_ref[...] * cx + bx_ref[...]
            amount = jnp.zeros((ny * rows, blocks), jnp.float32)
            for t in range(STEPS):
                amount = jnp.where(moment == t, wave_ref[t : t + 1, :], amount)
            weights = jnp.where(spot == key, amount, 0.0)
            for c in range(3):
                sums = jnp.dot(
                    weights,
                    pat_ref[c],
                    precision=lax.Precision.HIGHEST,
                    preferred_element_type=jnp.float32,
                )
                for d in range(ny):
                    part[d, c] = sums[d * rows : (d + 1) * rows]
            got[iy] = part[iy]

        lane = masks(tile, 1)
        sub = masks(tile, 0)
        at_lane = lax.broadcasted_iota(jnp.int32, tile, 1)
        at_sub = lax.broadcasted_iota(jnp.int32, tile, 0)
        n_lane = tile[1]
        edge_lane = (at_lane < 2) | (at_lane >= n_lane - 2)
        from_low = at_lane % 4 < 2

        def rdma(src, dst, r, k, where):
            return pltpu.make_async_remote_copy(
                src_ref=src,
                dst_ref=dst,
                send_sem=ssem.at[r, k],
                recv_sem=rsem.at[r, k],
                device_id=where,
                device_id_type=MESH,
            )

        def copies(r):
            to_r, to_l = (5, 4) if r % 2 == 0 else (4, 5)
            return (
                (has_r, has_l, rdma(sxr.at[r, pl.ds(0, to_r)], hxl.at[r, pl.ds(0, to_r)], r, 0, {"gx": ix + 1})),
                (has_l, has_r, rdma(sxl.at[r, pl.ds(0, to_l)], hxr.at[r, pl.ds(0, to_l)], r, 1, {"gx": ix - 1})),
                (has_u, has_d, rdma(sy.at[r], hy.at[r, 0], r, 2, {"gy": iy + 1})),
                (has_d, has_u, rdma(sy.at[r], hy.at[r, 1], r, 3, {"gy": iy - 1})),
            )

        def when(cond, act):
            if cond is None:
                act()
            else:
                pl.when(cond)(act)

        def derivatives(r, fx, fy, fz, first=None):
            to_r = [(f, w) for f, w in fx]
            moves = copies(r)
            k = 0
            for f, way in fx:
                for p in (cx - 1,) if way == "f" else (cx - 2, cx - 1):
                    sxr[r, k] = f[p]
                    k += 1
            k = 0
            for f, way in fx:
                for p in (0, 1) if way == "f" else (0,):
                    sxl[r, k] = f[p]
                    k += 1
            if first is not None:
                first()
            odd = ix % 2 == 1
            when(has_r & odd, moves[0][2].start)
            when(has_l, moves[1][2].start)
            when(has_r & jnp.logical_not(odd), moves[0][2].start)
            dy, packed, slot = [], None, 0
            for f, way in fy:
                inside, across = in_tile(f, way, lane, 2)
                dy.append(inside)
                for p in range(cx):
                    turned = across[p] if slot == 0 else pltpu.roll(across[p], 4 * slot, 1)
                    packed = turned if packed is None else packed + turned
                    slot += 1
            sy[r] = packed
            for m in moves[2:4]:
                when(m[0], m[2].start)
            dz = []
            for f, way in fz:
                dz.append(in_tile(f, way, sub, 1)[0])

            def finish():
                out_z = dz
                for m in moves[2:4]:
                    when(m[1], m[2].wait_recv)
                both = jnp.where(from_low, hy[r, 0], hy[r, 1])
                out_y = []
                for c in range(3):
                    planes = []
                    for p in range(cx):
                        slot = c * cx + p
                        turned = both if slot == 0 else pltpu.roll(both, n_lane - 4 * slot, 1)
                        planes.append(jnp.where(edge_lane, turned, 0.0))
                    out_y.append(dy[c] + jnp.stack(planes))
                for m in moves[:2]:
                    when(m[1], m[2].wait_recv)
                out_x, kl, kr = [], 0, 0
                for f, way in fx:
                    left = 1 if way == "f" else 2
                    right = 3 - left
                    pad = jnp.concatenate([hxl[r, kl : kl + left], f, hxr[r, kr : kr + right]], axis=0)
                    kl, kr = kl + left, kr + right
                    s = [pad[i : i + cx] for i in range(4)]
                    out_x.append(NEAR * (s[2] - s[1]) - FAR * (s[3] - s[0]))
                return out_x, out_y, out_z

            return finish

        def forces(act):
            for d in range(ny):
                @pl.when(iy != d)
                def _():
                    copy = pltpu.make_async_remote_copy(
                        src_ref=part.at[d],
                        dst_ref=got.at[iy if act == "start" else d],
                        send_sem=fs.at[d],
                        recv_sem=fr.at[iy if act == "start" else d],
                        device_id={"gy": d},
                        device_id_type=MESH,
                    )
                    getattr(copy, act)()

        def enter():
            pl.semaphore_wait(barrier, count)
            forces("start")

        own[0].wait()
        given[0].wait_recv()
        vel = None
        txx, tyy, tzz, txy, txz, tyz = [sin[c] for c in range(6)]
        surface = None
        for t in range(STEPS):
            finish = derivatives(
                2 * t,
                ((txx, "f"), (txy, "b"), (txz, "b")),
                ((txy, "b"), (tyy, "f"), (tyz, "b")),
                ((txz, "b"), (tyz, "b"), (tzz, "f")),
                enter if t == 0 else None,
            )
            if t == 0:
                for k in (1, 2):
                    own[k].wait()
                    given[k].wait_recv()
                vel = [vin[c] for c in range(3)]
                region = rin[...]
                lame = jnp.zeros(region.shape, jnp.float32)
                shear, buoy = lame, lame
                for k in range(lame_ref.shape[0]):
                    hit = region == k
                    lame = jnp.where(hit, lame_ref[k], lame)
                    shear = jnp.where(hit, shear_ref[k], shear)
                    buoy = jnp.where(hit, buoy_ref[k], buoy)
                lame, shear, buoy = DT * lame, DT * shear, DT * buoy
                forces("wait_recv")
                for c in range(3):
                    total = got[0, c]
                    for s in range(1, ny):
                        total = total + got[s, c]
                    got[0, c] = total
            dx, dy, dz = finish()
            for c in range(3):
                push = jnp.stack(
                    [
                        jnp.where(at_sub == 0, got[0, c, t * cx + p : t * cx + p + 1, :], 0.0)
                        for p in range(cx)
                    ]
                )
                vel[c] = vel[c] + buoy * (dx[c] + dy[c] + dz[c] + push)
            vx, vy, vz = vel
            if t == STEPS - 1:
                for c in range(3):
                    vo[c] = vel[c][:, :half]
            finish = derivatives(
                2 * t + 1,
                ((vx, "b"), (vy, "f"), (vz, "f")),
                ((vx, "f"), (vy, "b"), (vz, "f")),
                ((vx, "f"), (vy, "f"), (vz, "b")),
            )
            if t == STEPS - 1:
                back[0].start()
                for c in range(3):
                    vout_ref[c] = vel[c][:, half:]
            dx, dy, dz = finish()
            trace = lame * (dx[0] + dy[1] + dz[2])
            twice = 2.0 * shear
            txx = txx + (trace + twice * dx[0])
            tyy = tyy + (trace + twice * dy[1])
            tzz = tzz + (trace + twice * dz[2])
            txy = txy + shear * (dy[0] + dx[1])
            txz = txz + shear * (dz[0] + dx[2])
            tyz = tyz + shear * (dz[1] + dy[2])
        for c, f in enumerate((txx, tyy, tzz, txy, txz, tyz)):
            so[c] = f[:, :half]
            sout_ref[c] = f[:, half:]
        back[1].start()
        forces("wait_send")
        for r in range(ROUNDS):
            for m in copies(r):
                when(m[0], m[2].wait_send)
        for copy in back:
            copy.wait_send()


def shards(sizes, velocity, stress, region_map, lame_table, shear_table, buoy_table,
           block_pattern, block_wave, block_x, block_dest):
    cx = velocity.shape[1]
    tile = (2 * velocity.shape[2], velocity.shape[3])
    blocks = block_pattern.shape[0]
    ny = sizes[1]
    vmem = pl.BlockSpec(memory_space=pltpu.VMEM)
    smem = pl.BlockSpec(memory_space=pltpu.SMEM)
    hbm = pl.BlockSpec(memory_space=pl.ANY)
    f32 = jnp.float32
    held = pl.pallas_call(
        functools.partial(kernel, sizes),
        out_shape=(pltpu.VMEM(velocity.shape, f32), pltpu.VMEM(stress.shape, f32)),
        in_specs=[hbm, hbm, hbm, smem, smem, smem, vmem, vmem, vmem, vmem],
        out_specs=(vmem, vmem),
        scratch_shapes=[
            pltpu.VMEM((ny, 3, STEPS * cx, tile[1]), f32),
            pltpu.VMEM((ny, 3, STEPS * cx, tile[1]), f32),
            pltpu.VMEM((ROUNDS, 5) + tile, f32),
            pltpu.VMEM((ROUNDS, 5) + tile, f32),
            pltpu.VMEM((ROUNDS, 5) + tile, f32),
            pltpu.VMEM((ROUNDS, 5) + tile, f32),
            pltpu.VMEM((ROUNDS,) + tile, f32),
            pltpu.VMEM((ROUNDS, 2) + tile, f32),
            pltpu.VMEM((3, cx) + tile, f32),
            pltpu.VMEM((6, cx) + tile, f32),
            pltpu.VMEM((cx,) + tile, jnp.int32),
            pltpu.VMEM(velocity.shape, f32),
            pltpu.VMEM(stress.shape, f32),
            pltpu.SemaphoreType.DMA((ROUNDS, 4)),
            pltpu.SemaphoreType.DMA((ROUNDS, 4)),
            pltpu.SemaphoreType.DMA((ny,)),
            pltpu.SemaphoreType.DMA((ny,)),
            pltpu.SemaphoreType.DMA((5,)),
            pltpu.SemaphoreType.DMA((5,)),
            pltpu.SemaphoreType.DMA((3,)),
        ],
        compiler_params=pltpu.CompilerParams(collective_id=0, has_side_effects=True),
        name="waves",
    )(
        velocity,
        stress,
        region_map,
        lame_table,
        shear_table,
        buoy_table,
        block_pattern.transpose(1, 0, 2),
        block_wave.T,
        block_x.reshape(1, blocks),
        block_dest.reshape(1, blocks),
    )
    return held


HALO = 16
WIDE = 64
FIELDS = 10
FIRST = 7
BAND = 12
BANDS = WIDE // BAND


def slab_kernel(
    sizes,
    vel_ref,
    str_ref,
    reg_ref,
    lame_ref,
    shear_ref,
    buoy_ref,
    pat_ref,
    wave_ref,
    bx_ref,
    dest_ref,
    back_v,
    back_s,
    raw,
    raw_r,
    pat,
    wave,
    bx,
    dest,
    lame_t,
    shear_t,
    buoy_t,
    packed,
    strip,
    got_strip,
    grid,
    coef,
    early,
    taps,
    push_out,
    push_in,
    push,
    done_v,
    done_s,
    isem,
    bulk_ss,
    bulk_rs,
    strip_ss,
    strip_rs,
    push_ss,
    push_rs,
    back_ss,
    back_rs,
    go,
    far,
):
    nx, ny, nz = sizes
    ix, iy, iz = lax.axis_index("gx"), lax.axis_index("gy"), lax.axis_index("gz")
    cx, half, lanes = vel_ref.shape[1:]
    pairs = cx // 2
    total = nx * pairs
    last = nx - 1
    top = nz - 1
    lead = iz == top
    slab = lanes // nx
    has_d, has_u = iy > 0, iy < ny - 1
    tall = pl.ds(half, 2 * half)
    peers = (last - ix, lax.rem(ix + 2, nx), ix + 1 - 2 * lax.rem(ix, 2))
    groups = (pl.ds(0, FIRST), pl.ds(FIRST, FIELDS - FIRST))

    barrier = pltpu.get_barrier_semaphore()

    def signal(where):
        pl.semaphore_signal(barrier, inc=1, device_id=where, device_id_type=MESH)

    at = lax.broadcasted_iota(jnp.int32, (half, lanes), 1)
    at_lane = at
    at = at % WIDE
    spin = [(HALO - slab * j) % lanes for j in range(nx)]

    def remote(src, dst, ssem, rsem, where):
        return pltpu.make_async_remote_copy(
            src_ref=src, dst_ref=dst, send_sem=ssem, recv_sem=rsem, device_id=where, device_id_type=MESH
        )

    loads = (
        pltpu.make_async_copy(str_ref, raw.at[pl.ds(0, FIRST - 1)], isem.at[0]),
        pltpu.make_async_copy(vel_ref, raw.at[pl.ds(FIRST, 3)], isem.at[1]),
        pltpu.make_async_copy(reg_ref, raw_r, isem.at[2]),
    )
    tables = (
        pltpu.make_async_copy(lame_ref, lame_t, isem.at[3]),
        pltpu.make_async_copy(shear_ref, shear_t, isem.at[4]),
        pltpu.make_async_copy(buoy_ref, buoy_t, isem.at[5]),
    )
    blocks_in = (
        pltpu.make_async_copy(pat_ref, pat, isem.at[6]),
        pltpu.make_async_copy(wave_ref, wave, isem.at[7]),
        pltpu.make_async_copy(bx_ref, bx, isem.at[8]),
        pltpu.make_async_copy(dest_ref, dest, isem.at[9]),
    )

    def blends(even, odd):
        odd = pltpu.roll(odd, WIDE, 1)
        out = []
        for r in spin:
            begin = (lanes - r) % lanes
            inside = at_lane >= begin
            if begin + WIDE <= lanes:
                inside = inside & (at_lane < begin + WIDE)
            else:
                inside = inside | (at_lane < begin + WIDE - lanes)
            out.append(jnp.where(inside, even, odd))
        return out

    def windows(even, odd):
        return [pltpu.roll(both, r, 1) for both, r in zip(blends(even, odd), spin, strict=True)]

    def pack():
        for copy in loads:
            copy.wait()
        edges = [None, None]
        for f in range(FIELDS):
            for p in range(pairs):
                i = f * pairs + p
                g = i % BANDS
                pair = [raw_r[2 * p + q].astype(jnp.float32) if f == FIRST - 1 else raw[f, 2 * p + q] for q in range(2)]
                mixed = blends(*pair)
                for j in range(nx):
                    both = pltpu.roll(mixed[j], spin[j], 1)
                    if j in (0, last):
                        way = 0 if j == 0 else 1
                        origin = HALO - BAND if j == 0 else WIDE - HALO
                        moved = pltpu.roll(mixed[j], (spin[j] + BAND * g - origin) % lanes, 1)
                        edges[way] = moved if g == 0 else jnp.where(at >= BAND * g, moved, edges[way])
                        if g == BANDS - 1:
                            strip[way, i // BANDS] = edges[way]
                        both = jnp.where(at < HALO if j == 0 else at >= WIDE - HALO, 0.0, both)
                    packed[j, f, p] = both

    def place(j, zt, part):
        return grid.at[groups[part], pl.ds(pairs * j, pairs), pl.ds(half * (zt + 1), half)]

    def bulk(to, zt, part):
        return remote(
            packed.at[to, groups[part]],
            place(ix, zt, part),
            bulk_ss.at[to, part],
            bulk_rs.at[part],
            {"gx": to, "gz": top},
        )

    def arrived(ref, sem):
        remote(ref, ref, sem, sem, {"gz": 0}).wait_recv()

    def edge(way, zt):
        where = {"gx": 0, "gy": iy + 1, "gz": top} if way == 0 else {"gx": last, "gy": iy - 1, "gz": top}
        return remote(strip.at[way], got_strip.at[ix, zt], strip_ss.at[way], strip_rs.at[0], where)

    def edges_do(zt, act):
        @pl.when(has_u)
        def _():
            getattr(edge(0, zt), act)()

        @pl.when(has_d)
        def _():
            getattr(edge(1, zt), act)()

    def result(to, zt, part):
        done, back = ((done_v, back_v), (done_s, back_s))[part]
        return remote(
            done.at[to, zt], back.at[ix], back_ss.at[to, zt, part], back_rs.at[part], {"gx": to, "gz": zt}
        )

    def results_wait():
        arrived(back_v, back_rs.at[0])
        arrived(back_s, back_rs.at[1])

    def keep(part):
        return pltpu.make_async_copy(packed.at[ix, groups[part]], place(ix, top, part), bulk_rs.at[part])

    def send(d, j, part):
        src, dst = push_out.at[d, j, spans[part]], push_in.at[ix, iy, spans[part]]
        return remote(src, dst, push_ss.at[d, j, part], push_rs.at[part], {"gx": j, "gy": d, "gz": top})

    def force_maker():
        for copy in blocks_in:
            copy.wait()
        blocks = pat.shape[1]
        size = 2 * half
        row = lax.broadcasted_iota(jnp.int32, (ny * size, blocks), 0)
        spot = (row // size) * cx + (row % pairs) * 2 + (row // half) % 2
        hit = spot == dest[...] * cx + bx[...]

        def forces(m):
            entry = half * m + row % half
            moment, kind = entry // (3 * pairs), (entry // pairs) % 3
            amount = jnp.zeros(row.shape, jnp.float32)
            for t in range(STEPS):
                amount = jnp.where(hit & (moment == t), wave[t : t + 1, :], amount)
            sums = None
            for c in range(3):
                term = jnp.dot(
                    jnp.where(kind == c, amount, 0.0),
                    pat[c],
                    precision=lax.Precision.HIGHEST,
                    preferred_element_type=jnp.float32,
                )
                sums = term if sums is None else sums + term
            views = [
                windows(sums[d * size : d * size + half], sums[d * size + half : (d + 1) * size])
                for d in range(ny)
            ]
            for d in range(ny):
                for j in range(nx):
                    both = views[d][j]
                    if j == 0:
                        both = jnp.where(at < HALO, views[d - 1][j] if d > 0 else 0.0, both)
                    if j == last:
                        both = jnp.where(at >= WIDE - HALO, views[d + 1][j] if d < ny - 1 else 0.0, both)
                    push_out[d, j, m] = both

        return forces

    tiles = push_in.shape[2]
    spans = (pl.ds(0, 1), pl.ds(1, tiles - 1))
    rest = pltpu.make_async_copy(push_out.at[iy, ix, spans[1]], push_in.at[ix, iy, spans[1]], push_rs.at[1])

    @pl.when(lead)
    def _():
        for to in peers:
            signal({"gx": to})

        @pl.when((ix == 0) & has_d)
        def _():
            for j in range(nx):
                signal({"gx": j, "gy": iy - 1})

        @pl.when((ix == last) & has_u)
        def _():
            for j in range(nx):
                signal({"gx": j, "gy": iy + 1})

        for copy in loads + tables + blocks_in:
            copy.start()
        for d in range(ny):
            for j in range(nx):
                signal({"gx": j, "gy": d, "gz": 0})
        blank = jnp.zeros((FIELDS, total, half, lanes), jnp.float32)
        grid[:, :, pl.ds(0, half)] = blank
        grid[:, :, pl.ds(3 * half, half)] = blank
        pack()
        source = lax.broadcasted_iota(jnp.int32, (lanes, lanes), 0)
        target = lax.broadcasted_iota(jnp.int32, (lanes, lanes), 1)
        for way in range(2):
            off = source - target + way
            tap = jnp.where(off == 1, NEAR / FAR, 0.0) + jnp.where(off == 0, -NEAR / FAR, 0.0)
            tap = tap + jnp.where(off == -1, 1.0, 0.0) + jnp.where(off == 2, -1.0, 0.0)
            tap = jnp.where(source // WIDE == target // WIDE, tap, 0.0).astype(jnp.bfloat16)
            taps[way, pl.ds(0, lanes)] = tap
            taps[way, pl.ds(lanes, lanes)] = tap
        pl.semaphore_wait(barrier, nx + has_d.astype(jnp.int32) + has_u.astype(jnp.int32))
        pl.semaphore_signal(go, inc=1, device_id={"gz": 0}, device_id_type=MESH)
        edges_do(top, "start")
        for part in range(2):
            for to in peers:
                bulk(to, top, part).start()
            keep(part).start()
        forces = force_maker()
        lax.fori_loop(1, tiles, lambda m, carry: (forces(m), carry)[1], 0)
        pl.semaphore_wait(far, 1)
        for d in range(ny):
            for j in range(nx):
                pl.when((ix != j) | (iy != d))(send(d, j, 1).start)
        rest.start()

    @pl.when(jnp.logical_not(lead))
    def _():
        signal({"gz": top})
        for copy in loads + blocks_in:
            copy.start()
        pack()
        pl.semaphore_wait(go, 1)
        edges_do(0, "start")
        for to in peers:
            bulk(to, 0, 0).start()
        bulk(ix, 0, 0).start()
        for to in peers:
            bulk(to, 0, 1).start()
        bulk(ix, 0, 1).start()
        forces = force_maker()
        forces(0)
        for j in range(nx):
            remote(
                push_out.at[iy, j, pl.ds(0, 1)],
                push_in.at[ix, iy, pl.ds(0, 1)],
                push_ss.at[iy, j, 0],
                push_rs.at[0],
                {"gx": j, "gz": top},
            ).start()
        pl.semaphore_wait(barrier, nx * ny)
        pl.semaphore_signal(far, inc=1, device_id={"gz": top}, device_id_type=MESH)
        for d in range(ny):
            for j in range(nx):
                pl.when(iy != d)(send(d, j, 0).start)
        for d in range(ny):
            for j in range(nx):
                send(d, j, 0).wait_send()
        for part in range(2):
            for j in range(nx):
                bulk(j, 0, part).wait_send()
        edges_do(0, "wait_send")
        results_wait()

    @pl.when(lead)
    def _():
        shape = (2 * half, lanes)
        lane = lax.broadcasted_iota(jnp.int32, shape, 1)
        left = lane < WIDE
        lane = lane % WIDE
        first = lax.broadcasted_iota(jnp.int32, shape, 0) == 0
        beyond = ((lane < HALO) & (ix == 0) & (iy == 0)) | (
            (lane >= WIDE - HALO) & (ix == last) & (iy == ny - 1)
        )
        within = jnp.where(beyond, 0.0, DT * FAR).astype(jnp.float32)
        ratio = NEAR / FAR
        zero = jnp.zeros(shape, jnp.float32)

        def bulk_wait(part):
            arrived(grid.at[groups[part], :, tall], bulk_rs.at[part])

        def merges(part):
            at_low = (ix == 0) & has_d
            at_high = (ix == last) & has_u

            @pl.when(at_low | at_high)
            def _():
                if part == 0:
                    arrived(got_strip, strip_rs.at[0])
                origin = jnp.where(ix == 0, HALO - BAND, WIDE - HALO)
                bound = jnp.where(ix == 0, HALO, WIDE - HALO)
                inside = (at >= bound) == (ix == 0)

                def body(j, carry):
                    for zt in range(2):
                        for f in range(*((0, FIRST), (FIRST, FIELDS))[part]):
                            for p in range(pairs):
                                i = f * pairs + p
                                shift = lax.rem(origin + lanes - BAND * (i % BANDS), lanes)
                                moved = pltpu.roll(got_strip[j, zt, i // BANDS], shift, 1)
                                here = (f, pairs * j + p, pl.ds(half * (zt + 1), half))
                                grid[here] = jnp.where(inside, grid[here], moved)
                    return carry

                lax.fori_loop(0, nx, body, 0)

        def push_wait(part):
            arrived(push_in.at[:, :, spans[part]], push_rs.at[part])
            for m in (0,) if part == 0 else range(1, tiles):
                for j in range(nx):
                    amount = push_in[j, 0, m]
                    for i in range(1, ny):
                        amount = amount + push_in[j, i, m]
                    push[j, half * m : half * (m + 1)] = (1.0 / FAR) * amount

        def rows(f, k, s):
            return grid[f, k, pl.ds(half + s, 2 * half)]

        def turned(memo, f, k):
            if k < 0 or k >= total:
                return zero
            if (f, k) not in memo:
                memo[f, k] = pltpu.roll(grid[f, k, tall], WIDE, 1)
            return memo[f, k]

        def step(memo, f, k):
            if (f, k, "s") not in memo:
                memo[f, k, "s"] = jnp.where(left, turned(memo, f, k - 1), turned(memo, f, k))
            return memo[f, k, "s"]

        def along_x(memo, f, way, k):
            v, near, far = grid[f, k, tall], step(memo, f, k), step(memo, f, k + 1)
            if way == "f":
                after = grid[f, k + 1, tall] if k + 1 < total else zero
                return ratio * (far - v) - (after - near)
            before = grid[f, k - 1, tall] if k > 0 else zero
            return ratio * (v - near) - (far - before)

        def along_y(f, way):
            v = grid[f, :, tall].reshape(total * 2 * half, lanes)
            coarse = v.astype(jnp.bfloat16)
            fine = (v - coarse.astype(jnp.float32)).astype(jnp.bfloat16)
            out = jnp.dot(
                jnp.concatenate([coarse, fine], axis=1),
                taps[0 if way == "f" else 1],
                preferred_element_type=jnp.float32,
            )
            return [out[2 * half * k : 2 * half * (k + 1)] for k in range(total)]

        def along_z(f, way, k):
            o = 0 if way == "b" else 1
            return ratio * (rows(f, k, o) - rows(f, k, o - 1)) - (rows(f, k, o + 1) - rows(f, k, o - 2))

        txx, tyy, tzz, txy, txz, tyz = range(6)
        vx, vy, vz = range(FIRST, FIRST + 3)

        def rates(use):
            memo = {}
            dy = along_y(txy, "b"), along_y(tyy, "f"), along_y(tyz, "b")
            for k in range(total):
                for c, (fx, wx, fz, wz) in enumerate(
                    ((txx, "f", txz, "b"), (txy, "b", tyz, "b"), (txz, "b", tzz, "f"))
                ):
                    use(c, k, along_x(memo, fx, wx, k) + along_z(fz, wz, k) + dy[c][k])

        def kick(t, c, k, rate):
            now = push[k // pairs, pl.ds((t * 3 + c) * pairs + k % pairs, 1), :]
            grid[vx + c, k, tall] = grid[vx + c, k, tall] + coef[2, k] * (rate + jnp.where(first, now, 0.0))

        def strain():
            memo = {}
            dy = along_y(vx, "f"), along_y(vy, "b"), along_y(vz, "f")
            for k in range(total):
                exx, eyy, ezz = along_x(memo, vx, "b", k), dy[1][k], along_z(vz, "b", k)
                shear = coef[1, k]
                twice = 2.0 * shear
                trace = coef[0, k] * (exx + eyy + ezz)
                grid[txx, k, tall] = grid[txx, k, tall] + (trace + twice * exx)
                grid[tyy, k, tall] = grid[tyy, k, tall] + (trace + twice * eyy)
                grid[tzz, k, tall] = grid[tzz, k, tall] + (trace + twice * ezz)
                grid[txy, k, tall] = grid[txy, k, tall] + shear * (dy[0][k] + along_x(memo, vy, "f", k))
                grid[txz, k, tall] = grid[txz, k, tall] + shear * (along_z(vx, "f", k) + along_x(memo, vz, "f", k))
                grid[tyz, k, tall] = grid[tyz, k, tall] + shear * (along_z(vy, "f", k) + dy[2][k])

        own_lanes = (at >= HALO) & (at < HALO + slab)

        def finish(part):
            done, start, count = ((done_v, FIRST, 3), (done_s, 0, 6))[part]
            def body(j, carry):
                for zt in range(2):
                    for f in range(count):
                        here = pl.ds(half * (zt + 1), half)
                        a, b = grid[start + f, pairs * j, here], grid[start + f, pairs * j + 1, here]
                        done[j, zt, f] = jnp.where(own_lanes, a, pltpu.roll(b, slab, 1))
                return carry

            lax.fori_loop(0, nx, body, 0)
            for to in peers:
                for zt in range(2):
                    result(to, zt, part).start()
            result(ix, 0, part).start()

        def mine(part):
            done, back = ((done_v, back_v), (done_s, back_s))[part]
            return pltpu.make_async_copy(done.at[ix, top], back.at[ix], back_rs.at[part])

        for copy in tables:
            copy.wait()
        bulk_wait(0)
        merges(0)

        def fill(k, carry):
            region = grid[FIRST - 1, k, tall]
            picks = [zero] * 3
            for r in range(lame_t.shape[0]):
                hit = region == float(r)
                for q, table in enumerate((lame_t, shear_t, buoy_t)):
                    picks[q] = jnp.where(hit, table[r], picks[q])
            for q in range(3):
                coef[q, k] = within * picks[q]
            return carry

        for k in range(total):
            fill(k, 0)

        def store(c, k, rate):
            early[c, k] = rate

        rates(store)
        bulk_wait(1)
        merges(1)
        push_wait(0)
        for c in range(3):
            for k in range(total):
                kick(0, c, k, early[c, k])
        strain()
        push_wait(1)

        def middle(t, carry):
            rates(functools.partial(kick, t))
            strain()
            return carry

        lax.fori_loop(1, STEPS - 1, middle, 0)
        rates(functools.partial(kick, STEPS - 1))
        finish(0)
        mine(0).start()
        strain()
        finish(1)
        mine(1).start()

        for part in range(2):
            for to in peers:
                bulk(to, top, part).wait_send()
        for d in range(ny):
            for j in range(nx):
                pl.when((ix != j) | (iy != d))(send(d, j, 1).wait_send)
        edges_do(top, "wait_send")
        for part in range(2):
            for to in peers:
                for zt in range(2):
                    result(to, zt, part).wait_send()
            result(ix, 0, part).wait_send()
        results_wait()


def weave(back_v, back_s, vout_ref, sout_ref, vbuf, sbuf, sems):
    nx, _, half, lanes = back_v.shape
    slab = lanes // nx
    cx = vbuf.shape[1]
    offset = (0, WIDE, slab, WIDE + slab)
    lane = lax.broadcasted_iota(jnp.int32, (half, lanes), 1)
    for k, (back, buf, out) in enumerate(((back_v, vbuf, vout_ref), (back_s, sbuf, sout_ref))):
        for f in range(back.shape[1]):
            came = [back[j, f] for j in range(nx)]
            for x in range(cx):
                whole = None
                for j in range(nx):
                    moved = pltpu.roll(came[j], (slab * j - HALO - offset[x]) % lanes, 1)
                    whole = moved if whole is None else jnp.where(lane >= slab * j, moved, whole)
                buf[f, x] = whole
        pltpu.make_async_copy(buf, out, sems.at[k]).start()
    for k, (buf, out) in enumerate(((vbuf, vout_ref), (sbuf, sout_ref))):
        pltpu.make_async_copy(buf, out, sems.at[k]).wait()


def slabs(sizes, velocity, stress, region_map, lame_table, shear_table, buoy_table,
          block_pattern, block_wave, block_x, block_dest):
    nx, ny, nz = sizes
    cx, half, lanes = velocity.shape[1:]
    blocks = block_pattern.shape[0]
    pairs = cx // 2
    total = nx * pairs
    tile = (half, lanes)
    vmem = pl.BlockSpec(memory_space=pltpu.VMEM)
    hbm = pl.BlockSpec(memory_space=pl.ANY)
    tiles = STEPS * 3 * pairs // half
    f32, i32 = jnp.float32, jnp.int32
    dma = pltpu.SemaphoreType.DMA
    came = pl.pallas_call(
        functools.partial(slab_kernel, sizes),
        out_shape=(pltpu.VMEM((nx, 3) + tile, f32), pltpu.VMEM((nx, 6) + tile, f32)),
        in_specs=[hbm] * 10,
        out_specs=(vmem, vmem),
        scratch_shapes=[
            pltpu.VMEM((FIELDS, cx) + tile, f32),
            pltpu.VMEM(region_map.shape, i32),
            pltpu.VMEM((3, blocks, lanes), f32),
            pltpu.VMEM((STEPS, blocks), f32),
            pltpu.VMEM((1, blocks), i32),
            pltpu.VMEM((1, blocks), i32),
            pltpu.SMEM(lame_table.shape, f32),
            pltpu.SMEM(lame_table.shape, f32),
            pltpu.SMEM(lame_table.shape, f32),
            pltpu.VMEM((nx, FIELDS, pairs) + tile, f32),
            pltpu.VMEM((2, -(-FIELDS * pairs // BANDS)) + tile, f32),
            pltpu.VMEM((nx, 2, -(-FIELDS * pairs // BANDS)) + tile, f32),
            pltpu.VMEM((FIELDS, total, 4 * half, lanes), f32),
            pltpu.VMEM((3, total, 2 * half, lanes), f32),
            pltpu.VMEM((3, total, 2 * half, lanes), f32),
            pltpu.VMEM((2, 2 * lanes, lanes), jnp.bfloat16),
            pltpu.VMEM((ny, nx, tiles) + tile, f32),
            pltpu.VMEM((nx, ny, tiles) + tile, f32),
            pltpu.VMEM((nx, tiles * half, lanes), f32),
            pltpu.VMEM((nx, 2, 3) + tile, f32),
            pltpu.VMEM((nx, 2, 6) + tile, f32),
            dma((10,)),
            dma((nx, 2)),
            dma((2,)),
            dma((2,)),
            dma((1,)),
            dma((ny, nx, 2)),
            dma((2,)),
            dma((nx, 2, 2)),
            dma((2,)),
            pltpu.SemaphoreType.REGULAR,
            pltpu.SemaphoreType.REGULAR,
        ],
        compiler_params=pltpu.CompilerParams(collective_id=0, has_side_effects=True),
        name="slabs",
    )(
        velocity,
        stress,
        region_map,
        lame_table,
        shear_table,
        buoy_table,
        block_pattern.transpose(1, 0, 2),
        block_wave.T,
        block_x.reshape(1, blocks),
        block_dest.reshape(1, blocks),
    )
    return pl.pallas_call(
        weave,
        out_shape=(jax.ShapeDtypeStruct(velocity.shape, f32), jax.ShapeDtypeStruct(stress.shape, f32)),
        in_specs=[vmem, vmem],
        out_specs=(hbm, hbm),
        scratch_shapes=[pltpu.VMEM(velocity.shape, f32), pltpu.VMEM(stress.shape, f32), dma((2,))],
        name="weave",
    )(*(pltpu.with_memory_space_constraint(c, pltpu.VMEM) for c in came))


def local(sizes, velocity, *rest):
    nx, ny, nz = sizes
    cx, half, lanes = velocity.shape[1:]
    fits = nz == 2 and cx == 4 and half == 8 and lanes == 128 and lanes // nx + 2 * HALO == WIDE
    return (slabs if fits else shards)(sizes, velocity, *rest)


def solution(mesh):
    sizes = tuple(mesh.shape[a] for a in ("gx", "gy", "gz"))
    field = P(None, "gx", "gz", "gy")
    both = ("gx", "gy")
    placed = (
        field,
        field,
        P("gx", "gz", "gy"),
        P(),
        P(),
        P(),
        P(both, None, None),
        P(both, None),
        P(both),
        P(both, None),
    )
    return jax.shard_map(
        functools.partial(local, sizes),
        mesh=mesh,
        in_specs=placed,
        out_specs=(field, field),
        check_vma=False,
    )
```

```python
import functools
import jax
import jax.numpy as jnp
from jax import lax
from jax.experimental import pallas as pl
from jax.experimental.pallas import tpu as pltpu
from jax.sharding import PartitionSpec as P

STEPS = 4
ROUNDS = 2 * STEPS

NEAR = 9.0 / 8.0
FAR = 1.0 / 24.0
DT = 0.13
MESH = pl.DeviceIdType.MESH


def masks(shape, axis):
    n = shape[axis]
    at = lax.broadcasted_iota(jnp.int32, shape, axis)

    def split(test, value):
        inside = jnp.where(test, 0.0, value).astype(jnp.float32)
        across = jnp.where(test, value, 0.0).astype(jnp.float32)
        return inside, across

    fwd = (
        (n - 1, split(at == n - 1, NEAR)),
        (n - 2, split(at >= n - 2, -FAR)),
        (1, split(at == 0, FAR)),
    )
    bwd = (
        (1, split(at == 0, -NEAR)),
        (2, split(at < 2, FAR)),
        (n - 1, split(at == n - 1, -FAR)),
    )
    return {"f": (fwd, -NEAR), "b": (bwd, NEAR)}


def in_tile(f, way, coefs, axis):
    terms, own = coefs[way]
    inside = own * f
    across = None
    for turn, (here, there) in terms:
        rolled = pltpu.roll(f, turn, axis)
        inside = inside + here[None] * rolled
        add = there[None] * rolled
        across = add if across is None else across + add
    return inside, across


def kernel(
    sizes,
    vel_ref,
    str_ref,
    reg_ref,
    lame_ref,
    shear_ref,
    buoy_ref,
    pat_ref,
    wave_ref,
    bx_ref,
    dest_ref,
    vout_ref,
    sout_ref,
    part,
    got,
    sxr,
    sxl,
    hxl,
    hxr,
    sy,
    hy,
    vin,
    sin,
    rin,
    vo,
    so,
    ssem,
    rsem,
    fs,
    fr,
    ls,
    lr,
    ld,
):
    nx, ny, nz = sizes
    ix, iy, iz = lax.axis_index("gx"), lax.axis_index("gy"), lax.axis_index("gz")
    cx, half = vel_ref.shape[1:3]
    tile = (2 * half, vel_ref.shape[3])
    lead = iz == nz - 1
    low, high = pl.ds(0, half), pl.ds(half, half)
    has_l, has_r = lead & (ix > 0), lead & (ix < nx - 1)
    has_d, has_u = lead & (iy > 0), lead & (iy < ny - 1)

    barrier = pltpu.get_barrier_semaphore()

    def greet(cond, where):
        @pl.when(cond)
        def _():
            pl.semaphore_signal(barrier, inc=1, device_id=where, device_id_type=MESH)

        return cond.astype(jnp.int32)

    count = greet(has_l, {"gx": ix - 1}) + greet(has_r, {"gx": ix + 1}) + 1
    pl.semaphore_signal(barrier, inc=1, device_id={"gz": 1 - iz}, device_id_type=MESH)
    for d in range(ny):
        count = count + greet(lead & (iy != d), {"gy": d})

    def hand(src, dst, k):
        return pltpu.make_async_remote_copy(
            src_ref=src,
            dst_ref=dst,
            send_sem=ls.at[k],
            recv_sem=lr.at[k],
            device_id={"gz": 1 - iz},
            device_id_type=MESH,
        )

    given = (
        hand(str_ref, sin.at[:, :, low], 0),
        hand(vel_ref, vin.at[:, :, low], 1),
        hand(reg_ref, rin.at[:, low], 2),
    )
    back = (hand(vo, vout_ref, 3), hand(so, sout_ref, 4))

    @pl.when(jnp.logical_not(lead))
    def _():
        pl.semaphore_wait(barrier, count)
        for copy in given:
            copy.start()
        for copy in given:
            copy.wait_send()
        for copy in back:
            copy.wait_recv()

    @pl.when(lead)
    def _():
        own = (
            pltpu.make_async_copy(str_ref, sin.at[:, :, high], ld.at[0]),
            pltpu.make_async_copy(vel_ref, vin.at[:, :, high], ld.at[1]),
            pltpu.make_async_copy(reg_ref, rin.at[:, high], ld.at[2]),
        )
        for copy in own:
            copy.start()
        @pl.when(jnp.logical_not(has_l))
        def _():
            hxl[...] = jnp.zeros_like(hxl)

        @pl.when(jnp.logical_not(has_r))
        def _():
            hxr[...] = jnp.zeros_like(hxr)

        @pl.when(jnp.logical_not(has_d))
        def _():
            hy[:, 0] = jnp.zeros_like(hy[:, 0])

        @pl.when(jnp.logical_not(has_u))
        def _():
            hy[:, 1] = jnp.zeros_like(hy[:, 1])

        rows = STEPS * cx

        if True:
            blocks = pat_ref.shape[1]
            row = lax.broadcasted_iota(jnp.int32, (ny * rows, blocks), 0)
            moment = (row // cx) % STEPS
            spot = (row // rows) * cx + row % cx
            key = dest_ref[...] * cx + bx_ref[...]
            amount = jnp.zeros((ny * rows, blocks), jnp.float32)
            for t in range(STEPS):
                amount = jnp.where(moment == t, wave_ref[t : t + 1, :], amount)
            weights = jnp.where(spot == key, amount, 0.0)
            for c in range(3):
                sums = jnp.dot(
                    weights,
                    pat_ref[c],
                    precision=lax.Precision.HIGHEST,
                    preferred_element_type=jnp.float32,
                )
                for d in range(ny):
                    part[d, c] = sums[d * rows : (d + 1) * rows]
            got[iy] = part[iy]

        lane = masks(tile, 1)
        sub = masks(tile, 0)
        at_lane = lax.broadcasted_iota(jnp.int32, tile, 1)
        at_sub = lax.broadcasted_iota(jnp.int32, tile, 0)
        n_lane = tile[1]
        edge_lane = (at_lane < 2) | (at_lane >= n_lane - 2)
        from_low = at_lane % 4 < 2

        def rdma(src, dst, r, k, where):
            return pltpu.make_async_remote_copy(
                src_ref=src,
                dst_ref=dst,
                send_sem=ssem.at[r, k],
                recv_sem=rsem.at[r, k],
                device_id=where,
                device_id_type=MESH,
            )

        def copies(r):
            to_r, to_l = (5, 4) if r % 2 == 0 else (4, 5)
            return (
                (has_r, has_l, rdma(sxr.at[r, pl.ds(0, to_r)], hxl.at[r, pl.ds(0, to_r)], r, 0, {"gx": ix + 1})),
                (has_l, has_r, rdma(sxl.at[r, pl.ds(0, to_l)], hxr.at[r, pl.ds(0, to_l)], r, 1, {"gx": ix - 1})),
                (has_u, has_d, rdma(sy.at[r], hy.at[r, 0], r, 2, {"gy": iy + 1})),
                (has_d, has_u, rdma(sy.at[r], hy.at[r, 1], r, 3, {"gy": iy - 1})),
            )

        def when(cond, act):
            if cond is None:
                act()
            else:
                pl.when(cond)(act)

        def derivatives(r, fx, fy, fz, first=None):
            to_r = [(f, w) for f, w in fx]
            moves = copies(r)
            k = 0
            for f, way in fx:
                for p in (cx - 1,) if way == "f" else (cx - 2, cx - 1):
                    sxr[r, k] = f[p]
                    k += 1
            k = 0
            for f, way in fx:
                for p in (0, 1) if way == "f" else (0,):
                    sxl[r, k] = f[p]
                    k += 1
            if first is not None:
                first()
            odd = ix % 2 == 1
            when(has_r & odd, moves[0][2].start)
            when(has_l, moves[1][2].start)
            when(has_r & jnp.logical_not(odd), moves[0][2].start)
            dy, packed, slot = [], None, 0
            for f, way in fy:
                inside, across = in_tile(f, way, lane, 2)
                dy.append(inside)
                for p in range(cx):
                    turned = across[p] if slot == 0 else pltpu.roll(across[p], 4 * slot, 1)
                    packed = turned if packed is None else packed + turned
                    slot += 1
            sy[r] = packed
            for m in moves[2:4]:
                when(m[0], m[2].start)
            dz = []
            for f, way in fz:
                dz.append(in_tile(f, way, sub, 1)[0])

            def finish():
                out_z = dz
                for m in moves[2:4]:
                    when(m[1], m[2].wait_recv)
                both = jnp.where(from_low, hy[r, 0], hy[r, 1])
                out_y = []
                for c in range(3):
                    planes = []
                    for p in range(cx):
                        slot = c * cx + p
                        turned = both if slot == 0 else pltpu.roll(both, n_lane - 4 * slot, 1)
                        planes.append(jnp.where(edge_lane, turned, 0.0))
                    out_y.append(dy[c] + jnp.stack(planes))
                for m in moves[:2]:
                    when(m[1], m[2].wait_recv)
                out_x, kl, kr = [], 0, 0
                for f, way in fx:
                    left = 1 if way == "f" else 2
                    right = 3 - left
                    pad = jnp.concatenate([hxl[r, kl : kl + left], f, hxr[r, kr : kr + right]], axis=0)
                    kl, kr = kl + left, kr + right
                    s = [pad[i : i + cx] for i in range(4)]
                    out_x.append(NEAR * (s[2] - s[1]) - FAR * (s[3] - s[0]))
                return out_x, out_y, out_z

            return finish

        def forces(act):
            for d in range(ny):
                @pl.when(iy != d)
                def _():
                    copy = pltpu.make_async_remote_copy(
                        src_ref=part.at[d],
                        dst_ref=got.at[iy if act == "start" else d],
                        send_sem=fs.at[d],
                        recv_sem=fr.at[iy if act == "start" else d],
                        device_id={"gy": d},
                        device_id_type=MESH,
                    )
                    getattr(copy, act)()

        def enter():
            pl.semaphore_wait(barrier, count)
            forces("start")

        own[0].wait()
        given[0].wait_recv()
        vel = None
        txx, tyy, tzz, txy, txz, tyz = [sin[c] for c in range(6)]
        surface = None
        for t in range(STEPS):
            finish = derivatives(
                2 * t,
                ((txx, "f"), (txy, "b"), (txz, "b")),
                ((txy, "b"), (tyy, "f"), (tyz, "b")),
                ((txz, "b"), (tyz, "b"), (tzz, "f")),
                enter if t == 0 else None,
            )
            if t == 0:
                for k in (1, 2):
                    own[k].wait()
                    given[k].wait_recv()
                vel = [vin[c] for c in range(3)]
                region = rin[...]
                lame = jnp.zeros(region.shape, jnp.float32)
                shear, buoy = lame, lame
                for k in range(lame_ref.shape[0]):
                    hit = region == k
                    lame = jnp.where(hit, lame_ref[k], lame)
                    shear = jnp.where(hit, shear_ref[k], shear)
                    buoy = jnp.where(hit, buoy_ref[k], buoy)
                lame, shear, buoy = DT * lame, DT * shear, DT * buoy
                forces("wait_recv")
                for c in range(3):
                    total = got[0, c]
                    for s in range(1, ny):
                        total = total + got[s, c]
                    got[0, c] = total
            dx, dy, dz = finish()
            for c in range(3):
                push = jnp.stack(
                    [
                        jnp.where(at_sub == 0, got[0, c, t * cx + p : t * cx + p + 1, :], 0.0)
                        for p in range(cx)
                    ]
                )
                vel[c] = vel[c] + buoy * (dx[c] + dy[c] + dz[c] + push)
            vx, vy, vz = vel
            if t == STEPS - 1:
                for c in range(3):
                    vo[c] = vel[c][:, :half]
            finish = derivatives(
                2 * t + 1,
                ((vx, "b"), (vy, "f"), (vz, "f")),
                ((vx, "f"), (vy, "b"), (vz, "f")),
                ((vx, "f"), (vy, "f"), (vz, "b")),
            )
            if t == STEPS - 1:
                back[0].start()
                for c in range(3):
                    vout_ref[c] = vel[c][:, half:]
            dx, dy, dz = finish()
            trace = lame * (dx[0] + dy[1] + dz[2])
            twice = 2.0 * shear
            txx = txx + (trace + twice * dx[0])
            tyy = tyy + (trace + twice * dy[1])
            tzz = tzz + (trace + twice * dz[2])
            txy = txy + shear * (dy[0] + dx[1])
            txz = txz + shear * (dz[0] + dx[2])
            tyz = tyz + shear * (dz[1] + dy[2])
        for c, f in enumerate((txx, tyy, tzz, txy, txz, tyz)):
            so[c] = f[:, :half]
            sout_ref[c] = f[:, half:]
        back[1].start()
        forces("wait_send")
        for r in range(ROUNDS):
            for m in copies(r):
                when(m[0], m[2].wait_send)
        for copy in back:
            copy.wait_send()


def shards(sizes, velocity, stress, region_map, lame_table, shear_table, buoy_table,
           block_pattern, block_wave, block_x, block_dest):
    cx = velocity.shape[1]
    tile = (2 * velocity.shape[2], velocity.shape[3])
    blocks = block_pattern.shape[0]
    ny = sizes[1]
    vmem = pl.BlockSpec(memory_space=pltpu.VMEM)
    smem = pl.BlockSpec(memory_space=pltpu.SMEM)
    hbm = pl.BlockSpec(memory_space=pl.ANY)
    f32 = jnp.float32
    held = pl.pallas_call(
        functools.partial(kernel, sizes),
        out_shape=(pltpu.VMEM(velocity.shape, f32), pltpu.VMEM(stress.shape, f32)),
        in_specs=[hbm, hbm, hbm, smem, smem, smem, vmem, vmem, vmem, vmem],
        out_specs=(vmem, vmem),
        scratch_shapes=[
            pltpu.VMEM((ny, 3, STEPS * cx, tile[1]), f32),
            pltpu.VMEM((ny, 3, STEPS * cx, tile[1]), f32),
            pltpu.VMEM((ROUNDS, 5) + tile, f32),
            pltpu.VMEM((ROUNDS, 5) + tile, f32),
            pltpu.VMEM((ROUNDS, 5) + tile, f32),
            pltpu.VMEM((ROUNDS, 5) + tile, f32),
            pltpu.VMEM((ROUNDS,) + tile, f32),
            pltpu.VMEM((ROUNDS, 2) + tile, f32),
            pltpu.VMEM((3, cx) + tile, f32),
            pltpu.VMEM((6, cx) + tile, f32),
            pltpu.VMEM((cx,) + tile, jnp.int32),
            pltpu.VMEM(velocity.shape, f32),
            pltpu.VMEM(stress.shape, f32),
            pltpu.SemaphoreType.DMA((ROUNDS, 4)),
            pltpu.SemaphoreType.DMA((ROUNDS, 4)),
            pltpu.SemaphoreType.DMA((ny,)),
            pltpu.SemaphoreType.DMA((ny,)),
            pltpu.SemaphoreType.DMA((5,)),
            pltpu.SemaphoreType.DMA((5,)),
            pltpu.SemaphoreType.DMA((3,)),
        ],
        compiler_params=pltpu.CompilerParams(collective_id=0, has_side_effects=True),
        name="waves",
    )(
        velocity,
        stress,
        region_map,
        lame_table,
        shear_table,
        buoy_table,
        block_pattern.transpose(1, 0, 2),
        block_wave.T,
        block_x.reshape(1, blocks),
        block_dest.reshape(1, blocks),
    )
    return held


HALO = 16
WIDE = 64
FIELDS = 10
FIRST = 7
BAND = 12
BANDS = WIDE // BAND


def slab_kernel(
    sizes,
    vel_ref,
    str_ref,
    reg_ref,
    lame_ref,
    shear_ref,
    buoy_ref,
    pat_ref,
    wave_ref,
    bx_ref,
    dest_ref,
    back_v,
    back_s,
    raw,
    raw_r,
    pat,
    wave,
    bx,
    dest,
    lame_t,
    shear_t,
    buoy_t,
    packed,
    strip,
    got_strip,
    grid,
    coef,
    early,
    taps,
    push_out,
    push_in,
    push,
    done_v,
    done_s,
    isem,
    bulk_ss,
    bulk_rs,
    strip_ss,
    strip_rs,
    push_ss,
    push_rs,
    back_ss,
    back_rs,
    go,
    far,
):
    nx, ny, nz = sizes
    ix, iy, iz = lax.axis_index("gx"), lax.axis_index("gy"), lax.axis_index("gz")
    cx, half, lanes = vel_ref.shape[1:]
    pairs = cx // 2
    total = nx * pairs
    last = nx - 1
    top = nz - 1
    lead = iz == top
    slab = lanes // nx
    has_d, has_u = iy > 0, iy < ny - 1
    tall = pl.ds(half, 2 * half)
    peers = (last - ix, lax.rem(ix + 2, nx), ix + 1 - 2 * lax.rem(ix, 2))
    groups = (pl.ds(0, FIRST), pl.ds(FIRST, FIELDS - FIRST))

    barrier = pltpu.get_barrier_semaphore()

    def signal(where):
        pl.semaphore_signal(barrier, inc=1, device_id=where, device_id_type=MESH)

    at = lax.broadcasted_iota(jnp.int32, (half, lanes), 1)
    at_lane = at
    at = at % WIDE
    spin = [(HALO - slab * j) % lanes for j in range(nx)]

    def remote(src, dst, ssem, rsem, where):
        return pltpu.make_async_remote_copy(
            src_ref=src, dst_ref=dst, send_sem=ssem, recv_sem=rsem, device_id=where, device_id_type=MESH
        )

    loads = (
        pltpu.make_async_copy(str_ref, raw.at[pl.ds(0, FIRST - 1)], isem.at[0]),
        pltpu.make_async_copy(vel_ref, raw.at[pl.ds(FIRST, 3)], isem.at[1]),
        pltpu.make_async_copy(reg_ref, raw_r, isem.at[2]),
    )
    tables = (
        pltpu.make_async_copy(lame_ref, lame_t, isem.at[3]),
        pltpu.make_async_copy(shear_ref, shear_t, isem.at[4]),
        pltpu.make_async_copy(buoy_ref, buoy_t, isem.at[5]),
    )
    blocks_in = (
        pltpu.make_async_copy(pat_ref, pat, isem.at[6]),
        pltpu.make_async_copy(wave_ref, wave, isem.at[7]),
        pltpu.make_async_copy(bx_ref, bx, isem.at[8]),
        pltpu.make_async_copy(dest_ref, dest, isem.at[9]),
    )

    def blends(even, odd):
        odd = pltpu.roll(odd, WIDE, 1)
        out = []
        for r in spin:
            begin = (lanes - r) % lanes
            inside = at_lane >= begin
            if begin + WIDE <= lanes:
                inside = inside & (at_lane < begin + WIDE)
            else:
                inside = inside | (at_lane < begin + WIDE - lanes)
            out.append(jnp.where(inside, even, odd))
        return out

    def windows(even, odd):
        return [pltpu.roll(both, r, 1) for both, r in zip(blends(even, odd), spin, strict=True)]

    def pack():
        for copy in loads:
            copy.wait()
        edges = [None, None]
        for f in range(FIELDS):
            for p in range(pairs):
                i = f * pairs + p
                g = i % BANDS
                pair = [raw_r[2 * p + q].astype(jnp.float32) if f == FIRST - 1 else raw[f, 2 * p + q] for q in range(2)]
                mixed = blends(*pair)
                for j in range(nx):
                    both = pltpu.roll(mixed[j], spin[j], 1)
                    if j in (0, last):
                        way = 0 if j == 0 else 1
                        origin = HALO - BAND if j == 0 else WIDE - HALO
                        moved = pltpu.roll(mixed[j], (spin[j] + BAND * g - origin) % lanes, 1)
                        edges[way] = moved if g == 0 else jnp.where(at >= BAND * g, moved, edges[way])
                        if g == BANDS - 1:
                            strip[way, i // BANDS] = edges[way]
                        both = jnp.where(at < HALO if j == 0 else at >= WIDE - HALO, 0.0, both)
                    packed[j, f, p] = both

    def place(j, zt, part):
        return grid.at[groups[part], pl.ds(pairs * j, pairs), pl.ds(half * (zt + 1), half)]

    def bulk(to, zt, part):
        return remote(
            packed.at[to, groups[part]],
            place(ix, zt, part),
            bulk_ss.at[to, part],
            bulk_rs.at[part],
            {"gx": to, "gz": top},
        )

    def arrived(ref, sem):
        remote(ref, ref, sem, sem, {"gz": 0}).wait_recv()

    def edge(way, zt):
        where = {"gx": 0, "gy": iy + 1, "gz": top} if way == 0 else {"gx": last, "gy": iy - 1, "gz": top}
        return remote(strip.at[way], got_strip.at[ix, zt], strip_ss.at[way], strip_rs.at[0], where)

    def edges_do(zt, act):
        @pl.when(has_u)
        def _():
            getattr(edge(0, zt), act)()

        @pl.when(has_d)
        def _():
            getattr(edge(1, zt), act)()

    def result(to, zt, part):
        done, back = ((done_v, back_v), (done_s, back_s))[part]
        return remote(
            done.at[to, zt], back.at[ix], back_ss.at[to, zt, part], back_rs.at[part], {"gx": to, "gz": zt}
        )

    def results_wait():
        arrived(back_v, back_rs.at[0])
        arrived(back_s, back_rs.at[1])

    def keep(part):
        return pltpu.make_async_copy(packed.at[ix, groups[part]], place(ix, top, part), bulk_rs.at[part])

    def send(d, j, part):
        src, dst = push_out.at[d, j, spans[part]], push_in.at[ix, iy, spans[part]]
        return remote(src, dst, push_ss.at[d, j, part], push_rs.at[part], {"gx": j, "gy": d, "gz": top})

    def force_maker():
        for copy in blocks_in:
            copy.wait()
        blocks = pat.shape[1]
        size = 2 * half
        row = lax.broadcasted_iota(jnp.int32, (ny * size, blocks), 0)
        spot = (row // size) * cx + (row % pairs) * 2 + (row // half) % 2
        hit = spot == dest[...] * cx + bx[...]

        def forces(m):
            entry = half * m + row % half
            moment, kind = entry // (3 * pairs), (entry // pairs) % 3
            amount = jnp.zeros(row.shape, jnp.float32)
            for t in range(STEPS):
                amount = jnp.where(hit & (moment == t), wave[t : t + 1, :], amount)
            sums = None
            for c in range(3):
                term = jnp.dot(
                    jnp.where(kind == c, amount, 0.0),
                    pat[c],
                    precision=lax.Precision.HIGHEST,
                    preferred_element_type=jnp.float32,
                )
                sums = term if sums is None else sums + term
            views = [
                windows(sums[d * size : d * size + half], sums[d * size + half : (d + 1) * size])
                for d in range(ny)
            ]
            for d in range(ny):
                for j in range(nx):
                    both = views[d][j]
                    if j == 0:
                        both = jnp.where(at < HALO, views[d - 1][j] if d > 0 else 0.0, both)
                    if j == last:
                        both = jnp.where(at >= WIDE - HALO, views[d + 1][j] if d < ny - 1 else 0.0, both)
                    push_out[d, j, m] = both

        return forces

    tiles = push_in.shape[2]
    spans = (pl.ds(0, 1), pl.ds(1, tiles - 1))
    rest = pltpu.make_async_copy(push_out.at[iy, ix, spans[1]], push_in.at[ix, iy, spans[1]], push_rs.at[1])

    @pl.when(lead)
    def _():
        for to in peers:
            signal({"gx": to})

        @pl.when((ix == 0) & has_d)
        def _():
            for j in range(nx):
                signal({"gx": j, "gy": iy - 1})

        @pl.when((ix == last) & has_u)
        def _():
            for j in range(nx):
                signal({"gx": j, "gy": iy + 1})

        for copy in loads + tables + blocks_in:
            copy.start()
        for d in range(ny):
            for j in range(nx):
                signal({"gx": j, "gy": d, "gz": 0})
        blank = jnp.zeros((FIELDS, total, half, lanes), jnp.float32)
        grid[:, :, pl.ds(0, half)] = blank
        grid[:, :, pl.ds(3 * half, half)] = blank
        pack()
        source = lax.broadcasted_iota(jnp.int32, (lanes, lanes), 0)
        target = lax.broadcasted_iota(jnp.int32, (lanes, lanes), 1)
        for way in range(2):
            off = source - target + way
            tap = jnp.where(off == 1, NEAR / FAR, 0.0) + jnp.where(off == 0, -NEAR / FAR, 0.0)
            tap = tap + jnp.where(off == -1, 1.0, 0.0) + jnp.where(off == 2, -1.0, 0.0)
            tap = jnp.where(source // WIDE == target // WIDE, tap, 0.0).astype(jnp.bfloat16)
            taps[way, pl.ds(0, lanes)] = tap
            taps[way, pl.ds(lanes, lanes)] = tap
        pl.semaphore_wait(barrier, nx + has_d.astype(jnp.int32) + has_u.astype(jnp.int32))
        pl.semaphore_signal(go, inc=1, device_id={"gz": 0}, device_id_type=MESH)
        edges_do(top, "start")
        for part in range(2):
            for to in peers:
                bulk(to, top, part).start()
            keep(part).start()
        forces = force_maker()
        lax.fori_loop(1, tiles, lambda m, carry: (forces(m), carry)[1], 0)
        pl.semaphore_wait(far, 1)
        for d in range(ny):
            for j in range(nx):
                pl.when((ix != j) | (iy != d))(send(d, j, 1).start)
        rest.start()

    @pl.when(jnp.logical_not(lead))
    def _():
        signal({"gz": top})
        for copy in loads + blocks_in:
            copy.start()
        pack()
        pl.semaphore_wait(go, 1)
        edges_do(0, "start")
        for to in peers:
            bulk(to, 0, 0).start()
        bulk(ix, 0, 0).start()
        for to in peers:
            bulk(to, 0, 1).start()
        bulk(ix, 0, 1).start()
        forces = force_maker()
        forces(0)
        for j in range(nx):
            remote(
                push_out.at[iy, j, pl.ds(0, 1)],
                push_in.at[ix, iy, pl.ds(0, 1)],
                push_ss.at[iy, j, 0],
                push_rs.at[0],
                {"gx": j, "gz": top},
            ).start()
        pl.semaphore_wait(barrier, nx * ny)
        pl.semaphore_signal(far, inc=1, device_id={"gz": top}, device_id_type=MESH)
        for d in range(ny):
            for j in range(nx):
                pl.when(iy != d)(send(d, j, 0).start)
        for d in range(ny):
            for j in range(nx):
                send(d, j, 0).wait_send()
        for part in range(2):
            for j in range(nx):
                bulk(j, 0, part).wait_send()
        edges_do(0, "wait_send")
        results_wait()

    @pl.when(lead)
    def _():
        shape = (2 * half, lanes)
        lane = lax.broadcasted_iota(jnp.int32, shape, 1)
        left = lane < WIDE
        lane = lane % WIDE
        first = lax.broadcasted_iota(jnp.int32, shape, 0) == 0
        beyond = ((lane < HALO) & (ix == 0) & (iy == 0)) | (
            (lane >= WIDE - HALO) & (ix == last) & (iy == ny - 1)
        )
        within = jnp.where(beyond, 0.0, DT * FAR).astype(jnp.float32)
        ratio = NEAR / FAR
        zero = jnp.zeros(shape, jnp.float32)

        def bulk_wait(part):
            arrived(grid.at[groups[part], :, tall], bulk_rs.at[part])

        def merges(part):
            at_low = (ix == 0) & has_d
            at_high = (ix == last) & has_u

            @pl.when(at_low | at_high)
            def _():
                if part == 0:
                    arrived(got_strip, strip_rs.at[0])
                origin = jnp.where(ix == 0, HALO - BAND, WIDE - HALO)
                bound = jnp.where(ix == 0, HALO, WIDE - HALO)
                inside = (at >= bound) == (ix == 0)

                def body(j, carry):
                    for zt in range(2):
                        for f in range(*((0, FIRST), (FIRST, FIELDS))[part]):
                            for p in range(pairs):
                                i = f * pairs + p
                                shift = lax.rem(origin + lanes - BAND * (i % BANDS), lanes)
                                moved = pltpu.roll(got_strip[j, zt, i // BANDS], shift, 1)
                                here = (f, pairs * j + p, pl.ds(half * (zt + 1), half))
                                grid[here] = jnp.where(inside, grid[here], moved)
                    return carry

                lax.fori_loop(0, nx, body, 0)

        def push_wait(part):
            arrived(push_in.at[:, :, spans[part]], push_rs.at[part])
            for m in (0,) if part == 0 else range(1, tiles):
                for j in range(nx):
                    amount = push_in[j, 0, m]
                    for i in range(1, ny):
                        amount = amount + push_in[j, i, m]
                    push[j, half * m : half * (m + 1)] = (1.0 / FAR) * amount

        def rows(f, k, s):
            return grid[f, k, pl.ds(half + s, 2 * half)]

        def turned(memo, f, k):
            if k < 0 or k >= total:
                return zero
            if (f, k) not in memo:
                memo[f, k] = pltpu.roll(grid[f, k, tall], WIDE, 1)
            return memo[f, k]

        def step(memo, f, k):
            if (f, k, "s") not in memo:
                memo[f, k, "s"] = jnp.where(left, turned(memo, f, k - 1), turned(memo, f, k))
            return memo[f, k, "s"]

        def along_x(memo, f, way, k):
            v, near, far = grid[f, k, tall], step(memo, f, k), step(memo, f, k + 1)
            if way == "f":
                after = grid[f, k + 1, tall] if k + 1 < total else zero
                return ratio * (far - v) - (after - near)
            before = grid[f, k - 1, tall] if k > 0 else zero
            return ratio * (v - near) - (far - before)

        def along_y(f, way):
            v = grid[f, :, tall].reshape(total * 2 * half, lanes)
            coarse = v.astype(jnp.bfloat16)
            fine = (v - coarse.astype(jnp.float32)).astype(jnp.bfloat16)
            out = jnp.dot(
                jnp.concatenate([coarse, fine], axis=1),
                taps[0 if way == "f" else 1],
                preferred_element_type=jnp.float32,
            )
            return [out[2 * half * k : 2 * half * (k + 1)] for k in range(total)]

        def along_z(f, way, k):
            o = 0 if way == "b" else 1
            return ratio * (rows(f, k, o) - rows(f, k, o - 1)) - (rows(f, k, o + 1) - rows(f, k, o - 2))

        txx, tyy, tzz, txy, txz, tyz = range(6)
        vx, vy, vz = range(FIRST, FIRST + 3)

        def rates(use):
            memo = {}
            dy = along_y(txy, "b"), along_y(tyy, "f"), along_y(tyz, "b")
            for k in range(total):
                for c, (fx, wx, fz, wz) in enumerate(
                    ((txx, "f", txz, "b"), (txy, "b", tyz, "b"), (txz, "b", tzz, "f"))
                ):
                    use(c, k, along_x(memo, fx, wx, k) + along_z(fz, wz, k) + dy[c][k])

        def kick(t, c, k, rate):
            now = push[k // pairs, pl.ds((t * 3 + c) * pairs + k % pairs, 1), :]
            grid[vx + c, k, tall] = grid[vx + c, k, tall] + coef[2, k] * (rate + jnp.where(first, now, 0.0))

        def strain():
            memo = {}
            dy = along_y(vx, "f"), along_y(vy, "b"), along_y(vz, "f")
            for k in range(total):
                exx, eyy, ezz = along_x(memo, vx, "b", k), dy[1][k], along_z(vz, "b", k)
                shear = coef[1, k]
                twice = 2.0 * shear
                trace = coef[0, k] * (exx + eyy + ezz)
                grid[txx, k, tall] = grid[txx, k, tall] + (trace + twice * exx)
                grid[tyy, k, tall] = grid[tyy, k, tall] + (trace + twice * eyy)
                grid[tzz, k, tall] = grid[tzz, k, tall] + (trace + twice * ezz)
                grid[txy, k, tall] = grid[txy, k, tall] + shear * (dy[0][k] + along_x(memo, vy, "f", k))
                grid[txz, k, tall] = grid[txz, k, tall] + shear * (along_z(vx, "f", k) + along_x(memo, vz, "f", k))
                grid[tyz, k, tall] = grid[tyz, k, tall] + shear * (along_z(vy, "f", k) + dy[2][k])

        own_lanes = (at >= HALO) & (at < HALO + slab)

        def finish(part):
            done, start, count = ((done_v, FIRST, 3), (done_s, 0, 6))[part]
            def body(j, carry):
                for zt in range(2):
                    for f in range(count):
                        here = pl.ds(half * (zt + 1), half)
                        a, b = grid[start + f, pairs * j, here], grid[start + f, pairs * j + 1, here]
                        done[j, zt, f] = jnp.where(own_lanes, a, pltpu.roll(b, slab, 1))
                return carry

            for j in range(nx):
                body(j, 0)
            for to in peers:
                for zt in range(2):
                    result(to, zt, part).start()
            result(ix, 0, part).start()

        def mine(part):
            done, back = ((done_v, back_v), (done_s, back_s))[part]
            return pltpu.make_async_copy(done.at[ix, top], back.at[ix], back_rs.at[part])

        for copy in tables:
            copy.wait()
        bulk_wait(0)
        merges(0)

        def fill(k, carry):
            region = grid[FIRST - 1, k, tall]
            picks = [zero] * 3
            for r in range(lame_t.shape[0]):
                hit = region == float(r)
                for q, table in enumerate((lame_t, shear_t, buoy_t)):
                    picks[q] = jnp.where(hit, table[r], picks[q])
            for q in range(3):
                coef[q, k] = within * picks[q]
            return carry

        for k in range(total):
            fill(k, 0)

        def store(c, k, rate):
            early[c, k] = rate

        rates(store)
        bulk_wait(1)
        merges(1)
        push_wait(0)
        for c in range(3):
            for k in range(total):
                kick(0, c, k, early[c, k])
        strain()
        push_wait(1)

        def middle(t, carry):
            rates(functools.partial(kick, t))
            strain()
            return carry

        lax.fori_loop(1, STEPS - 1, middle, 0)
        rates(functools.partial(kick, STEPS - 1))
        finish(0)
        mine(0).start()
        strain()
        finish(1)
        mine(1).start()

        for part in range(2):
            for to in peers:
                bulk(to, top, part).wait_send()
        for d in range(ny):
            for j in range(nx):
                pl.when((ix != j) | (iy != d))(send(d, j, 1).wait_send)
        edges_do(top, "wait_send")
        for part in range(2):
            for to in peers:
                for zt in range(2):
                    result(to, zt, part).wait_send()
            result(ix, 0, part).wait_send()
        results_wait()


def weave(back_v, back_s, vout_ref, sout_ref, vbuf, sbuf, sems):
    nx, _, half, lanes = back_v.shape
    slab = lanes // nx
    cx = vbuf.shape[1]
    offset = (0, WIDE, slab, WIDE + slab)
    lane = lax.broadcasted_iota(jnp.int32, (half, lanes), 1)
    for k, (back, buf, out) in enumerate(((back_v, vbuf, vout_ref), (back_s, sbuf, sout_ref))):
        for f in range(back.shape[1]):
            came = [back[j, f] for j in range(nx)]
            for x in range(cx):
                whole = None
                for j in range(nx):
                    moved = pltpu.roll(came[j], (slab * j - HALO - offset[x]) % lanes, 1)
                    whole = moved if whole is None else jnp.where(lane >= slab * j, moved, whole)
                buf[f, x] = whole
        pltpu.make_async_copy(buf, out, sems.at[k]).start()
    for k, (buf, out) in enumerate(((vbuf, vout_ref), (sbuf, sout_ref))):
        pltpu.make_async_copy(buf, out, sems.at[k]).wait()


def slabs(sizes, velocity, stress, region_map, lame_table, shear_table, buoy_table,
          block_pattern, block_wave, block_x, block_dest):
    nx, ny, nz = sizes
    cx, half, lanes = velocity.shape[1:]
    blocks = block_pattern.shape[0]
    pairs = cx // 2
    total = nx * pairs
    tile = (half, lanes)
    vmem = pl.BlockSpec(memory_space=pltpu.VMEM)
    hbm = pl.BlockSpec(memory_space=pl.ANY)
    tiles = STEPS * 3 * pairs // half
    f32, i32 = jnp.float32, jnp.int32
    dma = pltpu.SemaphoreType.DMA
    came = pl.pallas_call(
        functools.partial(slab_kernel, sizes),
        out_shape=(pltpu.VMEM((nx, 3) + tile, f32), pltpu.VMEM((nx, 6) + tile, f32)),
        in_specs=[hbm] * 10,
        out_specs=(vmem, vmem),
        scratch_shapes=[
            pltpu.VMEM((FIELDS, cx) + tile, f32),
            pltpu.VMEM(region_map.shape, i32),
            pltpu.VMEM((3, blocks, lanes), f32),
            pltpu.VMEM((STEPS, blocks), f32),
            pltpu.VMEM((1, blocks), i32),
            pltpu.VMEM((1, blocks), i32),
            pltpu.SMEM(lame_table.shape, f32),
            pltpu.SMEM(lame_table.shape, f32),
            pltpu.SMEM(lame_table.shape, f32),
            pltpu.VMEM((nx, FIELDS, pairs) + tile, f32),
            pltpu.VMEM((2, -(-FIELDS * pairs // BANDS)) + tile, f32),
            pltpu.VMEM((nx, 2, -(-FIELDS * pairs // BANDS)) + tile, f32),
            pltpu.VMEM((FIELDS, total, 4 * half, lanes), f32),
            pltpu.VMEM((3, total, 2 * half, lanes), f32),
            pltpu.VMEM((3, total, 2 * half, lanes), f32),
            pltpu.VMEM((2, 2 * lanes, lanes), jnp.bfloat16),
            pltpu.VMEM((ny, nx, tiles) + tile, f32),
            pltpu.VMEM((nx, ny, tiles) + tile, f32),
            pltpu.VMEM((nx, tiles * half, lanes), f32),
            pltpu.VMEM((nx, 2, 3) + tile, f32),
            pltpu.VMEM((nx, 2, 6) + tile, f32),
            dma((10,)),
            dma((nx, 2)),
            dma((2,)),
            dma((2,)),
            dma((1,)),
            dma((ny, nx, 2)),
            dma((2,)),
            dma((nx, 2, 2)),
            dma((2,)),
            pltpu.SemaphoreType.REGULAR,
            pltpu.SemaphoreType.REGULAR,
        ],
        compiler_params=pltpu.CompilerParams(collective_id=0, has_side_effects=True),
        name="slabs",
    )(
        velocity,
        stress,
        region_map,
        lame_table,
        shear_table,
        buoy_table,
        block_pattern.transpose(1, 0, 2),
        block_wave.T,
        block_x.reshape(1, blocks),
        block_dest.reshape(1, blocks),
    )
    return pl.pallas_call(
        weave,
        out_shape=(jax.ShapeDtypeStruct(velocity.shape, f32), jax.ShapeDtypeStruct(stress.shape, f32)),
        in_specs=[vmem, vmem],
        out_specs=(hbm, hbm),
        scratch_shapes=[pltpu.VMEM(velocity.shape, f32), pltpu.VMEM(stress.shape, f32), dma((2,))],
        name="weave",
    )(*(pltpu.with_memory_space_constraint(c, pltpu.VMEM) for c in came))


def local(sizes, velocity, *rest):
    nx, ny, nz = sizes
    cx, half, lanes = velocity.shape[1:]
    fits = nz == 2 and cx == 4 and half == 8 and lanes == 128 and lanes // nx + 2 * HALO == WIDE
    return (slabs if fits else shards)(sizes, velocity, *rest)


def solution(mesh):
    sizes = tuple(mesh.shape[a] for a in ("gx", "gy", "gz"))
    field = P(None, "gx", "gz", "gy")
    both = ("gx", "gy")
    placed = (
        field,
        field,
        P("gx", "gz", "gy"),
        P(),
        P(),
        P(),
        P(both, None, None),
        P(both, None),
        P(both),
        P(both, None),
    )
    return jax.shard_map(
        functools.partial(local, sizes),
        mesh=mesh,
        in_specs=placed,
        out_specs=(field, field),
        check_vma=False,
    )
```

```python
import functools
import jax
import jax.numpy as jnp
from jax import lax
from jax.experimental import pallas as pl
from jax.experimental.pallas import tpu as pltpu
from jax.sharding import PartitionSpec as P

STEPS = 4
ROUNDS = 2 * STEPS

NEAR = 9.0 / 8.0
FAR = 1.0 / 24.0
DT = 0.13
MESH = pl.DeviceIdType.MESH


def masks(shape, axis):
    n = shape[axis]
    at = lax.broadcasted_iota(jnp.int32, shape, axis)

    def split(test, value):
        inside = jnp.where(test, 0.0, value).astype(jnp.float32)
        across = jnp.where(test, value, 0.0).astype(jnp.float32)
        return inside, across

    fwd = (
        (n - 1, split(at == n - 1, NEAR)),
        (n - 2, split(at >= n - 2, -FAR)),
        (1, split(at == 0, FAR)),
    )
    bwd = (
        (1, split(at == 0, -NEAR)),
        (2, split(at < 2, FAR)),
        (n - 1, split(at == n - 1, -FAR)),
    )
    return {"f": (fwd, -NEAR), "b": (bwd, NEAR)}


def in_tile(f, way, coefs, axis):
    terms, own = coefs[way]
    inside = own * f
    across = None
    for turn, (here, there) in terms:
        rolled = pltpu.roll(f, turn, axis)
        inside = inside + here[None] * rolled
        add = there[None] * rolled
        across = add if across is None else across + add
    return inside, across


def kernel(
    sizes,
    vel_ref,
    str_ref,
    reg_ref,
    lame_ref,
    shear_ref,
    buoy_ref,
    pat_ref,
    wave_ref,
    bx_ref,
    dest_ref,
    vout_ref,
    sout_ref,
    part,
    got,
    sxr,
    sxl,
    hxl,
    hxr,
    sy,
    hy,
    vin,
    sin,
    rin,
    vo,
    so,
    ssem,
    rsem,
    fs,
    fr,
    ls,
    lr,
    ld,
):
    nx, ny, nz = sizes
    ix, iy, iz = lax.axis_index("gx"), lax.axis_index("gy"), lax.axis_index("gz")
    cx, half = vel_ref.shape[1:3]
    tile = (2 * half, vel_ref.shape[3])
    lead = iz == nz - 1
    low, high = pl.ds(0, half), pl.ds(half, half)
    has_l, has_r = lead & (ix > 0), lead & (ix < nx - 1)
    has_d, has_u = lead & (iy > 0), lead & (iy < ny - 1)

    barrier = pltpu.get_barrier_semaphore()

    def greet(cond, where):
        @pl.when(cond)
        def _():
            pl.semaphore_signal(barrier, inc=1, device_id=where, device_id_type=MESH)

        return cond.astype(jnp.int32)

    count = greet(has_l, {"gx": ix - 1}) + greet(has_r, {"gx": ix + 1}) + 1
    pl.semaphore_signal(barrier, inc=1, device_id={"gz": 1 - iz}, device_id_type=MESH)
    for d in range(ny):
        count = count + greet(lead & (iy != d), {"gy": d})

    def hand(src, dst, k):
        return pltpu.make_async_remote_copy(
            src_ref=src,
            dst_ref=dst,
            send_sem=ls.at[k],
            recv_sem=lr.at[k],
            device_id={"gz": 1 - iz},
            device_id_type=MESH,
        )

    given = (
        hand(str_ref, sin.at[:, :, low], 0),
        hand(vel_ref, vin.at[:, :, low], 1),
        hand(reg_ref, rin.at[:, low], 2),
    )
    back = (hand(vo, vout_ref, 3), hand(so, sout_ref, 4))

    @pl.when(jnp.logical_not(lead))
    def _():
        pl.semaphore_wait(barrier, count)
        for copy in given:
            copy.start()
        for copy in given:
            copy.wait_send()
        for copy in back:
            copy.wait_recv()

    @pl.when(lead)
    def _():
        own = (
            pltpu.make_async_copy(str_ref, sin.at[:, :, high], ld.at[0]),
            pltpu.make_async_copy(vel_ref, vin.at[:, :, high], ld.at[1]),
            pltpu.make_async_copy(reg_ref, rin.at[:, high], ld.at[2]),
        )
        for copy in own:
            copy.start()
        @pl.when(jnp.logical_not(has_l))
        def _():
            hxl[...] = jnp.zeros_like(hxl)

        @pl.when(jnp.logical_not(has_r))
        def _():
            hxr[...] = jnp.zeros_like(hxr)

        @pl.when(jnp.logical_not(has_d))
        def _():
            hy[:, 0] = jnp.zeros_like(hy[:, 0])

        @pl.when(jnp.logical_not(has_u))
        def _():
            hy[:, 1] = jnp.zeros_like(hy[:, 1])

        rows = STEPS * cx

        if True:
            blocks = pat_ref.shape[1]
            row = lax.broadcasted_iota(jnp.int32, (ny * rows, blocks), 0)
            moment = (row // cx) % STEPS
            spot = (row // rows) * cx + row % cx
            key = dest_ref[...] * cx + bx_ref[...]
            amount = jnp.zeros((ny * rows, blocks), jnp.float32)
            for t in range(STEPS):
                amount = jnp.where(moment == t, wave_ref[t : t + 1, :], amount)
            weights = jnp.where(spot == key, amount, 0.0)
            for c in range(3):
                sums = jnp.dot(
                    weights,
                    pat_ref[c],
                    precision=lax.Precision.HIGHEST,
                    preferred_element_type=jnp.float32,
                )
                for d in range(ny):
                    part[d, c] = sums[d * rows : (d + 1) * rows]
            got[iy] = part[iy]

        lane = masks(tile, 1)
        sub = masks(tile, 0)
        at_lane = lax.broadcasted_iota(jnp.int32, tile, 1)
        at_sub = lax.broadcasted_iota(jnp.int32, tile, 0)
        n_lane = tile[1]
        edge_lane = (at_lane < 2) | (at_lane >= n_lane - 2)
        from_low = at_lane % 4 < 2

        def rdma(src, dst, r, k, where):
            return pltpu.make_async_remote_copy(
                src_ref=src,
                dst_ref=dst,
                send_sem=ssem.at[r, k],
                recv_sem=rsem.at[r, k],
                device_id=where,
                device_id_type=MESH,
            )

        def copies(r):
            to_r, to_l = (5, 4) if r % 2 == 0 else (4, 5)
            return (
                (has_r, has_l, rdma(sxr.at[r, pl.ds(0, to_r)], hxl.at[r, pl.ds(0, to_r)], r, 0, {"gx": ix + 1})),
                (has_l, has_r, rdma(sxl.at[r, pl.ds(0, to_l)], hxr.at[r, pl.ds(0, to_l)], r, 1, {"gx": ix - 1})),
                (has_u, has_d, rdma(sy.at[r], hy.at[r, 0], r, 2, {"gy": iy + 1})),
                (has_d, has_u, rdma(sy.at[r], hy.at[r, 1], r, 3, {"gy": iy - 1})),
            )

        def when(cond, act):
            if cond is None:
                act()
            else:
                pl.when(cond)(act)

        def derivatives(r, fx, fy, fz, first=None):
            to_r = [(f, w) for f, w in fx]
            moves = copies(r)
            k = 0
            for f, way in fx:
                for p in (cx - 1,) if way == "f" else (cx - 2, cx - 1):
                    sxr[r, k] = f[p]
                    k += 1
            k = 0
            for f, way in fx:
                for p in (0, 1) if way == "f" else (0,):
                    sxl[r, k] = f[p]
                    k += 1
            if first is not None:
                first()
            odd = ix % 2 == 1
            when(has_r & odd, moves[0][2].start)
            when(has_l, moves[1][2].start)
            when(has_r & jnp.logical_not(odd), moves[0][2].start)
            dy, packed, slot = [], None, 0
            for f, way in fy:
                inside, across = in_tile(f, way, lane, 2)
                dy.append(inside)
                for p in range(cx):
                    turned = across[p] if slot == 0 else pltpu.roll(across[p], 4 * slot, 1)
                    packed = turned if packed is None else packed + turned
                    slot += 1
            sy[r] = packed
            for m in moves[2:4]:
                when(m[0], m[2].start)
            dz = []
            for f, way in fz:
                dz.append(in_tile(f, way, sub, 1)[0])

            def finish():
                out_z = dz
                for m in moves[2:4]:
                    when(m[1], m[2].wait_recv)
                both = jnp.where(from_low, hy[r, 0], hy[r, 1])
                out_y = []
                for c in range(3):
                    planes = []
                    for p in range(cx):
                        slot = c * cx + p
                        turned = both if slot == 0 else pltpu.roll(both, n_lane - 4 * slot, 1)
                        planes.append(jnp.where(edge_lane, turned, 0.0))
                    out_y.append(dy[c] + jnp.stack(planes))
                for m in moves[:2]:
                    when(m[1], m[2].wait_recv)
                out_x, kl, kr = [], 0, 0
                for f, way in fx:
                    left = 1 if way == "f" else 2
                    right = 3 - left
                    pad = jnp.concatenate([hxl[r, kl : kl + left], f, hxr[r, kr : kr + right]], axis=0)
                    kl, kr = kl + left, kr + right
                    s = [pad[i : i + cx] for i in range(4)]
                    out_x.append(NEAR * (s[2] - s[1]) - FAR * (s[3] - s[0]))
                return out_x, out_y, out_z

            return finish

        def forces(act):
            for d in range(ny):
                @pl.when(iy != d)
                def _():
                    copy = pltpu.make_async_remote_copy(
                        src_ref=part.at[d],
                        dst_ref=got.at[iy if act == "start" else d],
                        send_sem=fs.at[d],
                        recv_sem=fr.at[iy if act == "start" else d],
                        device_id={"gy": d},
                        device_id_type=MESH,
                    )
                    getattr(copy, act)()

        def enter():
            pl.semaphore_wait(barrier, count)
            forces("start")

        own[0].wait()
        given[0].wait_recv()
        vel = None
        txx, tyy, tzz, txy, txz, tyz = [sin[c] for c in range(6)]
        surface = None
        for t in range(STEPS):
            finish = derivatives(
                2 * t,
                ((txx, "f"), (txy, "b"), (txz, "b")),
                ((txy, "b"), (tyy, "f"), (tyz, "b")),
                ((txz, "b"), (tyz, "b"), (tzz, "f")),
                enter if t == 0 else None,
            )
            if t == 0:
                for k in (1, 2):
                    own[k].wait()
                    given[k].wait_recv()
                vel = [vin[c] for c in range(3)]
                region = rin[...]
                lame = jnp.zeros(region.shape, jnp.float32)
                shear, buoy = lame, lame
                for k in range(lame_ref.shape[0]):
                    hit = region == k
                    lame = jnp.where(hit, lame_ref[k], lame)
                    shear = jnp.where(hit, shear_ref[k], shear)
                    buoy = jnp.where(hit, buoy_ref[k], buoy)
                lame, shear, buoy = DT * lame, DT * shear, DT * buoy
                forces("wait_recv")
                for c in range(3):
                    total = got[0, c]
                    for s in range(1, ny):
                        total = total + got[s, c]
                    got[0, c] = total
            dx, dy, dz = finish()
            for c in range(3):
                push = jnp.stack(
                    [
                        jnp.where(at_sub == 0, got[0, c, t * cx + p : t * cx + p + 1, :], 0.0)
                        for p in range(cx)
                    ]
                )
                vel[c] = vel[c] + buoy * (dx[c] + dy[c] + dz[c] + push)
            vx, vy, vz = vel
            if t == STEPS - 1:
                for c in range(3):
                    vo[c] = vel[c][:, :half]
            finish = derivatives(
                2 * t + 1,
                ((vx, "b"), (vy, "f"), (vz, "f")),
                ((vx, "f"), (vy, "b"), (vz, "f")),
                ((vx, "f"), (vy, "f"), (vz, "b")),
            )
            if t == STEPS - 1:
                back[0].start()
                for c in range(3):
                    vout_ref[c] = vel[c][:, half:]
            dx, dy, dz = finish()
            trace = lame * (dx[0] + dy[1] + dz[2])
            twice = 2.0 * shear
            txx = txx + (trace + twice * dx[0])
            tyy = tyy + (trace + twice * dy[1])
            tzz = tzz + (trace + twice * dz[2])
            txy = txy + shear * (dy[0] + dx[1])
            txz = txz + shear * (dz[0] + dx[2])
            tyz = tyz + shear * (dz[1] + dy[2])
        for c, f in enumerate((txx, tyy, tzz, txy, txz, tyz)):
            so[c] = f[:, :half]
            sout_ref[c] = f[:, half:]
        back[1].start()
        forces("wait_send")
        for r in range(ROUNDS):
            for m in copies(r):
                when(m[0], m[2].wait_send)
        for copy in back:
            copy.wait_send()


def shards(sizes, velocity, stress, region_map, lame_table, shear_table, buoy_table,
           block_pattern, block_wave, block_x, block_dest):
    cx = velocity.shape[1]
    tile = (2 * velocity.shape[2], velocity.shape[3])
    blocks = block_pattern.shape[0]
    ny = sizes[1]
    vmem = pl.BlockSpec(memory_space=pltpu.VMEM)
    smem = pl.BlockSpec(memory_space=pltpu.SMEM)
    hbm = pl.BlockSpec(memory_space=pl.ANY)
    f32 = jnp.float32
    held = pl.pallas_call(
        functools.partial(kernel, sizes),
        out_shape=(pltpu.VMEM(velocity.shape, f32), pltpu.VMEM(stress.shape, f32)),
        in_specs=[hbm, hbm, hbm, smem, smem, smem, vmem, vmem, vmem, vmem],
        out_specs=(vmem, vmem),
        scratch_shapes=[
            pltpu.VMEM((ny, 3, STEPS * cx, tile[1]), f32),
            pltpu.VMEM((ny, 3, STEPS * cx, tile[1]), f32),
            pltpu.VMEM((ROUNDS, 5) + tile, f32),
            pltpu.VMEM((ROUNDS, 5) + tile, f32),
            pltpu.VMEM((ROUNDS, 5) + tile, f32),
            pltpu.VMEM((ROUNDS, 5) + tile, f32),
            pltpu.VMEM((ROUNDS,) + tile, f32),
            pltpu.VMEM((ROUNDS, 2) + tile, f32),
            pltpu.VMEM((3, cx) + tile, f32),
            pltpu.VMEM((6, cx) + tile, f32),
            pltpu.VMEM((cx,) + tile, jnp.int32),
            pltpu.VMEM(velocity.shape, f32),
            pltpu.VMEM(stress.shape, f32),
            pltpu.SemaphoreType.DMA((ROUNDS, 4)),
            pltpu.SemaphoreType.DMA((ROUNDS, 4)),
            pltpu.SemaphoreType.DMA((ny,)),
            pltpu.SemaphoreType.DMA((ny,)),
            pltpu.SemaphoreType.DMA((5,)),
            pltpu.SemaphoreType.DMA((5,)),
            pltpu.SemaphoreType.DMA((3,)),
        ],
        compiler_params=pltpu.CompilerParams(collective_id=0, has_side_effects=True),
        name="waves",
    )(
        velocity,
        stress,
        region_map,
        lame_table,
        shear_table,
        buoy_table,
        block_pattern.transpose(1, 0, 2),
        block_wave.T,
        block_x.reshape(1, blocks),
        block_dest.reshape(1, blocks),
    )
    return held


HALO = 16
WIDE = 64
FIELDS = 10
FIRST = 7
BAND = 12
BANDS = WIDE // BAND


def slab_kernel(
    sizes,
    vel_ref,
    str_ref,
    reg_ref,
    lame_ref,
    shear_ref,
    buoy_ref,
    pat_ref,
    wave_ref,
    bx_ref,
    dest_ref,
    back_v,
    back_s,
    raw,
    raw_r,
    pat,
    wave,
    bx,
    dest,
    lame_t,
    shear_t,
    buoy_t,
    packed,
    strip,
    got_strip,
    grid,
    coef,
    early,
    taps,
    push_out,
    push_in,
    push,
    done_v,
    done_s,
    isem,
    bulk_ss,
    bulk_rs,
    strip_ss,
    strip_rs,
    push_ss,
    push_rs,
    back_ss,
    back_rs,
    go,
    far,
):
    nx, ny, nz = sizes
    ix, iy, iz = lax.axis_index("gx"), lax.axis_index("gy"), lax.axis_index("gz")
    cx, half, lanes = vel_ref.shape[1:]
    pairs = cx // 2
    total = nx * pairs
    last = nx - 1
    top = nz - 1
    lead = iz == top
    slab = lanes // nx
    has_d, has_u = iy > 0, iy < ny - 1
    tall = pl.ds(half, 2 * half)
    peers = (last - ix, lax.rem(ix + 2, nx), ix + 1 - 2 * lax.rem(ix, 2))
    groups = (pl.ds(0, FIRST), pl.ds(FIRST, FIELDS - FIRST))

    barrier = pltpu.get_barrier_semaphore()

    def signal(where):
        pl.semaphore_signal(barrier, inc=1, device_id=where, device_id_type=MESH)

    at = lax.broadcasted_iota(jnp.int32, (half, lanes), 1)
    at_lane = at
    at = at % WIDE
    spin = [(HALO - slab * j) % lanes for j in range(nx)]

    def remote(src, dst, ssem, rsem, where):
        return pltpu.make_async_remote_copy(
            src_ref=src, dst_ref=dst, send_sem=ssem, recv_sem=rsem, device_id=where, device_id_type=MESH
        )

    loads = (
        pltpu.make_async_copy(str_ref, raw.at[pl.ds(0, FIRST - 1)], isem.at[0]),
        pltpu.make_async_copy(vel_ref, raw.at[pl.ds(FIRST, 3)], isem.at[1]),
        pltpu.make_async_copy(reg_ref, raw_r, isem.at[2]),
    )
    tables = (
        pltpu.make_async_copy(lame_ref, lame_t, isem.at[3]),
        pltpu.make_async_copy(shear_ref, shear_t, isem.at[4]),
        pltpu.make_async_copy(buoy_ref, buoy_t, isem.at[5]),
    )
    blocks_in = (
        pltpu.make_async_copy(pat_ref, pat, isem.at[6]),
        pltpu.make_async_copy(wave_ref, wave, isem.at[7]),
        pltpu.make_async_copy(bx_ref, bx, isem.at[8]),
        pltpu.make_async_copy(dest_ref, dest, isem.at[9]),
    )

    def blends(even, odd):
        odd = pltpu.roll(odd, WIDE, 1)
        out = []
        for r in spin:
            begin = (lanes - r) % lanes
            inside = at_lane >= begin
            if begin + WIDE <= lanes:
                inside = inside & (at_lane < begin + WIDE)
            else:
                inside = inside | (at_lane < begin + WIDE - lanes)
            out.append(jnp.where(inside, even, odd))
        return out

    def windows(even, odd):
        return [pltpu.roll(both, r, 1) for both, r in zip(blends(even, odd), spin, strict=True)]

    def pack():
        for copy in loads:
            copy.wait()
        edges = [None, None]
        for f in range(FIELDS):
            for p in range(pairs):
                i = f * pairs + p
                g = i % BANDS
                pair = [raw_r[2 * p + q].astype(jnp.float32) if f == FIRST - 1 else raw[f, 2 * p + q] for q in range(2)]
                mixed = blends(*pair)
                for j in range(nx):
                    both = pltpu.roll(mixed[j], spin[j], 1)
                    if j in (0, last):
                        way = 0 if j == 0 else 1
                        origin = HALO - BAND if j == 0 else WIDE - HALO
                        moved = pltpu.roll(mixed[j], (spin[j] + BAND * g - origin) % lanes, 1)
                        edges[way] = moved if g == 0 else jnp.where(at >= BAND * g, moved, edges[way])
                        if g == BANDS - 1:
                            strip[way, i // BANDS] = edges[way]
                        both = jnp.where(at < HALO if j == 0 else at >= WIDE - HALO, 0.0, both)
                    packed[j, f, p] = both

    def place(j, zt, part):
        return grid.at[groups[part], pl.ds(pairs * j, pairs), pl.ds(half * (zt + 1), half)]

    def bulk(to, zt, part):
        return remote(
            packed.at[to, groups[part]],
            place(ix, zt, part),
            bulk_ss.at[to, part],
            bulk_rs.at[part],
            {"gx": to, "gz": top},
        )

    def arrived(ref, sem):
        remote(ref, ref, sem, sem, {"gz": 0}).wait_recv()

    def edge(way, zt):
        where = {"gx": 0, "gy": iy + 1, "gz": top} if way == 0 else {"gx": last, "gy": iy - 1, "gz": top}
        return remote(strip.at[way], got_strip.at[ix, zt], strip_ss.at[way], strip_rs.at[0], where)

    def edges_do(zt, act):
        @pl.when(has_u)
        def _():
            getattr(edge(0, zt), act)()

        @pl.when(has_d)
        def _():
            getattr(edge(1, zt), act)()

    def result(to, zt, part):
        done, back = ((done_v, back_v), (done_s, back_s))[part]
        return remote(
            done.at[to, zt], back.at[ix], back_ss.at[to, zt, part], back_rs.at[part], {"gx": to, "gz": zt}
        )

    def results_wait():
        arrived(back_v, back_rs.at[0])
        arrived(back_s, back_rs.at[1])

    def keep(part):
        return pltpu.make_async_copy(packed.at[ix, groups[part]], place(ix, top, part), bulk_rs.at[part])

    def send(d, j, part):
        src, dst = push_out.at[d, j, spans[part]], push_in.at[ix, iy, spans[part]]
        return remote(src, dst, push_ss.at[d, j, part], push_rs.at[part], {"gx": j, "gy": d, "gz": top})

    def force_maker():
        for copy in blocks_in:
            copy.wait()
        blocks = pat.shape[1]
        size = 2 * half
        row = lax.broadcasted_iota(jnp.int32, (ny * size, blocks), 0)
        spot = (row // size) * cx + (row % pairs) * 2 + (row // half) % 2
        hit = spot == dest[...] * cx + bx[...]

        def forces(m):
            entry = half * m + row % half
            moment, kind = entry // (3 * pairs), (entry // pairs) % 3
            amount = jnp.zeros(row.shape, jnp.float32)
            for t in range(STEPS):
                amount = jnp.where(hit & (moment == t), wave[t : t + 1, :], amount)
            sums = None
            for c in range(3):
                term = jnp.dot(
                    jnp.where(kind == c, amount, 0.0),
                    pat[c],
                    precision=lax.Precision.HIGHEST,
                    preferred_element_type=jnp.float32,
                )
                sums = term if sums is None else sums + term
            views = [
                windows(sums[d * size : d * size + half], sums[d * size + half : (d + 1) * size])
                for d in range(ny)
            ]
            for d in range(ny):
                for j in range(nx):
                    both = views[d][j]
                    if j == 0:
                        both = jnp.where(at < HALO, views[d - 1][j] if d > 0 else 0.0, both)
                    if j == last:
                        both = jnp.where(at >= WIDE - HALO, views[d + 1][j] if d < ny - 1 else 0.0, both)
                    push_out[d, j, m] = both

        return forces

    tiles = push_in.shape[2]
    spans = (pl.ds(0, 1), pl.ds(1, tiles - 1))
    rest = pltpu.make_async_copy(push_out.at[iy, ix, spans[1]], push_in.at[ix, iy, spans[1]], push_rs.at[1])

    @pl.when(lead)
    def _():
        for to in peers:
            signal({"gx": to})

        @pl.when((ix == 0) & has_d)
        def _():
            for j in range(nx):
                signal({"gx": j, "gy": iy - 1})

        @pl.when((ix == last) & has_u)
        def _():
            for j in range(nx):
                signal({"gx": j, "gy": iy + 1})

        for copy in loads + tables + blocks_in:
            copy.start()
        for d in range(ny):
            for j in range(nx):
                signal({"gx": j, "gy": d, "gz": 0})
        blank = jnp.zeros((FIELDS, total, half, lanes), jnp.float32)
        grid[:, :, pl.ds(0, half)] = blank
        grid[:, :, pl.ds(3 * half, half)] = blank
        pack()
        source = lax.broadcasted_iota(jnp.int32, (lanes, lanes), 0)
        target = lax.broadcasted_iota(jnp.int32, (lanes, lanes), 1)
        for way in range(2):
            off = source - target + way
            tap = jnp.where(off == 1, NEAR / FAR, 0.0) + jnp.where(off == 0, -NEAR / FAR, 0.0)
            tap = tap + jnp.where(off == -1, 1.0, 0.0) + jnp.where(off == 2, -1.0, 0.0)
            tap = jnp.where(source // WIDE == target // WIDE, tap, 0.0).astype(jnp.bfloat16)
            taps[way, pl.ds(0, lanes)] = tap
            taps[way, pl.ds(lanes, lanes)] = tap
        pl.semaphore_wait(barrier, nx + has_d.astype(jnp.int32) + has_u.astype(jnp.int32))
        pl.semaphore_signal(go, inc=1, device_id={"gz": 0}, device_id_type=MESH)
        edges_do(top, "start")
        for part in range(2):
            for to in peers:
                bulk(to, top, part).start()
            keep(part).start()
        forces = force_maker()
        lax.fori_loop(1, tiles, lambda m, carry: (forces(m), carry)[1], 0)
        pl.semaphore_wait(far, 1)
        for d in range(ny):
            for j in range(nx):
                pl.when((ix != j) | (iy != d))(send(d, j, 1).start)
        rest.start()

    @pl.when(jnp.logical_not(lead))
    def _():
        signal({"gz": top})
        for copy in loads + blocks_in:
            copy.start()
        pack()
        pl.semaphore_wait(go, 1)
        edges_do(0, "start")
        for to in peers:
            bulk(to, 0, 0).start()
        bulk(ix, 0, 0).start()
        for to in peers:
            bulk(to, 0, 1).start()
        bulk(ix, 0, 1).start()
        forces = force_maker()
        forces(0)
        for j in range(nx):
            remote(
                push_out.at[iy, j, pl.ds(0, 1)],
                push_in.at[ix, iy, pl.ds(0, 1)],
                push_ss.at[iy, j, 0],
                push_rs.at[0],
                {"gx": j, "gz": top},
            ).start()
        pl.semaphore_wait(barrier, nx * ny)
        pl.semaphore_signal(far, inc=1, device_id={"gz": top}, device_id_type=MESH)
        for d in range(ny):
            for j in range(nx):
                pl.when(iy != d)(send(d, j, 0).start)
        for d in range(ny):
            for j in range(nx):
                send(d, j, 0).wait_send()
        for part in range(2):
            for j in range(nx):
                bulk(j, 0, part).wait_send()
        edges_do(0, "wait_send")
        results_wait()

    @pl.when(lead)
    def _():
        shape = (2 * half, lanes)
        lane = lax.broadcasted_iota(jnp.int32, shape, 1)
        left = lane < WIDE
        lane = lane % WIDE
        first = lax.broadcasted_iota(jnp.int32, shape, 0) == 0
        beyond = ((lane < HALO) & (ix == 0) & (iy == 0)) | (
            (lane >= WIDE - HALO) & (ix == last) & (iy == ny - 1)
        )
        within = jnp.where(beyond, 0.0, DT * FAR).astype(jnp.float32)
        ratio = NEAR / FAR
        zero = jnp.zeros(shape, jnp.float32)

        def bulk_wait(part):
            arrived(grid.at[groups[part], :, tall], bulk_rs.at[part])

        def merges(part):
            at_low = (ix == 0) & has_d
            at_high = (ix == last) & has_u

            @pl.when(at_low | at_high)
            def _():
                if part == 0:
                    arrived(got_strip, strip_rs.at[0])
                origin = jnp.where(ix == 0, HALO - BAND, WIDE - HALO)
                bound = jnp.where(ix == 0, HALO, WIDE - HALO)
                inside = (at >= bound) == (ix == 0)

                def body(j, carry):
                    for zt in range(2):
                        for f in range(*((0, FIRST), (FIRST, FIELDS))[part]):
                            for p in range(pairs):
                                i = f * pairs + p
                                shift = lax.rem(origin + lanes - BAND * (i % BANDS), lanes)
                                moved = pltpu.roll(got_strip[j, zt, i // BANDS], shift, 1)
                                here = (f, pairs * j + p, pl.ds(half * (zt + 1), half))
                                grid[here] = jnp.where(inside, grid[here], moved)
                    return carry

                for j in range(nx):
                    body(j, 0)

        def push_wait(part):
            arrived(push_in.at[:, :, spans[part]], push_rs.at[part])
            for m in (0,) if part == 0 else range(1, tiles):
                for j in range(nx):
                    amount = push_in[j, 0, m]
                    for i in range(1, ny):
                        amount = amount + push_in[j, i, m]
                    push[j, half * m : half * (m + 1)] = (1.0 / FAR) * amount

        def rows(f, k, s):
            return grid[f, k, pl.ds(half + s, 2 * half)]

        def turned(memo, f, k):
            if k < 0 or k >= total:
                return zero
            if (f, k) not in memo:
                memo[f, k] = pltpu.roll(grid[f, k, tall], WIDE, 1)
            return memo[f, k]

        def step(memo, f, k):
            if (f, k, "s") not in memo:
                memo[f, k, "s"] = jnp.where(left, turned(memo, f, k - 1), turned(memo, f, k))
            return memo[f, k, "s"]

        def along_x(memo, f, way, k):
            v, near, far = grid[f, k, tall], step(memo, f, k), step(memo, f, k + 1)
            if way == "f":
                after = grid[f, k + 1, tall] if k + 1 < total else zero
                return ratio * (far - v) - (after - near)
            before = grid[f, k - 1, tall] if k > 0 else zero
            return ratio * (v - near) - (far - before)

        def along_y(f, way):
            v = grid[f, :, tall].reshape(total * 2 * half, lanes)
            coarse = v.astype(jnp.bfloat16)
            fine = (v - coarse.astype(jnp.float32)).astype(jnp.bfloat16)
            out = jnp.dot(
                jnp.concatenate([coarse, fine], axis=1),
                taps[0 if way == "f" else 1],
                preferred_element_type=jnp.float32,
            )
            return [out[2 * half * k : 2 * half * (k + 1)] for k in range(total)]

        def along_z(f, way, k):
            o = 0 if way == "b" else 1
            return ratio * (rows(f, k, o) - rows(f, k, o - 1)) - (rows(f, k, o + 1) - rows(f, k, o - 2))

        txx, tyy, tzz, txy, txz, tyz = range(6)
        vx, vy, vz = range(FIRST, FIRST + 3)

        def rates(use):
            memo = {}
            dy = along_y(txy, "b"), along_y(tyy, "f"), along_y(tyz, "b")
            for k in range(total):
                for c, (fx, wx, fz, wz) in enumerate(
                    ((txx, "f", txz, "b"), (txy, "b", tyz, "b"), (txz, "b", tzz, "f"))
                ):
                    use(c, k, along_x(memo, fx, wx, k) + along_z(fz, wz, k) + dy[c][k])

        def kick(t, c, k, rate):
            now = push[k // pairs, pl.ds((t * 3 + c) * pairs + k % pairs, 1), :]
            grid[vx + c, k, tall] = grid[vx + c, k, tall] + coef[2, k] * (rate + jnp.where(first, now, 0.0))

        def strain():
            memo = {}
            dy = along_y(vx, "f"), along_y(vy, "b"), along_y(vz, "f")
            for k in range(total):
                exx, eyy, ezz = along_x(memo, vx, "b", k), dy[1][k], along_z(vz, "b", k)
                shear = coef[1, k]
                twice = 2.0 * shear
                trace = coef[0, k] * (exx + eyy + ezz)
                grid[txx, k, tall] = grid[txx, k, tall] + (trace + twice * exx)
                grid[tyy, k, tall] = grid[tyy, k, tall] + (trace + twice * eyy)
                grid[tzz, k, tall] = grid[tzz, k, tall] + (trace + twice * ezz)
                grid[txy, k, tall] = grid[txy, k, tall] + shear * (dy[0][k] + along_x(memo, vy, "f", k))
                grid[txz, k, tall] = grid[txz, k, tall] + shear * (along_z(vx, "f", k) + along_x(memo, vz, "f", k))
                grid[tyz, k, tall] = grid[tyz, k, tall] + shear * (along_z(vy, "f", k) + dy[2][k])

        own_lanes = (at >= HALO) & (at < HALO + slab)

        def finish(part):
            done, start, count = ((done_v, FIRST, 3), (done_s, 0, 6))[part]
            def body(j, carry):
                for zt in range(2):
                    for f in range(count):
                        here = pl.ds(half * (zt + 1), half)
                        a, b = grid[start + f, pairs * j, here], grid[start + f, pairs * j + 1, here]
                        done[j, zt, f] = jnp.where(own_lanes, a, pltpu.roll(b, slab, 1))
                return carry

            for j in range(nx):
                body(j, 0)
            for to in peers:
                for zt in range(2):
                    result(to, zt, part).start()
            result(ix, 0, part).start()

        def mine(part):
            done, back = ((done_v, back_v), (done_s, back_s))[part]
            return pltpu.make_async_copy(done.at[ix, top], back.at[ix], back_rs.at[part])

        for copy in tables:
            copy.wait()
        bulk_wait(0)
        merges(0)

        def fill(k, carry):
            region = grid[FIRST - 1, k, tall]
            picks = [zero] * 3
            for r in range(lame_t.shape[0]):
                hit = region == float(r)
                for q, table in enumerate((lame_t, shear_t, buoy_t)):
                    picks[q] = jnp.where(hit, table[r], picks[q])
            for q in range(3):
                coef[q, k] = within * picks[q]
            return carry

        for k in range(total):
            fill(k, 0)

        def store(c, k, rate):
            early[c, k] = rate

        rates(store)
        bulk_wait(1)
        merges(1)
        push_wait(0)
        for c in range(3):
            for k in range(total):
                kick(0, c, k, early[c, k])
        strain()
        push_wait(1)

        def middle(t, carry):
            rates(functools.partial(kick, t))
            strain()
            return carry

        for t in range(1, STEPS - 1):
            middle(t, 0)
        rates(functools.partial(kick, STEPS - 1))
        finish(0)
        mine(0).start()
        strain()
        finish(1)
        mine(1).start()

        for part in range(2):
            for to in peers:
                bulk(to, top, part).wait_send()
        for d in range(ny):
            for j in range(nx):
                pl.when((ix != j) | (iy != d))(send(d, j, 1).wait_send)
        edges_do(top, "wait_send")
        for part in range(2):
            for to in peers:
                for zt in range(2):
                    result(to, zt, part).wait_send()
            result(ix, 0, part).wait_send()
        results_wait()


def weave(back_v, back_s, vout_ref, sout_ref, vbuf, sbuf, sems):
    nx, _, half, lanes = back_v.shape
    slab = lanes // nx
    cx = vbuf.shape[1]
    offset = (0, WIDE, slab, WIDE + slab)
    lane = lax.broadcasted_iota(jnp.int32, (half, lanes), 1)
    for k, (back, buf, out) in enumerate(((back_v, vbuf, vout_ref), (back_s, sbuf, sout_ref))):
        for f in range(back.shape[1]):
            came = [back[j, f] for j in range(nx)]
            for x in range(cx):
                whole = None
                for j in range(nx):
                    moved = pltpu.roll(came[j], (slab * j - HALO - offset[x]) % lanes, 1)
                    whole = moved if whole is None else jnp.where(lane >= slab * j, moved, whole)
                buf[f, x] = whole
        pltpu.make_async_copy(buf, out, sems.at[k]).start()
    for k, (buf, out) in enumerate(((vbuf, vout_ref), (sbuf, sout_ref))):
        pltpu.make_async_copy(buf, out, sems.at[k]).wait()


def slabs(sizes, velocity, stress, region_map, lame_table, shear_table, buoy_table,
          block_pattern, block_wave, block_x, block_dest):
    nx, ny, nz = sizes
    cx, half, lanes = velocity.shape[1:]
    blocks = block_pattern.shape[0]
    pairs = cx // 2
    total = nx * pairs
    tile = (half, lanes)
    vmem = pl.BlockSpec(memory_space=pltpu.VMEM)
    hbm = pl.BlockSpec(memory_space=pl.ANY)
    tiles = STEPS * 3 * pairs // half
    f32, i32 = jnp.float32, jnp.int32
    dma = pltpu.SemaphoreType.DMA
    came = pl.pallas_call(
        functools.partial(slab_kernel, sizes),
        out_shape=(pltpu.VMEM((nx, 3) + tile, f32), pltpu.VMEM((nx, 6) + tile, f32)),
        in_specs=[hbm] * 10,
        out_specs=(vmem, vmem),
        scratch_shapes=[
            pltpu.VMEM((FIELDS, cx) + tile, f32),
            pltpu.VMEM(region_map.shape, i32),
            pltpu.VMEM((3, blocks, lanes), f32),
            pltpu.VMEM((STEPS, blocks), f32),
            pltpu.VMEM((1, blocks), i32),
            pltpu.VMEM((1, blocks), i32),
            pltpu.SMEM(lame_table.shape, f32),
            pltpu.SMEM(lame_table.shape, f32),
            pltpu.SMEM(lame_table.shape, f32),
            pltpu.VMEM((nx, FIELDS, pairs) + tile, f32),
            pltpu.VMEM((2, -(-FIELDS * pairs // BANDS)) + tile, f32),
            pltpu.VMEM((nx, 2, -(-FIELDS * pairs // BANDS)) + tile, f32),
            pltpu.VMEM((FIELDS, total, 4 * half, lanes), f32),
            pltpu.VMEM((3, total, 2 * half, lanes), f32),
            pltpu.VMEM((3, total, 2 * half, lanes), f32),
            pltpu.VMEM((2, 2 * lanes, lanes), jnp.bfloat16),
            pltpu.VMEM((ny, nx, tiles) + tile, f32),
            pltpu.VMEM((nx, ny, tiles) + tile, f32),
            pltpu.VMEM((nx, tiles * half, lanes), f32),
            pltpu.VMEM((nx, 2, 3) + tile, f32),
            pltpu.VMEM((nx, 2, 6) + tile, f32),
            dma((10,)),
            dma((nx, 2)),
            dma((2,)),
            dma((2,)),
            dma((1,)),
            dma((ny, nx, 2)),
            dma((2,)),
            dma((nx, 2, 2)),
            dma((2,)),
            pltpu.SemaphoreType.REGULAR,
            pltpu.SemaphoreType.REGULAR,
        ],
        compiler_params=pltpu.CompilerParams(collective_id=0, has_side_effects=True),
        name="slabs",
    )(
        velocity,
        stress,
        region_map,
        lame_table,
        shear_table,
        buoy_table,
        block_pattern.transpose(1, 0, 2),
        block_wave.T,
        block_x.reshape(1, blocks),
        block_dest.reshape(1, blocks),
    )
    return pl.pallas_call(
        weave,
        out_shape=(jax.ShapeDtypeStruct(velocity.shape, f32), jax.ShapeDtypeStruct(stress.shape, f32)),
        in_specs=[vmem, vmem],
        out_specs=(hbm, hbm),
        scratch_shapes=[pltpu.VMEM(velocity.shape, f32), pltpu.VMEM(stress.shape, f32), dma((2,))],
        name="weave",
    )(*(pltpu.with_memory_space_constraint(c, pltpu.VMEM) for c in came))


def local(sizes, velocity, *rest):
    nx, ny, nz = sizes
    cx, half, lanes = velocity.shape[1:]
    fits = nz == 2 and cx == 4 and half == 8 and lanes == 128 and lanes // nx + 2 * HALO == WIDE
    return (slabs if fits else shards)(sizes, velocity, *rest)


def solution(mesh):
    sizes = tuple(mesh.shape[a] for a in ("gx", "gy", "gz"))
    field = P(None, "gx", "gz", "gy")
    both = ("gx", "gy")
    placed = (
        field,
        field,
        P("gx", "gz", "gy"),
        P(),
        P(),
        P(),
        P(both, None, None),
        P(both, None),
        P(both),
        P(both, None),
    )
    return jax.shard_map(
        functools.partial(local, sizes),
        mesh=mesh,
        in_specs=placed,
        out_specs=(field, field),
        check_vma=False,
    )
```
